128 devices in a mesh: panel: 32 (over z, x, core), slab: 4 (over y).
Axes of the slice: x: 4, y: 4, z: 4, core: 2. Of those that a mesh axis runs over, the one named last changes fastest.
Arguments:
- charges: bfloat16 [1048576], P(('panel', 'slab')), may hold values from -6 to 6
- target: float32 [1048576], P(('panel', 'slab')), may hold values from -6 to 6
- stencil: bfloat16 [16384, 64, 256], P(('panel', 'slab')), may hold values from -0.375 to 0.375
- near_matrix: bfloat16 [16384, 4, 4096], P(('panel', 'slab')), may hold values from -0.375 to 0.375
- green: float32 [4096, 4096], P(None, ('panel', 'slab')), may hold values from 0.5 to 8
- block_dest: int32 [16384, 1], P(('panel', 'slab')), may hold values from 0 to 127; in each aligned block of 128 rows (0 to 127, 128 to 255, ...) at most 2 rows name the same one
- block_tile: int32 [16384], P(('panel', 'slab')), may hold values from 0 to 511
- near_offset: int32 [16384, 4], P(('panel', 'slab')), may hold values from -8 to 8
Outputs:
- potentials: float32 [1048576], P(('panel', 'slab'))
- gradient: float32 [1048576], P(('panel', 'slab'))
The draws below stay inside these ranges and needn't reach their ends.
Inputs may be any that keep to these rules, and one draw needn't show every extreme that they name: `block_dest`: in the 128 blocks of one device no owner is named more than 2 times; in some device's blocks one owner is named exactly 2 times.
All inputs are finite; a program needn't handle non-finite values.
Results may differ from the reference program's by a relative error of at most 0.0025.
The reference program's roundings to bfloat16 on the way (of `picked` and `residual`) count: a program that leaves them out, or rounds other values in their place, can miss the bound.
Values may be sent and summed in bfloat16 or wider, within the bound.
A program may use at most 128 MiB of HBM per device.

```python
import math
import jax
import jax.numpy as jnp
import numpy as np
from jax import lax

GRID = 4096
TILE = 16
BLOCK = 64
NEAR = 4
REACH = 8
BLK_DEV = 128
NDEV = 128
CAP = 2
TILE_CELLS = 256
TILES_DEV = 512
NBLK = 16384
PANELS = 1048576


def touch_ends(values, own_key, low, largest):
    longest = values.shape.index(max(values.shape))
    spots = []
    for shift in (0, 1):
        where = [jax.random.randint(jax.random.fold_in(own_key, axis), (), 0, length) for axis, length in enumerate(values.shape)]
        where[longest] = (where[longest] + shift) % values.shape[longest]
        spots.append(tuple(where))
    return values.at[spots[0]].set(low).at[spots[1]].set(largest)


def level_of(rng, shape, split, low, high):
    factor_of, own = 1.0, jax.random.fold_in(rng, 6)
    for position, shards_of in split:
        draws = jnp.exp(jax.random.uniform(jax.random.fold_in(own, position), (shards_of,), jnp.float32, low / len(split), high / len(split)))
        factor_of = factor_of * jnp.repeat(draws, shape[position] // shards_of).reshape([-1 if axis == position else 1 for axis in range(len(shape))])
    return factor_of


def routed_block(key, own, number, rows, number_of, top, limit, lean):
    sequence = jax.random.permutation(key, number_of)
    heavy_load, common = load_shares(number_of, rows * top, limit, lean, True), load_shares(number_of, rows * top, limit, lean, False)
    places = jnp.arange(number_of)

    def named(lengths, offset_by):
        used = int((lengths > 0).sum())
        fixed = max(1, used // 4)
        passed = fixed + (places - fixed + offset_by * (used - fixed)) % max(1, number_of - fixed)
        return jnp.zeros((number_of,), jnp.int32).at[sequence[jnp.where(places < fixed, places, passed)]].set(jnp.asarray(lengths, jnp.int32))

    lengths = jnp.where(number % 4 == 0, named(heavy_load, number // 4), named(common, number - number // 4 - 1))
    mixed = jax.random.permutation(jax.random.fold_in(own, 3), number_of)
    giver, taker = mixed[0:number_of // 2 * 2:2], mixed[1:number_of // 2 * 2:2]
    margin = jnp.minimum(lengths[giver] - 1, limit - lengths[taker]) // 2
    margin = jnp.where((giver == sequence[0]) | (taker == sequence[0]) | (lengths[taker] == 0), 0, jnp.maximum(margin, 0))
    passed = jax.random.randint(jax.random.fold_in(own, 4), (number_of // 2,), 0, 1 << 20) % (margin + 1)
    lengths = lengths.at[giver].add(-passed).at[taker].add(passed)
    items = jnp.searchsorted(jnp.cumsum(lengths), jnp.arange(rows * top), side="right").astype(jnp.int32)
    grid = items.reshape(top, rows).T
    grid = grid[jax.random.permutation(jax.random.fold_in(own, 1), rows)]
    offset_by = jax.random.randint(jax.random.fold_in(own, 2), (rows, 1), 0, top)
    return jnp.take_along_axis(grid, (jnp.arange(top)[None, :] + offset_by) % top, axis=1)


def load_shares(count, total, limit, lean, full):
    portions = [(1 << 20) // math.isqrt(grade ** lean) + 1 for grade in range(1, count + 1)]
    largest = limit if full else min(limit, max(-(-total // count), total * portions[0] // sum(portions)))
    least = 1 if total - largest >= count - 1 else 0
    holding, rest = [largest] + [least] * (count - 1), total - largest - least * (count - 1)
    while rest > 0:
        movable = [i for i in range(1, count) if holding[i] < largest] or [i for i in range(1, count) if holding[i] < limit]
        mass, left = sum([portions[i] for i in movable]), rest
        for i in movable:
            addition = min(limit - holding[i], max(1, left * portions[i] // mass), rest)
            holding[i] = holding[i] + addition
            rest = rest - addition
    return np.array(holding)


def normal_values(key, dims, scale, reach, cuts=(), kind=jnp.bfloat16):
    array = scale * jax.random.normal(key, dims, jnp.float32)
    if cuts:
        array = array * level_of(key, dims, cuts, -0.22, 0.18)
    return jnp.clip(array, -reach, reach).astype(kind)


def setup_inputs(seed: int = 0) -> dict:
    splits = jax.random.split(jax.random.key(seed), 9)
    charges = normal_values(splits[0], (PANELS,), 1.0, 6.0, ((0, 128),))
    target = normal_values(splits[1], (PANELS,), 1.0, 6.0, ((0, 128),), jnp.float32)
    stencil = normal_values(splits[2], (NBLK, BLOCK, TILE_CELLS), TILE_CELLS ** -0.5, 0.375, ((0, 128),))
    near_matrix = normal_values(splits[3], (NBLK, NEAR, BLOCK * BLOCK), (NEAR * BLOCK) ** -0.5, 0.375, ((0, 128),))
    green = jnp.clip(jnp.exp(math.log(8.0) - 2.7725887 * jax.random.uniform(splits[4], (GRID, GRID), jnp.float32) ** level_of(splits[4], (GRID, GRID), ((1, 128),), -0.2, 0.2)), 0.5, 8.0)
    block_dest_keys = jax.random.split(jax.random.fold_in(splits[5], 1), NBLK // BLK_DEV)
    block_dest_turns = jax.random.permutation(jax.random.fold_in(splits[5], 3), NBLK // BLK_DEV)
    block_dest = jax.vmap(lambda own, number: routed_block(jax.random.fold_in(splits[5], 2), own, number, BLK_DEV, NDEV, 1, CAP, 2))(block_dest_keys, block_dest_turns).reshape((NBLK, 1))
    block_tile = touch_ends(jax.random.randint(splits[6], (NBLK,), 0, TILES_DEV), jax.random.fold_in(splits[6], 1), 0, TILES_DEV - 1).astype(jnp.int32)
    near_offset = touch_ends(jax.random.randint(splits[7], (NBLK, NEAR), 0 - REACH, REACH + 1), jax.random.fold_in(splits[7], 1), 0 - REACH, REACH).astype(jnp.int32)
    return {"charges": charges, "target": target, "stencil": stencil, "near_matrix": near_matrix, "green": green, "block_dest": block_dest, "block_tile": block_tile, "near_offset": near_offset}


def reference(charges, target, stencil, near_matrix, green, block_dest, block_tile, near_offset):
    count = NBLK
    sides = GRID // TILE
    weights = stencil.astype(jnp.float32)
    couple = near_matrix.astype(jnp.float32).reshape(count, NEAR, BLOCK, BLOCK)
    global_tile = (block_dest[:, 0] * TILES_DEV + block_tile).astype(jnp.int32)
    positions = (jnp.arange(count, dtype=jnp.int32)[:, None] + REACH + near_offset).astype(jnp.int32)

    def far_field(values):
        tile_values = jnp.einsum('bp,bpt->bt', values.astype(jnp.float32), weights)
        tile_sums = jnp.zeros((sides * sides, TILE_CELLS), jnp.float32).at[global_tile].add(tile_values)
        grid_cells = tile_sums.reshape(sides, sides, TILE, TILE).transpose(0, 2, 1, 3).reshape(GRID, GRID)
        field = jnp.real(jnp.fft.ifft2(green * jnp.fft.fft2(grid_cells)))
        back_tiles = field.reshape(sides, TILE, sides, TILE).transpose(0, 2, 1, 3).reshape(sides * sides, TILE_CELLS)
        picked = back_tiles[global_tile].astype(jnp.bfloat16)
        picked = lax.optimization_barrier(picked).astype(jnp.float32)
        return jnp.einsum('bpt,bt->bp', weights, picked)

    def near_field(values):
        padded = jnp.pad(values.astype(jnp.float32), ((REACH, REACH), (0, 0)))
        return jnp.einsum('bkps,bks->bp', couple, padded[positions])

    def near_adjoint(values):
        terms = jnp.einsum('bkps,bp->bks', couple, values.astype(jnp.float32))
        padded = jnp.zeros((count + 2 * REACH, BLOCK), jnp.float32)
        padded = padded.at[positions.reshape(-1)].add(terms.reshape(-1, BLOCK))
        return padded[REACH:REACH + count]

    charge_blocks = charges.reshape(count, BLOCK)
    potentials = far_field(charge_blocks) + near_field(charge_blocks)
    residual = (potentials - target.reshape(count, BLOCK)).astype(jnp.bfloat16)
    gradient = far_field(residual) + near_adjoint(residual)
    return potentials.reshape(-1), gradient.reshape(-1)
```

```python
import functools
import math

import jax
import jax.numpy as jnp
import numpy as np
from jax import lax
from jax.experimental import pallas as pl
from jax.experimental.pallas import tpu as pltpu
from jax.sharding import PartitionSpec as P

GRID = 4096
TILE = 16
REACH = 8
NDEV = 128
SLABS = 4
BLOCKS = 128
PANEL = 64
CELLS = 256
LANES = 128
MSG = 8
ROWS = NDEV * MSG
MESH = pl.DeviceIdType.MESH
F32 = jnp.float32
BF16 = jnp.bfloat16
TABLES = ("w1", "w2", "m0", "m0i", "a1", "w3", "t2", "t1", "tm")


def make_tables():
    def angle(rows, cols, modulus):
        return 2.0 * math.pi / modulus * ((np.outer(rows, cols)) % modulus)

    out = {}
    th = angle(np.arange(128), np.arange(256), 256)
    w1 = np.concatenate([np.cos(th), -np.sin(th)], 0)
    w1[128] = (-1.0) ** np.arange(256)
    out["w1"] = w1
    th = angle(np.arange(16), np.arange(16), 16)
    c, s = np.kron(np.eye(8), np.cos(th)), np.kron(np.eye(8), np.sin(th))
    out["w2"] = np.concatenate([c, s], 1)
    m0 = np.zeros((2, 16, 2, 16))
    idx = np.arange(16)
    m0[0, :, 0, 0] = 1.0
    m0[0, :, 1, 0] = (-1.0) ** idx
    for k in range(1, 8):
        t = 2 * math.pi * ((idx * k) % 16) / 16
        m0[0, :, 0, k], m0[0, :, 1, k] = np.cos(t), -np.sin(t)
    for n in range(8):
        t = 2 * math.pi * ((idx * (1 + 2 * n)) % 32) / 32
        m0[1, :, 0, 8 + n], m0[1, :, 1, 8 + n] = np.cos(t), -np.sin(t)
    big = np.zeros((2, 8, 16, 2, 8, 16))
    for a in range(8):
        big[:, a, :, :, a, :] = m0
    out["m0"] = big.reshape(256, 256)
    inv = m0.copy()
    inv[:, :, :, 0] *= 0.5
    big = np.zeros((2, 8, 16, 2, 8, 16))
    for a in range(8):
        big[:, a, :, :, a, :] = inv
    out["m0i"] = big.reshape(256, 256).T
    th = angle(np.arange(128), np.arange(128), 128)
    out["a1"] = np.concatenate([np.cos(th), np.sin(th)], 1)
    th = angle(np.arange(8), np.arange(8), 8)
    out["w3"] = np.concatenate([np.kron(np.cos(th), np.eye(16)), np.kron(np.sin(th), np.eye(16))], 1)
    th = np.tile(angle(np.arange(128), np.arange(16), GRID), (1, 8))
    th[0] = 0.0
    out["t2"] = np.concatenate([np.cos(th), np.sin(th)], 1)
    th = np.repeat(angle(np.arange(128), np.arange(32), GRID), 16, axis=1)
    out["t1"] = np.concatenate([np.cos(th), np.sin(th)], 1)
    th = np.repeat(angle(np.arange(4), np.arange(8), 32), 16, axis=1)
    tm = np.zeros((8, 256))
    tm[:4] = np.concatenate([np.cos(th), np.sin(th)], 1)
    out["tm"] = tm
    return {k: np.asarray(v, np.float32) for k, v in out.items()}


def dot(a, b):
    return lax.dot_general(a, b, (((1,), (0,)), ((), ())), preferred_element_type=F32)


def dot_nt(a, b):
    return lax.dot_general(a, b, (((1,), (1,)), ((), ())), preferred_element_type=F32)


def split(x):
    hi = x.astype(BF16)
    return hi, (x - hi.astype(F32)).astype(BF16)


def dot3(a, b):
    return dot(a[0], b[0]) + (dot(a[0], b[1]) + dot(a[1], b[0]))


def iota(shape, dim):
    return lax.broadcasted_iota(jnp.int32, shape, dim)


def cat(parts, axis):
    return jnp.concatenate(parts, axis=axis)


def kernel(
    q_ref, near_ref, target_ref, stencil_hbm, green_ref, dest_ref, tile_ref,
    w1_ref, w2_ref, m0_ref, m0i_ref, a1_ref, w3_ref, t2_ref, t1_ref, tm_ref,
    pot_ref, res_ref, far_ref,
    stencil, sbuf, rbuf, gsend, grecv, ga, gb, val, tv, wf, wi, mats,
    send_sem, recv_sem, gsend_sem, grecv_sem, load_sem,
):
    panel = lax.axis_index("panel")
    slab = lax.axis_index("slab")
    me = panel * SLABS + slab
    pz, px, pc = panel // 8, (panel // 2) % 4, panel % 2

    load = pltpu.make_async_copy(stencil_hbm, stencil, load_sem)
    load.start()

    def peer_panel(i):
        return ((pz + 2 + i // 8) % 4) * 8 + ((px + 2 + (i // 2) % 4) % 4) * 2 + (pc + i % 2) % 2

    own = 20

    barrier = pltpu.get_barrier_semaphore()

    def greet(i, carry):
        other = peer_panel(i)
        for dy in (2, 3, 1):
            pl.semaphore_signal(barrier, inc=1, device_id=(other, (slab + dy) % 4), device_id_type=MESH)

        @pl.when(i != own)
        def _():
            pl.semaphore_signal(barrier, inc=1, device_id=(other, slab), device_id_type=MESH)

        return carry

    lax.fori_loop(0, 32, greet, 0)

    def pair(slot, value):
        hi, lo = split(value)
        mats[2 * slot] = hi
        mats[2 * slot + 1] = lo

    def mat(slot):
        return mats[2 * slot], mats[2 * slot + 1]

    def circle(ref):
        return ref[:, :LANES], ref[:, LANES:]

    pair(0, w1_ref[...])
    c, s = circle(w2_ref)
    pair(1, cat([cat([c, -s], 1), cat([s, c], 1)], 0))
    pair(2, cat([cat([c, s], 1), cat([-s, c], 1)], 0))
    pair(3, m0_ref[...])
    pair(4, m0i_ref[...])
    c, s = circle(a1_ref)
    pair(5, cat([cat([c, s], 1), cat([-s, c], 1)], 0))
    pair(6, cat([cat([c, -s], 1), cat([s, c], 1)], 0))
    c, s = circle(w3_ref)
    pair(7, cat([cat([c, -s], 1), cat([s, c], 1)], 0))
    pair(8, cat([cat([c, s], 1), cat([-s, c], 1)], 0))

    rows128, lanes128 = iota((128, 128), 0), iota((128, 128), 1)
    dest_row = dest_ref[...]
    tile_row = tile_ref[...]

    def column(row):
        return jnp.sum(jnp.where(rows128 == lanes128, row, 0), axis=1, keepdims=True)

    dest_col = column(dest_row)
    same = dest_col == dest_row
    rank_row = jnp.sum(jnp.where(same & (rows128 < lanes128), 1, 0), axis=0, keepdims=True)
    rank_col = jnp.sum(jnp.where(same & (lanes128 < rows128), 1, 0), axis=1, keepdims=True)
    one, zero = F32(1.0), F32(0.0)
    out_pick = cat(
        [jnp.where((dest_row == rows128) & (rank_row == k), one, zero) for k in range(2)], 0
    )
    in_pick = cat(
        [jnp.where((dest_col == lanes128) & (rank_col == k), one, zero) for k in range(2)], 1
    ).astype(BF16)
    ids = jnp.sum(out_pick * (tile_row + 1).astype(F32), axis=1, keepdims=True)
    id_rows = jnp.where(lanes128 == 0, ids[:128], jnp.where(lanes128 == 1, ids[128:], 0.0))
    out_pick = out_pick.astype(BF16)

    def exchange(step):
        src, dst = sbuf.at[step], rbuf.at[step]
        mine = pl.ds(pl.multiple_of(me * MSG, MSG), MSG)

        def send(other, other_slab):
            theirs = pl.ds(pl.multiple_of((other * SLABS + other_slab) * MSG, MSG), MSG)
            pltpu.make_async_remote_copy(
                src_ref=src.at[theirs],
                dst_ref=dst.at[mine],
                send_sem=send_sem.at[step],
                recv_sem=recv_sem.at[step],
                device_id=(other, other_slab),
                device_id_type=MESH,
            ).start()

        def body(i, carry):
            other = peer_panel(i)
            for dy in (2, 3, 1):
                send(other, (slab + dy) % 4)

            @pl.when(i != own)
            def _():
                send(other, slab)

            return carry

        lax.fori_loop(0, 32, body, 0)
        pltpu.make_async_copy(src.at[mine], dst.at[mine], recv_sem.at[step]).start()

    def arrived(step):
        pltpu.make_async_copy(sbuf.at[step], rbuf.at[step], recv_sem.at[step]).wait()

    def sent(step):
        part = pl.ds(0, ROWS - MSG)
        pltpu.make_async_copy(
            sbuf.at[step, part], rbuf.at[step, part], send_sem.at[step]
        ).wait()

    def put(step, row, value):
        sbuf[step, pl.ds(row, NDEV, stride=MSG), :] = value

    def get(step, row):
        return rbuf[step, pl.ds(row, NDEV, stride=MSG), :]

    def pack(kk, carry):
        gsend[pl.ds(kk, 32, stride=32), :] = green_ref[:, pl.ds(pl.multiple_of(kk * LANES, LANES), LANES)]
        return carry

    lax.fori_loop(0, 32, pack, 0)

    def green_copies():
        k2 = me // 8

        def body(j, carry):
            k1 = (me % 8) * 32 + j
            low = jnp.where(k1 < 128, 1, 0)
            is_mid = jnp.where(k1 == 128, 1, 0)
            is_zero = jnp.where(k1 == 0, 1, 0)
            high = 1 - low - is_mid
            target_dev = low * k1 + high * (256 - k1)
            upper = k2 // 8
            beyond = jnp.where(k2 > 8, 1, 0)
            slot_zero = (1 - upper) * k2 + upper * (1 - beyond) * 16 + beyond * (32 - k2)
            slot_mid = (1 - upper) * (8 + k2) + upper * (39 - k2)
            slot = (low - is_zero) * k2 + is_zero * slot_zero + is_mid * slot_mid + high * (31 - k2)
            src = gsend.at[pl.ds(pl.multiple_of(j * 32, 32), 32)]
            dst = grecv.at[pl.ds(pl.multiple_of(slot * 32, 32), 32)]

            @pl.when(target_dev != me)
            def _():
                pltpu.make_async_remote_copy(
                    src_ref=src, dst_ref=dst, send_sem=gsend_sem.at[j], recv_sem=grecv_sem,
                    device_id=(target_dev // SLABS, target_dev % SLABS), device_id_type=MESH,
                ).start()

            @pl.when(target_dev == me)
            def _():
                pltpu.make_async_copy(src, dst, grecv_sem).start()

            return carry

        lax.fori_loop(0, 32, body, 0)

    def green_sent():
        def body(j, carry):
            k1 = (me % 8) * 32 + j
            low = jnp.where(k1 < 128, 1, 0)
            high = jnp.where(k1 > 128, 1, 0)
            target_dev = low * k1 + high * (256 - k1)

            @pl.when(target_dev != me)
            def _():
                part = pl.ds(pl.multiple_of(j * 32, 32), 32)
                pltpu.make_async_copy(gsend.at[part], grecv.at[part], gsend_sem.at[j]).wait()

            return carry

        lax.fori_loop(0, 32, body, 0)

    def green_ready():
        pltpu.make_async_copy(gsend, grecv, grecv_sem).wait()
        scale = 2.0 ** -24
        flip = jnp.where((rows128 + lanes128 == 128) & (rows128 > 0), one, zero).astype(BF16)
        first = jnp.where((rows128 == 0) & (lanes128 == 0), one, zero).astype(BF16)
        eye = jnp.where(rows128 == lanes128, one, zero).astype(BF16)
        turn = cat([flip, first], 1)
        special = (lanes128 % 16 == 0) & (me == 0)

        def rows_of(base, kappa):
            return cat(
                [grecv[pl.ds(base * 32 + kappa(n), 16, stride=32), :] for n in range(8)], 0
            )

        for m in range(4):
            def plain(base):
                hi, lo = split(rows_of(base, lambda n: m + 4 * n))
                return dot_nt(eye, hi) + dot_nt(eye, lo)

            def turned(base):
                one_ = rows_of(base, lambda n: 31 - m - 4 * n)
                two_ = rows_of(base, lambda n: (32 - m - 4 * n) % 32)
                hi, lo = split(cat([one_, two_], 1))
                return dot_nt(turn, hi) + dot_nt(turn, lo)

            d, dr, o, orr = plain(0), turned(0), plain(16), turned(16)
            ga[:, m * LANES:(m + 1) * LANES] = (d + jnp.where(special, dr, orr)) * scale
            gb[:, m * LANES:(m + 1) * LANES] = (jnp.where(special, o, d) + orr) * scale

    lane64 = iota((128, 128), 1) // 64
    row16 = iota((128, 128), 0) % 16

    def project():
        v = val[...]
        spread = cat(
            [jnp.where(lane64 + 2 * i == row16, v, 0.0).astype(BF16) for i in range(8)], 1
        )
        for g in range(8):
            part = stencil[g * 1024:(g + 1) * 1024, :]
            tv[g * 16:(g + 1) * 16, :] = dot(spread[g * 16:(g + 1) * 16, :], part)
        hi, lo = split(tv[...])
        return dot(out_pick, hi) + dot(out_pick, lo)

    def interpolate(own_tiles):
        rows = []
        l64, r16 = iota((16, 128), 1) // 64, iota((16, 128), 0)
        for g in range(8):
            part = stencil[g * 1024:(g + 1) * 1024, :]
            r = dot_nt(own_tiles[g * 16:(g + 1) * 16, :], part)
            acc = jnp.zeros((16, 128), F32)
            for i in range(8):
                acc = acc + jnp.where(l64 + 2 * i == r16, r[:, i * LANES:(i + 1) * LANES], 0.0)
            rows.append(acc)
        far = cat(rows, 0)
        return far + pltpu.roll(far, 64, 1)

    def cmul(re, im, c, s):
        return re * c + im * s, im * c - re * s

    def cmul_conj(re, im, c, s):
        return re * c - im * s, im * c + re * s

    def lane_tile(x, j):
        return x[:, j * LANES:(j + 1) * LANES]

    head = iota((8, 128), 0) == 0

    def special_rows(parts, slot, outs):
        small = dot3(split(cat([p[:8] for p in parts], 0)), mat(slot))
        fixed = []
        for j in range(4):
            out = outs[j]
            h2 = iota((8, 256), 0) == 0
            fixed.append(cat([jnp.where(h2, small[8 * j:8 * j + 8], out[:8]), out[8:]], 0))
        return fixed

    def evaluate(step0, which):
        out = project()
        for k in range(2):
            for h in range(2):
                put(step0, 2 * k + h, lane_tile(out[128 * k:128 * k + 128], h))
        put(step0, 4, id_rows)

        @pl.when(which == 0)
        def _():
            pl.semaphore_wait(barrier, NDEV - 1)

        exchange(step0)

        @pl.when(which == 0)
        def _():
            green_copies()

        arrived(step0)

        @pl.when(which == 0)
        def _():
            idm = get(step0, 4)
            tc = iota((128, 256), 1)
            for tr in range(2):
                pick = cat(
                    [
                        jnp.where(idm[:, k:k + 1].astype(jnp.int32) == tc + (tr * 256 + 1), one, zero)
                        for k in range(2)
                    ],
                    0,
                ).astype(BF16)
                for t in range(2):
                    wf[2 * tr + t] = dot_nt(mats[t], pick).astype(BF16)
                    wi[t, :, tr * 256:(tr + 1) * 256] = dot_nt(pick, mats[t]).astype(BF16)

        tiles = split(
            cat([cat([get(step0, 2 * k + h) for h in range(2)], 1) for k in range(2)], 0)
        )
        c2, s2 = t2_ref[:, :LANES], t2_ref[:, LANES:]
        parts = []
        for tr in range(2):
            y = dot3((wf[2 * tr], wf[2 * tr + 1]), tiles)
            for h in range(2):
                re, im = cmul(lane_tile(y[:128], h), lane_tile(y[128:], h), c2, s2)
                parts.append(cat([re, im], 1))
        prod = dot3(split(cat(parts, 0)), mat(1))
        outs = special_rows(parts, 3, [prod[128 * j:128 * j + 128] for j in range(4)])
        for j in range(4):
            put(step0 + 1, j, outs[j][:, :LANES])
            put(step0 + 1, 4 + j, outs[j][:, LANES:])
        exchange(step0 + 1)

        @pl.when(which == 0)
        def _():
            green_ready()

        arrived(step0 + 1)
        x = cat(
            [
                cat([get(step0 + 1, j) for j in range(4)], 1),
                cat([get(step0 + 1, 4 + j) for j in range(4)], 1),
            ],
            0,
        )
        y = dot3(mat(5), split(x))
        re, im = cmul(y[:128], y[128:], t1_ref[:, :512], t1_ref[:, 512:])
        r = [lane_tile(re, j) for j in range(4)]
        i = [lane_tile(im, j) for j in range(4)]
        er, ei, dr, di = r[0] + r[2], i[0] + i[2], r[0] - r[2], i[0] - i[2]
        fr, fi, hr, hi_ = r[1] + r[3], i[1] + i[3], r[1] - r[3], i[1] - i[3]
        vs = [(er + fr, ei + fi), (dr + hi_, di - hr), (er - fr, ei - fi), (dr - hi_, di + hr)]
        parts = []
        for m in range(4):
            cm, sm = tm_ref[m:m + 1, :LANES], tm_ref[m:m + 1, LANES:]
            parts.append(cat(list(cmul(vs[m][0], vs[m][1], cm, sm)), 1))
        f = dot3(split(cat(parts, 0)), mat(7))
        both = []
        for g in (ga, gb):
            for m in range(4):
                gm = g[:, m * LANES:(m + 1) * LANES]
                fm = f[128 * m:128 * m + 128]
                both.append(cat([fm[:, :LANES] * gm, fm[:, LANES:] * gm], 1))
        p = dot3(split(cat(both, 0)), mat(8))
        stacked = []
        for e in range(2):
            vs = []
            for m in range(4):
                cm, sm = tm_ref[m:m + 1, :LANES], tm_ref[m:m + 1, LANES:]
                pm = p[512 * e + 128 * m:512 * e + 128 * m + 128]
                vs.append(cmul_conj(pm[:, :LANES], pm[:, LANES:], cm, sm))
            r = [v[0] for v in vs]
            i = [v[1] for v in vs]
            er, ei, dr, di = r[0] + r[2], i[0] + i[2], r[0] - r[2], i[0] - i[2]
            fr, fi, hr, hi_ = r[1] + r[3], i[1] + i[3], r[1] - r[3], i[1] - i[3]
            zs = [(er + fr, ei + fi), (dr - hi_, di + hr), (er - fr, ei - fi), (dr + hi_, di - hr)]
            re, im = cmul_conj(
                cat([z[0] for z in zs], 1), cat([z[1] for z in zs], 1),
                t1_ref[:, :512], t1_ref[:, 512:],
            )
            stacked.append(split(cat([re, im], 0)))
        inv = mat(6)
        yr = dot3((inv[0][:128], inv[1][:128]), stacked[0])
        yi = dot3((inv[0][128:], inv[1][128:]), stacked[1])
        for j in range(4):
            put(step0 + 2, j, lane_tile(yr, j))
            put(step0 + 2, 4 + j, lane_tile(yi, j))
        exchange(step0 + 2)
        arrived(step0 + 2)
        parts = [cat([get(step0 + 2, j), get(step0 + 2, 4 + j)], 1) for j in range(4)]
        prod = dot3(split(cat(parts, 0)), mat(2))
        outs = special_rows(parts, 4, [prod[128 * j:128 * j + 128] for j in range(4)])
        zs = [cmul_conj(o[:, :LANES], o[:, LANES:], c2, s2) for o in outs]
        y = cat(
            [
                cat([cat([zs[2 * tr][0], zs[2 * tr + 1][0]], 1), cat([zs[2 * tr][1], zs[2 * tr + 1][1]], 1)], 0)
                for tr in range(2)
            ],
            0,
        )
        back = dot3((wi[0], wi[1]), split(y)).astype(BF16).astype(F32)
        for k in range(2):
            for h in range(2):
                put(step0 + 3, 2 * k + h, lane_tile(back[128 * k:128 * k + 128], h))
        put(step0 + 3, 4, id_rows)
        exchange(step0 + 3)
        arrived(step0 + 3)
        tiles = cat(
            [cat([get(step0 + 3, 2 * k + h) for h in range(2)], 1) for k in range(2)], 0
        ).astype(BF16)
        far = interpolate(dot(in_pick, tiles).astype(BF16))

        @pl.when(which == 0)
        def _():
            pot = far + near_ref[...]
            pot_ref[...] = pot
            residual = (pot - target_ref[...]).astype(BF16)
            res_ref[...] = residual
            val[...] = residual.astype(F32)

        @pl.when(which == 1)
        def _():
            far_ref[...] = far

    for step in range(8):
        for row in range(5, 8):
            if step % 4 in (0, 3):
                put(step, row, jnp.zeros((NDEV, LANES), F32))
    val[...] = q_ref[...].astype(F32)
    load.wait()

    def both_passes(which, carry):
        evaluate(which * 4, which)
        return carry

    lax.fori_loop(0, 2, both_passes, 0)
    for step in range(8):
        sent(step)
    green_sent()


def far_kernel(q, near, target, stencil, green, dest, tile, tables):
    vmem = pl.BlockSpec(memory_space=pltpu.VMEM)
    hbm = pl.BlockSpec(memory_space=pl.ANY)
    return pl.pallas_call(
        kernel,
        out_shape=(
            jax.ShapeDtypeStruct((BLOCKS, LANES), F32),
            jax.ShapeDtypeStruct((BLOCKS, LANES), BF16),
            jax.ShapeDtypeStruct((BLOCKS, LANES), F32),
        ),
        in_specs=[vmem, vmem, vmem, hbm] + [vmem] * (3 + len(tables)),
        out_specs=(vmem, vmem, vmem),
        scratch_shapes=[
            pltpu.VMEM((BLOCKS * PANEL, CELLS), BF16),
            pltpu.VMEM((8, ROWS, LANES), F32),
            pltpu.VMEM((8, ROWS, LANES), F32),
            pltpu.VMEM((1024, LANES), F32),
            pltpu.VMEM((1024, LANES), F32),
            pltpu.VMEM((128, 512), F32),
            pltpu.VMEM((128, 512), F32),
            pltpu.VMEM((128, 128), F32),
            pltpu.VMEM((128, 256), F32),
            pltpu.VMEM((4, 256, 256), BF16),
            pltpu.VMEM((2, 256, 512), BF16),
            pltpu.VMEM((18, 256, 256), BF16),
            pltpu.SemaphoreType.DMA((8,)),
            pltpu.SemaphoreType.DMA((8,)),
            pltpu.SemaphoreType.DMA((32,)),
            pltpu.SemaphoreType.DMA,
            pltpu.SemaphoreType.DMA,
        ],
        compiler_params=pltpu.CompilerParams(collective_id=0, has_side_effects=True),
        name="far_field",
    )(q, near, target, stencil, green, dest, tile, *tables)


def extended_2(cells, sides, width):
    for axis, dim in sides:
        count = lax.axis_size(axis)
        ends = count - 1
        head = lax.slice_in_dim(cells, 0, width, axis=dim)
        tail = lax.slice_in_dim(cells, cells.shape[dim] - width, cells.shape[dim], axis=dim)
        cells = jnp.concatenate(
            [
                lax.ppermute(tail, axis, [(i, (i + 1) % count) for i in range(ends)]),
                cells,
                lax.ppermute(head, axis, [((i + 1) % count, i) for i in range(ends)]),
            ],
            axis=dim,
        )
    return cells


def local(tables, charges, target, stencil, near_matrix, green, block_dest, block_tile, near_offset):
    blocks = stencil.shape[0]
    block_size = stencil.shape[1]
    pair_count = near_offset.shape[1]
    couple = near_matrix.reshape(blocks, pair_count, block_size, block_size)
    positions = jnp.arange(blocks, dtype=jnp.int32)[:, None] + REACH + near_offset
    charge_blocks = charges.reshape(blocks, block_size)
    extended = extended_2(charge_blocks, ((("panel", "slab"), 0),), REACH)
    near = jnp.einsum(
        "bkps,bks->bp", couple, extended[positions], preferred_element_type=jnp.float32
    )
    twice = lambda x: jnp.concatenate([x, x], axis=1)
    pot, res, far = far_kernel(
        twice(charge_blocks), twice(near), twice(target.reshape(blocks, block_size)),
        stencil.reshape(blocks * block_size, stencil.shape[2]), green.T,
        block_dest.reshape(1, blocks), block_tile.reshape(1, blocks), tables,
    )
    potentials, residual = pot[:, :block_size], res[:, :block_size]
    terms = jnp.einsum("bkps,bp->bks", couple, residual, preferred_element_type=jnp.float32)
    extended = jnp.zeros((blocks + 2 * REACH, block_size), jnp.float32)
    extended = extended.at[positions.reshape(-1)].add(terms.reshape(-1, block_size))
    rims = jnp.concatenate([extended[:REACH], extended[blocks + REACH :]], axis=0)
    neighbour = extended_2(rims, ((("panel", "slab"), 0),), REACH)
    own_part = extended[REACH : blocks + REACH]
    own_part = own_part.at[:REACH].add(neighbour[:REACH])
    gradient = far[:, :block_size] + own_part.at[blocks - REACH :].add(neighbour[3 * REACH :])
    return (potentials.reshape(-1), gradient.reshape(-1))


def solution(mesh):
    made = make_tables()
    tables = [jnp.asarray(made[name]) for name in TABLES]
    return jax.shard_map(
        functools.partial(local, tables),
        mesh=mesh,
        in_specs=(
            P(("panel", "slab")),
            P(("panel", "slab")),
            P(("panel", "slab"), None, None),
            P(("panel", "slab"), None, None),
            P(None, ("panel", "slab")),
            P(("panel", "slab"), None),
            P(("panel", "slab")),
            P(("panel", "slab"), None),
        ),
        out_specs=(P(("panel", "slab")), P(("panel", "slab"))),
        check_vma=False,
    )
```

```python
import functools
import math

import jax
import jax.numpy as jnp
import numpy as np
from jax import lax
from jax.experimental import pallas as pl
from jax.experimental.pallas import tpu as pltpu
from jax.sharding import PartitionSpec as P

GRID = 4096
TILE = 16
REACH = 8
NDEV = 128
SLABS = 4
BLOCKS = 128
PANEL = 64
CELLS = 256
LANES = 128
MSG = 8
ROWS = NDEV * MSG
MESH = pl.DeviceIdType.MESH
F32 = jnp.float32
BF16 = jnp.bfloat16
TABLES = ("w1", "w2", "m0", "m0i", "a1", "w3", "t2", "t1", "tm")


def make_tables():
    def angle(rows, cols, modulus):
        return 2.0 * math.pi / modulus * ((np.outer(rows, cols)) % modulus)

    out = {}
    th = angle(np.arange(128), np.arange(256), 256)
    w1 = np.concatenate([np.cos(th), -np.sin(th)], 0)
    w1[128] = (-1.0) ** np.arange(256)
    out["w1"] = w1
    th = angle(np.arange(16), np.arange(16), 16)
    c, s = np.kron(np.eye(8), np.cos(th)), np.kron(np.eye(8), np.sin(th))
    out["w2"] = np.concatenate([c, s], 1)
    m0 = np.zeros((2, 16, 2, 16))
    idx = np.arange(16)
    m0[0, :, 0, 0] = 1.0
    m0[0, :, 1, 0] = (-1.0) ** idx
    for k in range(1, 8):
        t = 2 * math.pi * ((idx * k) % 16) / 16
        m0[0, :, 0, k], m0[0, :, 1, k] = np.cos(t), -np.sin(t)
    for n in range(8):
        t = 2 * math.pi * ((idx * (1 + 2 * n)) % 32) / 32
        m0[1, :, 0, 8 + n], m0[1, :, 1, 8 + n] = np.cos(t), -np.sin(t)
    big = np.zeros((2, 8, 16, 2, 8, 16))
    for a in range(8):
        big[:, a, :, :, a, :] = m0
    out["m0"] = big.reshape(256, 256)
    inv = m0.copy()
    inv[:, :, :, 0] *= 0.5
    big = np.zeros((2, 8, 16, 2, 8, 16))
    for a in range(8):
        big[:, a, :, :, a, :] = inv
    out["m0i"] = big.reshape(256, 256).T
    th = angle(np.arange(128), np.arange(128), 128)
    out["a1"] = np.concatenate([np.cos(th), np.sin(th)], 1)
    th = angle(np.arange(8), np.arange(8), 8)
    out["w3"] = np.concatenate([np.kron(np.cos(th), np.eye(16)), np.kron(np.sin(th), np.eye(16))], 1)
    th = np.tile(angle(np.arange(128), np.arange(16), GRID), (1, 8))
    th[0] = 0.0
    out["t2"] = np.concatenate([np.cos(th), np.sin(th)], 1)
    th = np.repeat(angle(np.arange(128), np.arange(32), GRID), 16, axis=1)
    out["t1"] = np.concatenate([np.cos(th), np.sin(th)], 1)
    th = np.repeat(angle(np.arange(4), np.arange(8), 32), 16, axis=1)
    tm = np.zeros((8, 256))
    tm[:4] = np.concatenate([np.cos(th), np.sin(th)], 1)
    out["tm"] = tm
    return {k: np.asarray(v, np.float32) for k, v in out.items()}


def dot(a, b):
    return lax.dot_general(a, b, (((1,), (0,)), ((), ())), preferred_element_type=F32)


def dot_nt(a, b):
    return lax.dot_general(a, b, (((1,), (1,)), ((), ())), preferred_element_type=F32)


def split(x):
    hi = x.astype(BF16)
    return hi, (x - hi.astype(F32)).astype(BF16)


def dot3(a, b):
    return dot(a[0], b[0]) + (dot(a[0], b[1]) + dot(a[1], b[0]))


def iota(shape, dim):
    return lax.broadcasted_iota(jnp.int32, shape, dim)


def cat(parts, axis):
    return jnp.concatenate(parts, axis=axis)


COMBOS = sorted(
    ((dz, dx) for dz in range(4) for dx in range(4)),
    key=lambda c: -(min(c[0], 4 - c[0]) + min(c[1], 4 - c[1])),
)
Z_DIGITS = sum(c[0] << (2 * i) for i, c in enumerate(COMBOS))
X_DIGITS = sum(c[1] << (2 * i) for i, c in enumerate(COMBOS))


def encode(re, im):
    top = jnp.abs(re[0])
    for x in list(re[1:]) + list(im):
        top = jnp.maximum(top, jnp.abs(x))
    top = jnp.maximum(top, 2.0 ** -100)
    power = jnp.floor(jnp.log2(top)) + 1.0
    scale = jnp.exp2(14.0 - power)
    code = power.astype(jnp.int32) + 128

    def mantissa(x):
        return jnp.minimum(x * scale + 16384.5, 32767.5).astype(jnp.int32)

    return [
        (((code >> (2 * j)) & 3) << 30) | (mantissa(re[j]) << 15) | mantissa(im[j])
        for j in range(4)
    ]


def decode(words):
    code = words[0] >> 30 & 3
    for j in range(1, 4):
        code = code | ((words[j] >> 30 & 3) << (2 * j))
    scale = jnp.exp2(code.astype(F32) - 142.0)
    re = [((w >> 15 & 32767).astype(F32) - 16384.0) * scale for w in words]
    im = [((w & 32767).astype(F32) - 16384.0) * scale for w in words]
    return re, im


def kernel(
    q_ref, target_ref, stencil_hbm, near_hbm, green_ref, dest_ref, tile_ref, offset_ref,
    w1_ref, w2_ref, m0_ref, m0i_ref, a1_ref, w3_ref, t2_ref, t1_ref, tm_ref,
    pot_ref, grad_ref,
    stencil, near_mat, sbuf, rbuf, swords, rwords, gsend, grecv, ga, gb, val, charge, goal, tv,
    wf, wi, mats, xs, acc, near, ext, halo, rim,
    send_sem, recv_sem, gsend_sem, grecv_sem, load_sem, near_sem, halo_sem, rim_sem,
):
    panel = lax.axis_index("panel")
    slab = lax.axis_index("slab")
    me = panel * SLABS + slab
    pz, px, pc = panel // 8, (panel // 2) % 4, panel % 2

    load = pltpu.make_async_copy(stencil_hbm, stencil, load_sem)
    load.start()

    def others(visit):
        def body(g, carry):
            z = (pz + ((Z_DIGITS >> (2 * g)) & 3)) % 4
            x = (px + ((X_DIGITS >> (2 * g)) & 3)) % 4
            for dy in (2, 1, 3, 0):
                for dc in (1, 0):
                    def go(z=z, x=x, dy=dy, dc=dc):
                        visit(z * 8 + x * 2 + (pc + dc) % 2, (slab + dy) % 4)

                    if dy == 0 and dc == 0:
                        pl.when(g != 15)(go)
                    else:
                        go()
            return carry

        lax.fori_loop(0, 16, body, 0)

    barrier = pltpu.get_barrier_semaphore()
    others(
        lambda p, y: pl.semaphore_signal(barrier, inc=1, device_id=(p, y), device_id_type=MESH)
    )

    def near_load(b, carry):
        pltpu.make_async_copy(
            near_hbm.at[b], near_mat.at[pl.ds(pl.multiple_of(b * 4, 4), 4)], near_sem
        ).start()
        return carry

    lax.fori_loop(0, BLOCKS, near_load, 0)

    rows128, lanes128 = iota((128, 128), 0), iota((128, 128), 1)

    def unfold(ref, out):
        x = ref[...].astype(F32)
        y = pltpu.roll(x, 64, 1)
        low = iota((64, 128), 1) < 64
        out[pl.ds(0, 64, stride=2), :] = jnp.where(low, x, y)
        out[pl.ds(1, 64, stride=2), :] = jnp.where(low, y, x)

    def fold(out, scr, value):
        scr[...] = value
        low = iota((64, 128), 1) < 64
        out[...] = jnp.where(low, scr[pl.ds(0, 64, stride=2), :], scr[pl.ds(1, 64, stride=2), :])

    unfold(q_ref, charge)
    unfold(q_ref, val)
    unfold(target_ref, goal)

    def pair(slot, value):
        hi, lo = split(value)
        mats[2 * slot] = hi
        mats[2 * slot + 1] = lo

    def mat(slot):
        return mats[2 * slot], mats[2 * slot + 1]

    def circle(ref):
        return ref[:, :LANES], ref[:, LANES:]

    pair(0, w1_ref[...])
    c, s = circle(w2_ref)
    pair(1, cat([cat([c, -s], 1), cat([s, c], 1)], 0))
    pair(2, cat([cat([c, s], 1), cat([-s, c], 1)], 0))
    pair(3, m0_ref[...])
    pair(4, m0i_ref[...])
    c, s = circle(a1_ref)
    pair(5, cat([cat([c, s], 1), cat([-s, c], 1)], 0))
    pair(6, cat([cat([c, -s], 1), cat([s, c], 1)], 0))
    c, s = circle(w3_ref)
    pair(7, cat([cat([c, -s], 1), cat([s, c], 1)], 0))
    pair(8, cat([cat([c, s], 1), cat([-s, c], 1)], 0))

    dest_row = dest_ref[...]
    tile_row = tile_ref[...]

    def column(row):
        return jnp.sum(jnp.where(rows128 == lanes128, row, 0), axis=1, keepdims=True)

    dest_col = column(dest_row)
    same = dest_col == dest_row
    rank_row = jnp.sum(jnp.where(same & (rows128 < lanes128), 1, 0), axis=0, keepdims=True)
    rank_col = jnp.sum(jnp.where(same & (lanes128 < rows128), 1, 0), axis=1, keepdims=True)
    one, zero = F32(1.0), F32(0.0)
    out_pick = cat(
        [jnp.where((dest_row == rows128) & (rank_row == k), one, zero) for k in range(2)], 0
    )
    in_pick = cat(
        [jnp.where((dest_col == lanes128) & (rank_col == k), one, zero) for k in range(2)], 1
    ).astype(BF16)
    ids = jnp.sum(out_pick * (tile_row + 1).astype(F32), axis=1, keepdims=True)
    id_rows = jnp.where(lanes128 == 0, ids[:128], jnp.where(lanes128 == 1, ids[128:], 0.0))
    out_pick = out_pick.astype(BF16)

    def exchange(step, src, dst, stride, count):
        mine = pl.ds(pl.multiple_of(me * stride, stride), count)

        def send(p, y):
            theirs = pl.ds(pl.multiple_of((p * SLABS + y) * stride, stride), count)
            pltpu.make_async_remote_copy(
                src_ref=src.at[theirs],
                dst_ref=dst.at[mine],
                send_sem=send_sem.at[step],
                recv_sem=recv_sem.at[step],
                device_id=(p, y),
                device_id_type=MESH,
            ).start()

        others(send)
        pltpu.make_async_copy(src.at[mine], dst.at[mine], recv_sem.at[step]).start()

    def arrived(step, src, dst, count):
        part = pl.ds(0, NDEV * count)
        pltpu.make_async_copy(src.at[part], dst.at[part], recv_sem.at[step]).wait()

    def sent(step, src, dst, count):
        part = pl.ds(0, (NDEV - 1) * count)
        pltpu.make_async_copy(src.at[part], dst.at[part], send_sem.at[step]).wait()

    def put(slot, row, value):
        sbuf[slot, pl.ds(row, NDEV, stride=MSG), :] = value

    def get(slot, row):
        return rbuf[slot, pl.ds(row, NDEV, stride=MSG), :]

    def put_words(slot, re, im):
        for j, w in enumerate(encode(re, im)):
            swords[slot, pl.ds(j, NDEV, stride=4), :] = w

    def get_words(slot):
        return decode([rwords[slot, pl.ds(j, NDEV, stride=4), :] for j in range(4)])

    def next_to(shift):
        other = (me + shift + NDEV) % NDEV
        return (other // SLABS, other % SLABS)

    def edge_copies(src, rows_prev, rows_next, dst, sem):
        for way, (shift, rows) in enumerate(((-1, rows_prev), (1, rows_next))):
            yield pltpu.make_async_remote_copy(
                src_ref=src.at[pl.ds(rows, REACH)],
                dst_ref=dst.at[1 - way],
                send_sem=sem.at[way],
                recv_sem=sem.at[3 - way],
                device_id=next_to(shift),
                device_id_type=MESH,
            )

    halo_copies = list(edge_copies(charge, 0, BLOCKS - REACH, halo, halo_sem))
    rim_copies = list(edge_copies(ext, BLOCKS, BLOCKS + REACH, rim, rim_sem))

    def place(index):
        return jnp.where(index < 128, index, jnp.where(index < 136, index - 136, index - 8))

    def near_forward():
        for copy in halo_copies:
            copy.wait_recv()
        before = jnp.where(me == 0, 0.0, halo[0])
        after = jnp.where(me == NDEV - 1, 0.0, halo[1])
        source = cat([charge[...], before, after], 0).astype(BF16)
        spot = place(iota((128, 144), 1)) - iota((128, 144), 0)
        for k in range(4):
            pick = jnp.where(spot == column(offset_ref[k:k + 1, :]), one, zero).astype(BF16)
            xs[pl.ds(k, 128, stride=4), :] = dot(pick, source)
        pltpu.make_async_copy(near_mat, near_mat, near_sem).wait()
        acc[...] = jnp.zeros((512, 128), F32)

        def body(c, carry):
            col = pl.ds(pl.multiple_of(c * 256, 256), 256)
            gather = jnp.where(
                iota((256, 128), 1) % 64 == c * 4 + iota((256, 128), 0) // 64, one, zero
            ).astype(BF16)
            for r in range(4):
                row = pl.ds(128 * r, 128)
                x = xs[row, :]
                hi, lo = split(near_mat[row, col].astype(F32) * cat([x, x], 1))
                acc[row, :] = acc[row, :] + (dot(hi, gather) + dot(lo, gather))
            return carry

        lax.fori_loop(0, 16, body, 0)
        near[...] = sum(acc[pl.ds(k, 128, stride=4), :] for k in range(4))

    def near_adjoint():
        for k in range(4):
            xs[pl.ds(k, 128, stride=4), :] = val[...]
        acc[...] = jnp.zeros((512, 128), F32)

        def body(c, carry):
            col = pl.ds(pl.multiple_of(c * 256, 256), 256)
            spread = jnp.where(
                iota((128, 256), 0) == c * 4 + iota((128, 256), 1) // 64, one, zero
            ).astype(BF16)
            for r in range(4):
                row = pl.ds(128 * r, 128)
                p = near_mat[row, col].astype(F32) * dot(xs[row, :].astype(BF16), spread)
                acc[row, :] = acc[row, :] + (p[:, :128] + p[:, 128:])
            return carry

        lax.fori_loop(0, 16, body, 0)

    def near_scatter():
        acc[...] = acc[...] + pltpu.roll(acc[...], 64, 1)
        total = jnp.zeros((144, 128), F32)
        spot = place(iota((144, 128), 0)) - iota((144, 128), 1)
        for k in range(4):
            pick = jnp.where(spot == offset_ref[k:k + 1, :], one, zero).astype(BF16)
            hi, lo = split(acc[pl.ds(k, 128, stride=4), :])
            total = total + (dot(pick, hi) + dot(pick, lo))
        ext[...] = total
        for copy in rim_copies:
            copy.start()

    def pack(kk, carry):
        gsend[pl.ds(kk, 32, stride=32), :] = green_ref[:, pl.ds(pl.multiple_of(kk * LANES, LANES), LANES)]
        return carry

    lax.fori_loop(0, 32, pack, 0)

    def green_copies():
        k2 = me // 8

        def body(j, carry):
            k1 = (me % 8) * 32 + j
            low = jnp.where(k1 < 128, 1, 0)
            is_mid = jnp.where(k1 == 128, 1, 0)
            is_zero = jnp.where(k1 == 0, 1, 0)
            high = 1 - low - is_mid
            target_dev = low * k1 + high * (256 - k1)
            upper = k2 // 8
            beyond = jnp.where(k2 > 8, 1, 0)
            slot_zero = (1 - upper) * k2 + upper * (1 - beyond) * 16 + beyond * (32 - k2)
            slot_mid = (1 - upper) * (8 + k2) + upper * (39 - k2)
            slot = (low - is_zero) * k2 + is_zero * slot_zero + is_mid * slot_mid + high * (31 - k2)
            src = gsend.at[pl.ds(pl.multiple_of(j * 32, 32), 32)]
            dst = grecv.at[pl.ds(pl.multiple_of(slot * 32, 32), 32)]

            @pl.when(target_dev != me)
            def _():
                pltpu.make_async_remote_copy(
                    src_ref=src, dst_ref=dst, send_sem=gsend_sem.at[j], recv_sem=grecv_sem,
                    device_id=(target_dev // SLABS, target_dev % SLABS), device_id_type=MESH,
                ).start()

            @pl.when(target_dev == me)
            def _():
                pltpu.make_async_copy(src, dst, grecv_sem).start()

            return carry

        lax.fori_loop(0, 32, body, 0)

    def green_sent():
        def body(j, carry):
            k1 = (me % 8) * 32 + j
            low = jnp.where(k1 < 128, 1, 0)
            high = jnp.where(k1 > 128, 1, 0)
            target_dev = low * k1 + high * (256 - k1)

            @pl.when(target_dev != me)
            def _():
                part = pl.ds(pl.multiple_of(j * 32, 32), 32)
                pltpu.make_async_copy(gsend.at[part], grecv.at[part], gsend_sem.at[j]).wait()

            return carry

        lax.fori_loop(0, 32, body, 0)

    def green_ready():
        pltpu.make_async_copy(gsend, grecv, grecv_sem).wait()
        scale = 2.0 ** -24
        flip = jnp.where((rows128 + lanes128 == 128) & (rows128 > 0), one, zero).astype(BF16)
        first = jnp.where((rows128 == 0) & (lanes128 == 0), one, zero).astype(BF16)
        eye = jnp.where(rows128 == lanes128, one, zero).astype(BF16)
        turn = cat([flip, first], 1)
        special = (lanes128 % 16 == 0) & (me == 0)

        def rows_of(base, kappa):
            return cat(
                [grecv[pl.ds(base * 32 + kappa(n), 16, stride=32), :] for n in range(8)], 0
            )

        for m in range(4):
            def plain(base):
                hi, lo = split(rows_of(base, lambda n: m + 4 * n))
                return dot_nt(eye, hi) + dot_nt(eye, lo)

            def turned(base):
                one_ = rows_of(base, lambda n: 31 - m - 4 * n)
                two_ = rows_of(base, lambda n: (32 - m - 4 * n) % 32)
                hi, lo = split(cat([one_, two_], 1))
                return dot_nt(turn, hi) + dot_nt(turn, lo)

            d, dr, o, orr = plain(0), turned(0), plain(16), turned(16)
            ga[:, m * LANES:(m + 1) * LANES] = (d + jnp.where(special, dr, orr)) * scale
            gb[:, m * LANES:(m + 1) * LANES] = (jnp.where(special, o, d) + orr) * scale

    lane64 = iota((128, 128), 1) // 64
    row16 = iota((128, 128), 0) % 16

    def project():
        v = val[...]
        spread = cat(
            [jnp.where(lane64 + 2 * i == row16, v, 0.0).astype(BF16) for i in range(8)], 1
        )
        for g in range(8):
            part = stencil[g * 1024:(g + 1) * 1024, :]
            tv[g * 16:(g + 1) * 16, :] = dot(spread[g * 16:(g + 1) * 16, :], part)
        hi, lo = split(tv[...])
        return dot(out_pick, hi) + dot(out_pick, lo)

    def interpolate(own_tiles):
        rows = []
        l64, r16 = iota((16, 128), 1) // 64, iota((16, 128), 0)
        for g in range(8):
            part = stencil[g * 1024:(g + 1) * 1024, :]
            r = dot_nt(own_tiles[g * 16:(g + 1) * 16, :], part)
            acc = jnp.zeros((16, 128), F32)
            for i in range(8):
                acc = acc + jnp.where(l64 + 2 * i == r16, r[:, i * LANES:(i + 1) * LANES], 0.0)
            rows.append(acc)
        far = cat(rows, 0)
        return far + pltpu.roll(far, 64, 1)

    def cmul(re, im, c, s):
        return re * c + im * s, im * c - re * s

    def cmul_conj(re, im, c, s):
        return re * c - im * s, im * c + re * s

    def lane_tile(x, j):
        return x[:, j * LANES:(j + 1) * LANES]

    head = iota((8, 128), 0) == 0

    def special_rows(parts, slot, outs):
        small = dot3(split(cat([p[:8] for p in parts], 0)), mat(slot))
        fixed = []
        for j in range(4):
            out = outs[j]
            h2 = iota((8, 256), 0) == 0
            fixed.append(cat([jnp.where(h2, small[8 * j:8 * j + 8], out[:8]), out[8:]], 0))
        return fixed

    def evaluate(which):
        step0 = which * 4
        first, last = which == 0, which == 1
        fwd, inv_ = which * 2, which * 2 + 1
        out = project()
        for k in range(2):
            for h in range(2):
                put(fwd, 2 * k + h, lane_tile(out[128 * k:128 * k + 128], h))

        @pl.when(first)
        def _():
            put(0, 4, id_rows)
            pl.semaphore_wait(barrier, NDEV - 1)
            exchange(0, sbuf.at[0], rbuf.at[0], MSG, 5)
            green_copies()
            for copy in halo_copies:
                copy.start()
            arrived(0, sbuf.at[0], rbuf.at[0], 5)
            idm = get(0, 4)
            tc = iota((128, 256), 1)
            for tr in range(2):
                pick = cat(
                    [
                        jnp.where(idm[:, k:k + 1].astype(jnp.int32) == tc + (tr * 256 + 1), one, zero)
                        for k in range(2)
                    ],
                    0,
                ).astype(BF16)
                for t in range(2):
                    wf[2 * tr + t] = dot_nt(mats[t], pick).astype(BF16)
                    wi[t, :, tr * 256:(tr + 1) * 256] = dot_nt(pick, mats[t]).astype(BF16)

        @pl.when(last)
        def _():
            exchange(4, sbuf.at[2], rbuf.at[2], MSG, 4)
            near_adjoint()
            arrived(4, sbuf.at[2], rbuf.at[2], 4)

        tiles = split(
            cat([cat([get(fwd, 2 * k + h) for h in range(2)], 1) for k in range(2)], 0)
        )
        c2, s2 = t2_ref[:, :LANES], t2_ref[:, LANES:]
        parts = []
        for tr in range(2):
            y = dot3((wf[2 * tr], wf[2 * tr + 1]), tiles)
            for h in range(2):
                re, im = cmul(lane_tile(y[:128], h), lane_tile(y[128:], h), c2, s2)
                parts.append(cat([re, im], 1))
        prod = dot3(split(cat(parts, 0)), mat(1))
        outs = special_rows(parts, 3, [prod[128 * j:128 * j + 128] for j in range(4)])
        put_words(fwd, [o[:, :LANES] for o in outs], [o[:, LANES:] for o in outs])
        exchange(step0 + 1, swords.at[fwd], rwords.at[fwd], 4, 4)

        @pl.when(first)
        def _():
            green_ready()

        @pl.when(last)
        def _():
            near_scatter()

        arrived(step0 + 1, swords.at[fwd], rwords.at[fwd], 4)
        re, im = get_words(fwd)
        y = dot3(mat(5), split(cat([cat(re, 1), cat(im, 1)], 0)))
        re, im = cmul(y[:128], y[128:], t1_ref[:, :512], t1_ref[:, 512:])
        r = [lane_tile(re, j) for j in range(4)]
        i = [lane_tile(im, j) for j in range(4)]
        er, ei, dr, di = r[0] + r[2], i[0] + i[2], r[0] - r[2], i[0] - i[2]
        fr, fi, hr, hi_ = r[1] + r[3], i[1] + i[3], r[1] - r[3], i[1] - i[3]
        vs = [(er + fr, ei + fi), (dr + hi_, di - hr), (er - fr, ei - fi), (dr - hi_, di + hr)]
        parts = []
        for m in range(4):
            cm, sm = tm_ref[m:m + 1, :LANES], tm_ref[m:m + 1, LANES:]
            parts.append(cat(list(cmul(vs[m][0], vs[m][1], cm, sm)), 1))
        f = dot3(split(cat(parts, 0)), mat(7))
        both = []
        for g in (ga, gb):
            for m in range(4):
                gm = g[:, m * LANES:(m + 1) * LANES]
                fm = f[128 * m:128 * m + 128]
                both.append(cat([fm[:, :LANES] * gm, fm[:, LANES:] * gm], 1))
        p = dot3(split(cat(both, 0)), mat(8))
        stacked = []
        for e in range(2):
            vs = []
            for m in range(4):
                cm, sm = tm_ref[m:m + 1, :LANES], tm_ref[m:m + 1, LANES:]
                pm = p[512 * e + 128 * m:512 * e + 128 * m + 128]
                vs.append(cmul_conj(pm[:, :LANES], pm[:, LANES:], cm, sm))
            r = [v[0] for v in vs]
            i = [v[1] for v in vs]
            er, ei, dr, di = r[0] + r[2], i[0] + i[2], r[0] - r[2], i[0] - i[2]
            fr, fi, hr, hi_ = r[1] + r[3], i[1] + i[3], r[1] - r[3], i[1] - i[3]
            zs = [(er + fr, ei + fi), (dr - hi_, di + hr), (er - fr, ei - fi), (dr + hi_, di - hr)]
            re, im = cmul_conj(
                cat([z[0] for z in zs], 1), cat([z[1] for z in zs], 1),
                t1_ref[:, :512], t1_ref[:, 512:],
            )
            stacked.append(split(cat([re, im], 0)))
        inv = mat(6)
        yr = dot3((inv[0][:128], inv[1][:128]), stacked[0])
        yi = dot3((inv[0][128:], inv[1][128:]), stacked[1])
        put_words(inv_, [lane_tile(yr, j) for j in range(4)], [lane_tile(yi, j) for j in range(4)])
        exchange(step0 + 2, swords.at[inv_], rwords.at[inv_], 4, 4)

        @pl.when(first)
        def _():
            near_forward()

        arrived(step0 + 2, swords.at[inv_], rwords.at[inv_], 4)
        re, im = get_words(inv_)
        parts = [cat([re[j], im[j]], 1) for j in range(4)]
        prod = dot3(split(cat(parts, 0)), mat(2))
        outs = special_rows(parts, 4, [prod[128 * j:128 * j + 128] for j in range(4)])
        zs = [cmul_conj(o[:, :LANES], o[:, LANES:], c2, s2) for o in outs]
        y = cat(
            [
                cat([cat([zs[2 * tr][0], zs[2 * tr + 1][0]], 1), cat([zs[2 * tr][1], zs[2 * tr + 1][1]], 1)], 0)
                for tr in range(2)
            ],
            0,
        )
        back = dot3((wi[0], wi[1]), split(y)).astype(BF16).astype(F32)
        for k in range(2):
            for h in range(2):
                put(inv_, 2 * k + h, lane_tile(back[128 * k:128 * k + 128], h))
        exchange(step0 + 3, sbuf.at[inv_], rbuf.at[inv_], MSG, 4)
        arrived(step0 + 3, sbuf.at[inv_], rbuf.at[inv_], 4)
        tiles = cat(
            [cat([get(inv_, 2 * k + h) for h in range(2)], 1) for k in range(2)], 0
        ).astype(BF16)
        far = interpolate(dot(in_pick, tiles).astype(BF16))

        @pl.when(first)
        def _():
            pot = far + near[...]
            val[...] = (pot - goal[...]).astype(BF16).astype(F32)
            fold(pot_ref, tv2, pot)

        @pl.when(last)
        def _():
            for copy in rim_copies:
                copy.wait_recv()
            before = jnp.where(me == 0, 0.0, rim[0])
            after = jnp.where(me == NDEV - 1, 0.0, rim[1])
            grad = far + ext[:BLOCKS, :]
            grad = cat(
                [grad[:REACH] + before, grad[REACH:BLOCKS - REACH], grad[BLOCKS - REACH:] + after], 0
            )
            fold(grad_ref, tv2, grad)

    tv2 = goal
    load.wait()

    def both_passes(which, carry):
        evaluate(which)
        return carry

    lax.fori_loop(0, 2, both_passes, 0)
    for p in range(2):
        sent(4 * p, sbuf.at[2 * p], rbuf.at[2 * p], 5 - p)
        sent(4 * p + 1, swords.at[2 * p], rwords.at[2 * p], 4)
        sent(4 * p + 2, swords.at[2 * p + 1], rwords.at[2 * p + 1], 4)
        sent(4 * p + 3, sbuf.at[2 * p + 1], rbuf.at[2 * p + 1], 4)
    green_sent()
    for copy in halo_copies + rim_copies:
        copy.wait_send()


def local(tables, charges, target, stencil, near_matrix, green, block_dest, block_tile, near_offset):
    vmem = pl.BlockSpec(memory_space=pltpu.VMEM)
    hbm = pl.BlockSpec(memory_space=pl.ANY)
    pot, grad = pl.pallas_call(
        kernel,
        out_shape=(jax.ShapeDtypeStruct((64, LANES), F32),) * 2,
        in_specs=[vmem, vmem, hbm, hbm] + [vmem] * (4 + len(tables)),
        out_specs=(vmem, vmem),
        scratch_shapes=[
            pltpu.VMEM((BLOCKS * PANEL, CELLS), BF16),
            pltpu.VMEM((4 * BLOCKS, PANEL * PANEL), BF16),
            pltpu.VMEM((4, ROWS, LANES), F32),
            pltpu.VMEM((4, ROWS, LANES), F32),
            pltpu.VMEM((4, 4 * NDEV, LANES), jnp.int32),
            pltpu.VMEM((4, 4 * NDEV, LANES), jnp.int32),
            pltpu.VMEM((1024, LANES), F32),
            pltpu.VMEM((1024, LANES), F32),
            pltpu.VMEM((128, 512), F32),
            pltpu.VMEM((128, 512), F32),
            pltpu.VMEM((128, 128), F32),
            pltpu.VMEM((128, 128), F32),
            pltpu.VMEM((128, 128), F32),
            pltpu.VMEM((128, 256), F32),
            pltpu.VMEM((4, 256, 256), BF16),
            pltpu.VMEM((2, 256, 512), BF16),
            pltpu.VMEM((18, 256, 256), BF16),
            pltpu.VMEM((512, LANES), F32),
            pltpu.VMEM((512, LANES), F32),
            pltpu.VMEM((128, LANES), F32),
            pltpu.VMEM((144, LANES), F32),
            pltpu.VMEM((2, REACH, LANES), F32),
            pltpu.VMEM((2, REACH, LANES), F32),
            pltpu.SemaphoreType.DMA((8,)),
            pltpu.SemaphoreType.DMA((8,)),
            pltpu.SemaphoreType.DMA((32,)),
            pltpu.SemaphoreType.DMA,
            pltpu.SemaphoreType.DMA,
            pltpu.SemaphoreType.DMA,
            pltpu.SemaphoreType.DMA((4,)),
            pltpu.SemaphoreType.DMA((4,)),
        ],
        compiler_params=pltpu.CompilerParams(collective_id=0, has_side_effects=True),
        name="panel_solver",
    )(
        charges.reshape(64, LANES), target.reshape(64, LANES),
        stencil.reshape(BLOCKS * PANEL, CELLS), near_matrix, green.T,
        block_dest.reshape(1, BLOCKS), block_tile.reshape(1, BLOCKS), near_offset.T, *tables,
    )
    return (pot.reshape(-1), grad.reshape(-1))


def solution(mesh):
    made = make_tables()
    tables = [jnp.asarray(made[name]) for name in TABLES]
    return jax.shard_map(
        functools.partial(local, tables),
        mesh=mesh,
        in_specs=(
            P(("panel", "slab")),
            P(("panel", "slab")),
            P(("panel", "slab"), None, None),
            P(("panel", "slab"), None, None),
            P(None, ("panel", "slab")),
            P(("panel", "slab"), None),
            P(("panel", "slab")),
            P(("panel", "slab"), None),
        ),
        out_specs=(P(("panel", "slab")), P(("panel", "slab"))),
        check_vma=False,
    )
```

```python
import functools
import math

import jax
import jax.numpy as jnp
import numpy as np
from jax import lax
from jax.experimental import pallas as pl
from jax.experimental.pallas import tpu as pltpu
from jax.sharding import PartitionSpec as P

GRID = 4096
TILE = 16
REACH = 8
NDEV = 128
SLABS = 4
BLOCKS = 128
PANEL = 64
CELLS = 256
LANES = 128
MSG = 8
ROWS = NDEV * MSG
MESH = pl.DeviceIdType.MESH
F32 = jnp.float32
BF16 = jnp.bfloat16
TABLES = (("w1", 256), ("m0", 256), ("m0i", 256), ("w2", 128), ("a1", 128), ("w3", 128), ("t2", 128),
          ("c0", 128), ("c1", 128), ("s0", 128), ("s1", 128), ("tm", 8))
START = {name: sum(n for _, n in TABLES[:i]) for i, (name, _) in enumerate(TABLES)}
TABLE_ROWS = sum(n for _, n in TABLES)


def make_tables():
    def angle(rows, cols, modulus):
        return 2.0 * math.pi / modulus * ((np.outer(rows, cols)) % modulus)

    out = {}
    th = angle(np.arange(128), np.arange(256), 256)
    w1 = np.concatenate([np.cos(th), -np.sin(th)], 0)
    w1[128] = (-1.0) ** np.arange(256)
    out["w1"] = w1
    th = angle(np.arange(16), np.arange(16), 16)
    c, s = np.kron(np.eye(8), np.cos(th)), np.kron(np.eye(8), np.sin(th))
    out["w2"] = np.concatenate([c, s], 1)
    m0 = np.zeros((2, 16, 2, 16))
    idx = np.arange(16)
    m0[0, :, 0, 0] = 1.0
    m0[0, :, 1, 0] = (-1.0) ** idx
    for k in range(1, 8):
        t = 2 * math.pi * ((idx * k) % 16) / 16
        m0[0, :, 0, k], m0[0, :, 1, k] = np.cos(t), -np.sin(t)
    for n in range(8):
        t = 2 * math.pi * ((idx * (1 + 2 * n)) % 32) / 32
        m0[1, :, 0, 8 + n], m0[1, :, 1, 8 + n] = np.cos(t), -np.sin(t)
    big = np.zeros((2, 8, 16, 2, 8, 16))
    for a in range(8):
        big[:, a, :, :, a, :] = m0
    out["m0"] = big.reshape(256, 256)
    inv = m0.copy()
    inv[:, :, :, 0] *= 0.5
    big = np.zeros((2, 8, 16, 2, 8, 16))
    for a in range(8):
        big[:, a, :, :, a, :] = inv
    out["m0i"] = big.reshape(256, 256).T
    th = angle(np.arange(128), np.arange(128), 128)
    out["a1"] = np.concatenate([np.cos(th), np.sin(th)], 1)
    th = angle(np.arange(8), np.arange(8), 8)
    out["w3"] = np.concatenate([np.kron(np.cos(th), np.eye(16)), np.kron(np.sin(th), np.eye(16))], 1)
    th = np.tile(angle(np.arange(128), np.arange(16), GRID), (1, 8))
    th[0] = 0.0
    out["t2"] = np.concatenate([np.cos(th), np.sin(th)], 1)
    th = np.repeat(angle(np.arange(128), np.arange(32), GRID), 16, axis=1)
    out["c0"], out["c1"] = np.cos(th[:, :256]), np.cos(th[:, 256:])
    out["s0"], out["s1"] = np.sin(th[:, :256]), np.sin(th[:, 256:])
    th = np.repeat(angle(np.arange(4), np.arange(8), 32), 16, axis=1)
    tm = np.zeros((8, 256))
    tm[:4] = np.concatenate([np.cos(th), np.sin(th)], 1)
    out["tm"] = tm
    return np.concatenate([out[name] for name, _ in TABLES], 0).astype(np.float32)


def dot(a, b):
    return lax.dot_general(a, b, (((1,), (0,)), ((), ())), preferred_element_type=F32)


def dot_nt(a, b):
    return lax.dot_general(a, b, (((1,), (1,)), ((), ())), preferred_element_type=F32)


def split(x):
    hi = x.astype(BF16)
    return hi, (x - hi.astype(F32)).astype(BF16)


def dot3(a, b):
    return dot(a[0], b[0]) + (dot(a[0], b[1]) + dot(a[1], b[0]))


def iota(shape, dim):
    return lax.broadcasted_iota(jnp.int32, shape, dim)


def cat(parts, axis):
    return jnp.concatenate(parts, axis=axis)


COMBOS = sorted(
    ((dz, dx) for dz in range(4) for dx in range(4)),
    key=lambda c: -(min(c[0], 4 - c[0]) + min(c[1], 4 - c[1])),
)
Z_DIGITS = sum(c[0] << (2 * i) for i, c in enumerate(COMBOS))
X_DIGITS = sum(c[1] << (2 * i) for i, c in enumerate(COMBOS))


def encode(re, im):
    top = jnp.abs(re[0])
    for x in list(re[1:]) + list(im):
        top = jnp.maximum(top, jnp.abs(x))
    top = jnp.maximum(top, 2.0 ** -100)
    power = jnp.floor(jnp.log2(top)) + 1.0
    scale = jnp.exp2(14.0 - power)
    code = power.astype(jnp.int32) + 128

    def mantissa(x):
        return jnp.minimum(x * scale + 16384.5, 32767.5).astype(jnp.int32)

    return [
        (((code >> (2 * j)) & 3) << 30) | (mantissa(re[j]) << 15) | mantissa(im[j])
        for j in range(4)
    ]


def decode(words):
    code = words[0] >> 30 & 3
    for j in range(1, 4):
        code = code | ((words[j] >> 30 & 3) << (2 * j))
    scale = jnp.exp2(code.astype(F32) - 142.0)
    re = [((w >> 15 & 32767).astype(F32) - 16384.0) * scale for w in words]
    im = [((w & 32767).astype(F32) - 16384.0) * scale for w in words]
    return re, im


def kernel(
    q_hbm, target_hbm, stencil_hbm, near_hbm, green_hbm, dest_hbm, tile_hbm, offset_hbm, table_hbm,
    out_ref,
    q_ref, target_ref, green_ref, dest_ref, tile_ref, offset_ref, table,
    stencil, near_mat, sbuf, rbuf, sback, rback, swords, rwords, gsend, grecv, ga, gb, val, charge, goal, tv,
    wf, wi, mats, xs, acc, near, ext, halo, rim,
    send_sem, recv_sem, gsend_sem, grecv_sem, load_sem, near_sem, halo_sem, rim_sem,
):
    panel = lax.axis_index("panel")
    slab = lax.axis_index("slab")
    me = panel * SLABS + slab
    pz, px, pc = panel // 8, (panel // 2) % 4, panel % 2

    loads = {}
    for i, (name, src, dst) in enumerate((
        ("q", q_hbm, q_ref), ("dest", dest_hbm, dest_ref), ("tile", tile_hbm, tile_ref),
        ("stencil", stencil_hbm, stencil), ("table", table_hbm, table),
        ("green", green_hbm, green_ref), ("offset", offset_hbm, offset_ref),
        ("target", target_hbm, target_ref),
    )):
        loads[name] = pltpu.make_async_copy(src, dst, load_sem.at[i])
        loads[name].start()

    def rows_at(name):
        n = dict(TABLES)[name]
        return table[START[name]:START[name] + n, :]

    def half_at(name, half):
        n = dict(TABLES)[name]
        return table[START[name]:START[name] + n, half * LANES:(half + 1) * LANES]

    def others(visit):
        def body(g, carry):
            z = (pz + ((Z_DIGITS >> (2 * g)) & 3)) % 4
            x = (px + ((X_DIGITS >> (2 * g)) & 3)) % 4
            for dy in (2, 1, 3, 0):
                for dc in (1, 0):
                    def go(z=z, x=x, dy=dy, dc=dc):
                        visit(z * 8 + x * 2 + (pc + dc) % 2, (slab + dy) % 4)

                    if dy == 0 and dc == 0:
                        pl.when(g != 15)(go)
                    else:
                        go()
            return carry

        lax.fori_loop(0, 16, body, 0)

    barrier = pltpu.get_barrier_semaphore()
    others(
        lambda p, y: pl.semaphore_signal(barrier, inc=1, device_id=(p, y), device_id_type=MESH)
    )

    def near_load(b, carry):
        pltpu.make_async_copy(
            near_hbm.at[b], near_mat.at[pl.ds(pl.multiple_of(b * 4, 4), 4)], near_sem
        ).start()
        return carry

    rows128, lanes128 = iota((128, 128), 0), iota((128, 128), 1)

    def unfold(ref, out):
        x = ref[...].astype(F32)
        y = pltpu.roll(x, 64, 1)
        low = iota((64, 128), 1) < 64
        out[pl.ds(0, 64, stride=2), :] = jnp.where(low, x, y)
        out[pl.ds(1, 64, stride=2), :] = jnp.where(low, y, x)

    def fold(row, value):
        goal[...] = value
        low = iota((64, 128), 1) < 64
        out_ref[row:row + 64, :] = jnp.where(
            low, goal[pl.ds(0, 64, stride=2), :], goal[pl.ds(1, 64, stride=2), :]
        )

    loads["q"].wait()
    unfold(q_ref, charge)
    val[...] = charge[...]

    def pair(slot, value):
        hi, lo = split(value)
        mats[2 * slot] = hi
        mats[2 * slot + 1] = lo

    def mat(slot):
        return mats[2 * slot], mats[2 * slot + 1]

    def split_tables():
        def circle(name):
            return half_at(name, 0), half_at(name, 1)

        pair(0, rows_at("w1"))
        c, s = circle("w2")
        pair(1, cat([cat([c, -s], 1), cat([s, c], 1)], 0))
        pair(2, cat([cat([c, s], 1), cat([-s, c], 1)], 0))
        pair(3, rows_at("m0"))
        pair(4, rows_at("m0i"))
        c, s = circle("a1")
        pair(5, cat([cat([c, s], 1), cat([-s, c], 1)], 0))
        pair(6, cat([cat([c, -s], 1), cat([s, c], 1)], 0))
        c, s = circle("w3")
        pair(7, cat([cat([c, -s], 1), cat([s, c], 1)], 0))
        pair(8, cat([cat([c, s], 1), cat([-s, c], 1)], 0))

    loads["dest"].wait()
    loads["tile"].wait()
    dest_row = dest_ref[...]
    tile_row = tile_ref[...]

    def column(row):
        return jnp.sum(jnp.where(rows128 == lanes128, row, 0), axis=1, keepdims=True)

    dest_col = column(dest_row)
    same = dest_col == dest_row
    rank_row = jnp.sum(jnp.where(same & (rows128 < lanes128), 1, 0), axis=0, keepdims=True)
    rank_col = jnp.sum(jnp.where(same & (lanes128 < rows128), 1, 0), axis=1, keepdims=True)
    one, zero = F32(1.0), F32(0.0)
    out_pick = cat(
        [jnp.where((dest_row == rows128) & (rank_row == k), one, zero) for k in range(2)], 0
    )
    wanted = iota((128, 512), 1) - 4 * dest_col - 2 * rank_col
    in_pick = [jnp.where(wanted == h, one, zero).astype(BF16) for h in range(2)]
    ids = jnp.sum(out_pick * (tile_row + 1).astype(F32), axis=1, keepdims=True)
    id_rows = jnp.where(lanes128 == 0, ids[:128], jnp.where(lanes128 == 1, ids[128:], 0.0))
    out_pick = out_pick.astype(BF16)

    def exchange(step, src, dst, stride, count):
        mine = pl.ds(pl.multiple_of(me * stride, stride), count)

        def send(p, y):
            theirs = pl.ds(pl.multiple_of((p * SLABS + y) * stride, stride), count)
            pltpu.make_async_remote_copy(
                src_ref=src.at[theirs],
                dst_ref=dst.at[mine],
                send_sem=send_sem.at[step],
                recv_sem=recv_sem.at[step],
                device_id=(p, y),
                device_id_type=MESH,
            ).start()

        others(send)
        pltpu.make_async_copy(src.at[mine], dst.at[mine], recv_sem.at[step]).start()

    def arrived(step, src, dst, count):
        part = pl.ds(0, NDEV * count)
        pltpu.make_async_copy(src.at[part], dst.at[part], recv_sem.at[step]).wait()

    def sent(step, src, dst, count):
        part = pl.ds(0, (NDEV - 1) * count)
        pltpu.make_async_copy(src.at[part], dst.at[part], send_sem.at[step]).wait()

    def put(slot, row, value):
        sbuf[slot, pl.ds(row, NDEV, stride=MSG), :] = value

    def get(slot, row):
        return rbuf[slot, pl.ds(row, NDEV, stride=MSG), :]

    def put_words(slot, re, im):
        for j, w in enumerate(encode(re, im)):
            swords[slot, pl.ds(j, NDEV, stride=4), :] = w

    def get_words(slot):
        return decode([rwords[slot, pl.ds(j, NDEV, stride=4), :] for j in range(4)])

    def next_to(shift):
        other = (me + shift + NDEV) % NDEV
        return (other // SLABS, other % SLABS)

    def edge_copies(src, rows_prev, rows_next, dst, sem):
        for way, (shift, rows) in enumerate(((-1, rows_prev), (1, rows_next))):
            yield pltpu.make_async_remote_copy(
                src_ref=src.at[pl.ds(rows, REACH)],
                dst_ref=dst.at[1 - way],
                send_sem=sem.at[way],
                recv_sem=sem.at[3 - way],
                device_id=next_to(shift),
                device_id_type=MESH,
            )

    halo_copies = list(edge_copies(charge, 0, BLOCKS - REACH, halo, halo_sem))
    rim_copies = list(edge_copies(ext, BLOCKS, BLOCKS + REACH, rim, rim_sem))

    def place(index):
        return jnp.where(index < 128, index, jnp.where(index < 136, index - 136, index - 8))

    def near_forward():
        loads["offset"].wait()
        for copy in halo_copies:
            copy.wait_recv()
        before = jnp.where(me == 0, 0.0, halo[0])
        after = jnp.where(me == NDEV - 1, 0.0, halo[1])
        source = cat([charge[...], before, after], 0).astype(BF16)
        spot = place(iota((128, 144), 1)) - iota((128, 144), 0)
        for k in range(4):
            pick = jnp.where(spot == column(offset_ref[k:k + 1, :]), one, zero).astype(BF16)
            xs[pl.ds(k, 128, stride=4), :] = dot(pick, source)
        pltpu.make_async_copy(near_mat, near_mat, near_sem).wait()
        acc[...] = jnp.zeros((512, 128), F32)

        def body(c, carry):
            col = pl.ds(pl.multiple_of(c * 256, 256), 256)
            gather = jnp.where(
                iota((256, 128), 1) % 64 == c * 4 + iota((256, 128), 0) // 64, one, zero
            ).astype(BF16)
            for r in range(4):
                row = pl.ds(128 * r, 128)
                x = xs[row, :]
                hi, lo = split(near_mat[row, col].astype(F32) * cat([x, x], 1))
                acc[row, :] = acc[row, :] + (dot(hi, gather) + dot(lo, gather))
            return carry

        lax.fori_loop(0, 16, body, 0)
        near[...] = sum(acc[pl.ds(k, 128, stride=4), :] for k in range(4))

    def near_adjoint():
        for k in range(4):
            xs[pl.ds(k, 128, stride=4), :] = val[...]
        acc[...] = jnp.zeros((512, 128), F32)

        def body(c, carry):
            col = pl.ds(pl.multiple_of(c * 256, 256), 256)
            spread = jnp.where(
                iota((128, 256), 0) == c * 4 + iota((128, 256), 1) // 64, one, zero
            ).astype(BF16)
            for r in range(4):
                row = pl.ds(128 * r, 128)
                p = near_mat[row, col].astype(F32) * dot(xs[row, :].astype(BF16), spread)
                acc[row, :] = acc[row, :] + (p[:, :128] + p[:, 128:])
            return carry

        lax.fori_loop(0, 16, body, 0)

    def near_scatter():
        acc[...] = acc[...] + pltpu.roll(acc[...], 64, 1)
        total = jnp.zeros((144, 128), F32)
        spot = place(iota((144, 128), 0)) - iota((144, 128), 1)
        for k in range(4):
            pick = jnp.where(spot == offset_ref[k:k + 1, :], one, zero).astype(BF16)
            hi, lo = split(acc[pl.ds(k, 128, stride=4), :])
            total = total + (dot(pick, hi) + dot(pick, lo))
        ext[...] = total
        for copy in rim_copies:
            copy.start()

    def pack(kk, carry):
        gsend[pl.ds(kk, 32, stride=32), :] = green_ref[:, pl.ds(pl.multiple_of(kk * LANES, LANES), LANES)]
        return carry

    def green_copies():
        k2 = me // 8

        def body(j, carry):
            k1 = (me % 8) * 32 + j
            low = jnp.where(k1 < 128, 1, 0)
            is_mid = jnp.where(k1 == 128, 1, 0)
            is_zero = jnp.where(k1 == 0, 1, 0)
            high = 1 - low - is_mid
            target_dev = low * k1 + high * (256 - k1)
            upper = k2 // 8
            beyond = jnp.where(k2 > 8, 1, 0)
            slot_zero = (1 - upper) * k2 + upper * (1 - beyond) * 16 + beyond * (32 - k2)
            slot_mid = (1 - upper) * (8 + k2) + upper * (39 - k2)
            slot = (low - is_zero) * k2 + is_zero * slot_zero + is_mid * slot_mid + high * (31 - k2)
            src = gsend.at[pl.ds(pl.multiple_of(j * 32, 32), 32)]
            dst = grecv.at[pl.ds(pl.multiple_of(slot * 32, 32), 32)]

            @pl.when(target_dev != me)
            def _():
                pltpu.make_async_remote_copy(
                    src_ref=src, dst_ref=dst, send_sem=gsend_sem.at[j], recv_sem=grecv_sem,
                    device_id=(target_dev // SLABS, target_dev % SLABS), device_id_type=MESH,
                ).start()

            @pl.when(target_dev == me)
            def _():
                pltpu.make_async_copy(src, dst, grecv_sem).start()

            return carry

        lax.fori_loop(0, 32, body, 0)

    def green_sent():
        def body(j, carry):
            k1 = (me % 8) * 32 + j
            low = jnp.where(k1 < 128, 1, 0)
            high = jnp.where(k1 > 128, 1, 0)
            target_dev = low * k1 + high * (256 - k1)

            @pl.when(target_dev != me)
            def _():
                part = pl.ds(pl.multiple_of(j * 32, 32), 32)
                pltpu.make_async_copy(gsend.at[part], grecv.at[part], gsend_sem.at[j]).wait()

            return carry

        lax.fori_loop(0, 32, body, 0)

    def green_ready():
        pltpu.make_async_copy(gsend, grecv, grecv_sem).wait()
        scale = 2.0 ** -24
        flip = jnp.where((rows128 + lanes128 == 128) & (rows128 > 0), one, zero).astype(BF16)
        first = jnp.where((rows128 == 0) & (lanes128 == 0), one, zero).astype(BF16)
        eye = jnp.where(rows128 == lanes128, one, zero).astype(BF16)
        turn = cat([flip, first], 1)
        special = (lanes128 % 16 == 0) & (me == 0)

        def rows_of(base, kappa):
            return cat(
                [grecv[pl.ds(base * 32 + kappa(n), 16, stride=32), :] for n in range(8)], 0
            )

        for m in range(4):
            def plain(base):
                hi, lo = split(rows_of(base, lambda n: m + 4 * n))
                return dot_nt(eye, hi) + dot_nt(eye, lo)

            def turned(base):
                one_ = rows_of(base, lambda n: 31 - m - 4 * n)
                two_ = rows_of(base, lambda n: (32 - m - 4 * n) % 32)
                hi, lo = split(cat([one_, two_], 1))
                return dot_nt(turn, hi) + dot_nt(turn, lo)

            d, dr, o, orr = plain(0), turned(0), plain(16), turned(16)
            ga[:, m * LANES:(m + 1) * LANES] = (d + jnp.where(special, dr, orr)) * scale
            gb[:, m * LANES:(m + 1) * LANES] = (jnp.where(special, o, d) + orr) * scale

    lane64 = iota((128, 128), 1) // 64
    row16 = iota((128, 128), 0) % 16

    def project():
        v = val[...]
        spread = cat(
            [jnp.where(lane64 + 2 * i == row16, v, 0.0).astype(BF16) for i in range(8)], 1
        )
        for g in range(8):
            part = stencil[g * 1024:(g + 1) * 1024, :]
            tv[g * 16:(g + 1) * 16, :] = dot(spread[g * 16:(g + 1) * 16, :], part)
        hi, lo = split(tv[...])
        return dot(out_pick, hi) + dot(out_pick, lo)

    def interpolate(own_tiles):
        rows = []
        l64, r16 = iota((16, 128), 1) // 64, iota((16, 128), 0)
        for g in range(8):
            part = stencil[g * 1024:(g + 1) * 1024, :]
            r = dot_nt(own_tiles[g * 16:(g + 1) * 16, :], part)
            acc = jnp.zeros((16, 128), F32)
            for i in range(8):
                acc = acc + jnp.where(l64 + 2 * i == r16, r[:, i * LANES:(i + 1) * LANES], 0.0)
            rows.append(acc)
        far = cat(rows, 0)
        return far + pltpu.roll(far, 64, 1)

    def cmul(re, im, c, s):
        return re * c + im * s, im * c - re * s

    def cmul_conj(re, im, c, s):
        return re * c - im * s, im * c + re * s

    def lane_tile(x, j):
        return x[:, j * LANES:(j + 1) * LANES]

    head = iota((8, 128), 0) == 0

    def special_rows(parts, slot, outs):
        small = dot3(split(cat([p[:8] for p in parts], 0)), mat(slot))
        fixed = []
        for j in range(4):
            out = outs[j]
            h2 = iota((8, 256), 0) == 0
            fixed.append(cat([jnp.where(h2, small[8 * j:8 * j + 8], out[:8]), out[8:]], 0))
        return fixed

    def evaluate(which):
        step0 = which * 4
        first, last = which == 0, which == 1
        fwd, inv_ = which * 2, which * 2 + 1
        out = project()
        for k in range(2):
            for h in range(2):
                put(which, 2 * k + h, lane_tile(out[128 * k:128 * k + 128], h))

        @pl.when(first)
        def _():
            put(0, 4, id_rows)
            pl.semaphore_wait(barrier, NDEV - 1)
            exchange(0, sbuf.at[0], rbuf.at[0], MSG, 5)
            for copy in halo_copies:
                copy.start()
            loads["green"].wait()
            lax.fori_loop(0, 32, pack, 0)
            green_copies()
            lax.fori_loop(0, BLOCKS, near_load, 0)
            loads["table"].wait()
            split_tables()
            loads["target"].wait()
            unfold(target_ref, goal)
            arrived(0, sbuf.at[0], rbuf.at[0], 5)
            idm = get(0, 4)
            tc = iota((128, 256), 1)
            for k in range(2):
                xs[pl.ds(k, 128, stride=2), :] = jnp.broadcast_to(idm[:, k:k + 1], (128, 128))
            ordered = xs[:256, :1].astype(jnp.int32)
            for tr in range(2):
                pick = cat(
                    [
                        jnp.where(idm[:, k:k + 1].astype(jnp.int32) == tc + (tr * 256 + 1), one, zero)
                        for k in range(2)
                    ],
                    0,
                ).astype(BF16)
                back_pick = jnp.where(
                    ordered == iota((256, 256), 1) + (tr * 256 + 1), one, zero
                ).astype(BF16)
                for t in range(2):
                    wf[2 * tr + t] = dot_nt(mats[t], pick).astype(BF16)
                    wi[t, :, tr * 256:(tr + 1) * 256] = dot_nt(back_pick, mats[t]).astype(BF16)

        @pl.when(last)
        def _():
            exchange(4, sbuf.at[1], rbuf.at[1], MSG, 4)
            near_adjoint()
            arrived(4, sbuf.at[1], rbuf.at[1], 4)

        tiles = split(
            cat([cat([get(which, 2 * k + h) for h in range(2)], 1) for k in range(2)], 0)
        )
        c2, s2 = half_at("t2", 0), half_at("t2", 1)
        c1 = cat([rows_at("c0"), rows_at("c1")], 1)
        s1 = cat([rows_at("s0"), rows_at("s1")], 1)
        parts = []
        for tr in range(2):
            y = dot3((wf[2 * tr], wf[2 * tr + 1]), tiles)
            for h in range(2):
                re, im = cmul(lane_tile(y[:128], h), lane_tile(y[128:], h), c2, s2)
                parts.append(cat([re, im], 1))
        prod = dot3(split(cat(parts, 0)), mat(1))
        outs = special_rows(parts, 3, [prod[128 * j:128 * j + 128] for j in range(4)])
        put_words(fwd, [o[:, :LANES] for o in outs], [o[:, LANES:] for o in outs])
        exchange(step0 + 1, swords.at[fwd], rwords.at[fwd], 4, 4)

        @pl.when(first)
        def _():
            green_ready()

        @pl.when(last)
        def _():
            near_scatter()

        arrived(step0 + 1, swords.at[fwd], rwords.at[fwd], 4)
        re, im = get_words(fwd)
        y = dot3(mat(5), split(cat([cat(re, 1), cat(im, 1)], 0)))
        re, im = cmul(y[:128], y[128:], c1, s1)
        r = [lane_tile(re, j) for j in range(4)]
        i = [lane_tile(im, j) for j in range(4)]
        er, ei, dr, di = r[0] + r[2], i[0] + i[2], r[0] - r[2], i[0] - i[2]
        fr, fi, hr, hi_ = r[1] + r[3], i[1] + i[3], r[1] - r[3], i[1] - i[3]
        vs = [(er + fr, ei + fi), (dr + hi_, di - hr), (er - fr, ei - fi), (dr - hi_, di + hr)]
        parts = []
        for m in range(4):
            cm, sm = half_at("tm", 0)[m:m + 1], half_at("tm", 1)[m:m + 1]
            parts.append(cat(list(cmul(vs[m][0], vs[m][1], cm, sm)), 1))
        f = dot3(split(cat(parts, 0)), mat(7))
        both = []
        for g in (ga, gb):
            for m in range(4):
                gm = g[:, m * LANES:(m + 1) * LANES]
                fm = f[128 * m:128 * m + 128]
                both.append(cat([fm[:, :LANES] * gm, fm[:, LANES:] * gm], 1))
        p = dot3(split(cat(both, 0)), mat(8))
        stacked = []
        for e in range(2):
            vs = []
            for m in range(4):
                cm, sm = half_at("tm", 0)[m:m + 1], half_at("tm", 1)[m:m + 1]
                pm = p[512 * e + 128 * m:512 * e + 128 * m + 128]
                vs.append(cmul_conj(pm[:, :LANES], pm[:, LANES:], cm, sm))
            r = [v[0] for v in vs]
            i = [v[1] for v in vs]
            er, ei, dr, di = r[0] + r[2], i[0] + i[2], r[0] - r[2], i[0] - i[2]
            fr, fi, hr, hi_ = r[1] + r[3], i[1] + i[3], r[1] - r[3], i[1] - i[3]
            zs = [(er + fr, ei + fi), (dr - hi_, di + hr), (er - fr, ei - fi), (dr + hi_, di - hr)]
            re, im = cmul_conj(
                cat([z[0] for z in zs], 1), cat([z[1] for z in zs], 1), c1, s1,
            )
            stacked.append(split(cat([re, im], 0)))
        inv = mat(6)
        yr = dot3((inv[0][:128], inv[1][:128]), stacked[0])
        yi = dot3((inv[0][128:], inv[1][128:]), stacked[1])
        put_words(inv_, [lane_tile(yr, j) for j in range(4)], [lane_tile(yi, j) for j in range(4)])
        exchange(step0 + 2, swords.at[inv_], rwords.at[inv_], 4, 4)

        @pl.when(first)
        def _():
            near_forward()

        arrived(step0 + 2, swords.at[inv_], rwords.at[inv_], 4)
        re, im = get_words(inv_)
        parts = [cat([re[j], im[j]], 1) for j in range(4)]
        prod = dot3(split(cat(parts, 0)), mat(2))
        outs = special_rows(parts, 4, [prod[128 * j:128 * j + 128] for j in range(4)])
        zs = [cmul_conj(o[:, :LANES], o[:, LANES:], c2, s2) for o in outs]
        y = cat(
            [
                cat([cat([zs[2 * tr][0], zs[2 * tr + 1][0]], 1), cat([zs[2 * tr][1], zs[2 * tr + 1][1]], 1)], 0)
                for tr in range(2)
            ],
            0,
        )
        back = dot3((wi[0], wi[1]), split(y))
        for h in range(2):
            xs[pl.ds(h, 256, stride=2), :] = lane_tile(back, h)
        sback[which] = xs[...].astype(BF16)
        exchange(step0 + 3, sback.at[which], rback.at[which], 4, 4)
        arrived(step0 + 3, sback.at[which], rback.at[which], 4)
        tiles = rback[which]
        far = interpolate(cat([dot(in_pick[h], tiles) for h in range(2)], 1).astype(BF16))

        @pl.when(first)
        def _():
            pot = far + near[...]
            val[...] = (pot - goal[...]).astype(BF16).astype(F32)
            fold(0, pot)

        @pl.when(last)
        def _():
            for copy in rim_copies:
                copy.wait_recv()
            before = jnp.where(me == 0, 0.0, rim[0])
            after = jnp.where(me == NDEV - 1, 0.0, rim[1])
            grad = far + ext[:BLOCKS, :]
            grad = cat(
                [grad[:REACH] + before, grad[REACH:BLOCKS - REACH], grad[BLOCKS - REACH:] + after], 0
            )
            fold(64, grad)

    loads["stencil"].wait()

    def both_passes(which, carry):
        evaluate(which)
        return carry

    lax.fori_loop(0, 2, both_passes, 0)
    for p in range(2):
        sent(4 * p, sbuf.at[p], rbuf.at[p], 5 - p)
        sent(4 * p + 1, swords.at[2 * p], rwords.at[2 * p], 4)
        sent(4 * p + 2, swords.at[2 * p + 1], rwords.at[2 * p + 1], 4)
        sent(4 * p + 3, sback.at[p], rback.at[p], 4)
    green_sent()
    for copy in halo_copies + rim_copies:
        copy.wait_send()


def local(table, charges, target, stencil, near_matrix, green, block_dest, block_tile, near_offset):
    out = pl.pallas_call(
        kernel,
        out_shape=jax.ShapeDtypeStruct((128, LANES), F32),
        in_specs=[pl.BlockSpec(memory_space=pl.ANY)] * 9,
        out_specs=pl.BlockSpec(memory_space=pltpu.VMEM),
        scratch_shapes=[
            pltpu.VMEM((64, LANES), BF16),
            pltpu.VMEM((64, LANES), F32),
            pltpu.VMEM((32, GRID), F32),
            pltpu.VMEM((1, LANES), jnp.int32),
            pltpu.VMEM((1, LANES), jnp.int32),
            pltpu.VMEM((4, LANES), jnp.int32),
            pltpu.VMEM((TABLE_ROWS, 256), F32),
            pltpu.VMEM((BLOCKS * PANEL, CELLS), BF16),
            pltpu.VMEM((4 * BLOCKS, PANEL * PANEL), BF16),
            pltpu.VMEM((2, ROWS, LANES), F32),
            pltpu.VMEM((2, ROWS, LANES), F32),
            pltpu.VMEM((2, 4 * NDEV, LANES), BF16),
            pltpu.VMEM((2, 4 * NDEV, LANES), BF16),
            pltpu.VMEM((4, 4 * NDEV, LANES), jnp.int32),
            pltpu.VMEM((4, 4 * NDEV, LANES), jnp.int32),
            pltpu.VMEM((1024, LANES), F32),
            pltpu.VMEM((1024, LANES), F32),
            pltpu.VMEM((128, 512), F32),
            pltpu.VMEM((128, 512), F32),
            pltpu.VMEM((128, 128), F32),
            pltpu.VMEM((128, 128), F32),
            pltpu.VMEM((128, 128), F32),
            pltpu.VMEM((128, 256), F32),
            pltpu.VMEM((4, 256, 256), BF16),
            pltpu.VMEM((2, 256, 512), BF16),
            pltpu.VMEM((18, 256, 256), BF16),
            pltpu.VMEM((512, LANES), F32),
            pltpu.VMEM((512, LANES), F32),
            pltpu.VMEM((128, LANES), F32),
            pltpu.VMEM((144, LANES), F32),
            pltpu.VMEM((2, REACH, LANES), F32),
            pltpu.VMEM((2, REACH, LANES), F32),
            pltpu.SemaphoreType.DMA((8,)),
            pltpu.SemaphoreType.DMA((8,)),
            pltpu.SemaphoreType.DMA((32,)),
            pltpu.SemaphoreType.DMA,
            pltpu.SemaphoreType.DMA((8,)),
            pltpu.SemaphoreType.DMA,
            pltpu.SemaphoreType.DMA((4,)),
            pltpu.SemaphoreType.DMA((4,)),
        ],
        compiler_params=pltpu.CompilerParams(collective_id=0, has_side_effects=True),
        name="panel_solver",
    )(
        charges.reshape(64, LANES), target.reshape(64, LANES),
        stencil.reshape(BLOCKS * PANEL, CELLS), near_matrix, green.T,
        block_dest.reshape(1, BLOCKS), block_tile.reshape(1, BLOCKS), near_offset.T, table,
    )
    return (out[:64].reshape(-1), out[64:].reshape(-1))


def solution(mesh):
    table = jnp.asarray(make_tables())
    return jax.shard_map(
        functools.partial(local, table),
        mesh=mesh,
        in_specs=(
            P(("panel", "slab")),
            P(("panel", "slab")),
            P(("panel", "slab"), None, None),
            P(("panel", "slab"), None, None),
            P(None, ("panel", "slab")),
            P(("panel", "slab"), None),
            P(("panel", "slab")),
            P(("panel", "slab"), None),
        ),
        out_specs=(P(("panel", "slab")), P(("panel", "slab"))),
        check_vma=False,
    )
```

```python
import functools
import math

import jax
import jax.numpy as jnp
import numpy as np
from jax import lax
from jax.experimental import pallas as pl
from jax.experimental.pallas import tpu as pltpu
from jax.sharding import PartitionSpec as P

GRID = 4096
TILE = 16
REACH = 8
NDEV = 128
SLABS = 4
BLOCKS = 128
PANEL = 64
CELLS = 256
LANES = 128
MSG = 8
GREEN_UNIT = 8191.0
ROWS = NDEV * MSG
MESH = pl.DeviceIdType.MESH
F32 = jnp.float32
BF16 = jnp.bfloat16
TABLES = (("w1", 256), ("m0", 256), ("m0i", 256), ("w2", 128), ("a1", 128), ("w3", 512), ("w5", 128), ("t2", 128),
          ("c0", 128), ("c1", 128), ("s0", 128), ("s1", 128))
START = {name: sum(n for _, n in TABLES[:i]) for i, (name, _) in enumerate(TABLES)}
TABLE_ROWS = sum(n for _, n in TABLES)


def make_tables():
    def angle(rows, cols, modulus):
        return 2.0 * math.pi / modulus * ((np.outer(rows, cols)) % modulus)

    out = {}
    th = angle(np.arange(128), np.arange(256), 256)
    w1 = np.concatenate([np.cos(th), -np.sin(th)], 0)
    w1[128] = (-1.0) ** np.arange(256)
    out["w1"] = w1
    th = angle(np.arange(16), np.arange(16), 16)
    c, s = np.kron(np.eye(8), np.cos(th)), np.kron(np.eye(8), np.sin(th))
    out["w2"] = np.concatenate([c, s], 1)
    m0 = np.zeros((2, 16, 2, 16))
    idx = np.arange(16)
    m0[0, :, 0, 0] = 1.0
    m0[0, :, 1, 0] = (-1.0) ** idx
    for k in range(1, 8):
        t = 2 * math.pi * ((idx * k) % 16) / 16
        m0[0, :, 0, k], m0[0, :, 1, k] = np.cos(t), -np.sin(t)
    for n in range(8):
        t = 2 * math.pi * ((idx * (1 + 2 * n)) % 32) / 32
        m0[1, :, 0, 8 + n], m0[1, :, 1, 8 + n] = np.cos(t), -np.sin(t)
    big = np.zeros((2, 8, 16, 2, 8, 16))
    for a in range(8):
        big[:, a, :, :, a, :] = m0
    out["m0"] = big.reshape(256, 256)
    inv = m0.copy()
    inv[:, :, :, 0] *= 0.5
    big = np.zeros((2, 8, 16, 2, 8, 16))
    for a in range(8):
        big[:, a, :, :, a, :] = inv
    out["m0i"] = big.reshape(256, 256).T
    th = angle(np.arange(128), np.arange(128), 128)
    out["a1"] = np.concatenate([np.cos(th), np.sin(th)], 1)
    parts = []
    for m in range(4):
        th = angle(np.arange(8), m + 4 * np.arange(8), 32)
        parts.append(
            np.concatenate([np.kron(np.cos(th), np.eye(16)), np.kron(np.sin(th), np.eye(16))], 1)
        )
    out["w3"] = np.concatenate(parts, 0)
    w5 = np.zeros((2, 8, 16, 8, 16))
    for m in range(4):
        for j in range(4):
            th = angle(m + 4 * np.arange(8), 8 * j + np.arange(8), 32)
            w5[0, :, m, :, j], w5[1, :, m, :, j] = np.cos(th), np.sin(th)
    out["w5"] = np.concatenate([w5[0].reshape(128, 128), w5[1].reshape(128, 128)], 1)
    th = np.tile(angle(np.arange(128), np.arange(16), GRID), (1, 8))
    th[0] = 0.0
    out["t2"] = np.concatenate([np.cos(th), np.sin(th)], 1)
    th = np.repeat(angle(np.arange(128), np.arange(32), GRID), 16, axis=1)
    out["c0"], out["c1"] = np.cos(th[:, :256]), np.cos(th[:, 256:])
    out["s0"], out["s1"] = np.sin(th[:, :256]), np.sin(th[:, 256:])
    return np.concatenate([out[name] for name, _ in TABLES], 0).astype(np.float32)


def dot(a, b):
    return lax.dot_general(a, b, (((1,), (0,)), ((), ())), preferred_element_type=F32)


def dot_nt(a, b):
    return lax.dot_general(a, b, (((1,), (1,)), ((), ())), preferred_element_type=F32)


def split(x):
    hi = x.astype(BF16)
    return hi, (x - hi.astype(F32)).astype(BF16)


def dot3(a, b):
    return dot(a[0], b[0]) + (dot(a[0], b[1]) + dot(a[1], b[0]))


def iota(shape, dim):
    return lax.broadcasted_iota(jnp.int32, shape, dim)


def cat(parts, axis):
    return jnp.concatenate(parts, axis=axis)


COMBOS = sorted(
    ((dz, dx) for dz in range(4) for dx in range(4)),
    key=lambda c: -(min(c[0], 4 - c[0]) + min(c[1], 4 - c[1])),
)
Z_DIGITS = sum(c[0] << (2 * i) for i, c in enumerate(COMBOS))
X_DIGITS = sum(c[1] << (2 * i) for i, c in enumerate(COMBOS))


def encode(re, im):
    top = jnp.abs(re[0])
    for x in list(re[1:]) + list(im):
        top = jnp.maximum(top, jnp.abs(x))
    top = jnp.maximum(top, 2.0 ** -100)
    power = jnp.floor(jnp.log2(top)) + 1.0
    scale = jnp.exp2(14.0 - power)
    code = power.astype(jnp.int32) + 128

    def mantissa(x):
        return jnp.minimum(x * scale + 16384.5, 32767.5).astype(jnp.int32)

    return [
        (((code >> (2 * j)) & 3) << 30) | (mantissa(re[j]) << 15) | mantissa(im[j])
        for j in range(4)
    ]


def decode(words):
    code = words[0] >> 30 & 3
    for j in range(1, 4):
        code = code | ((words[j] >> 30 & 3) << (2 * j))
    scale = jnp.exp2(code.astype(F32) - 142.0)
    re = [((w >> 15 & 32767).astype(F32) - 16384.0) * scale for w in words]
    im = [((w & 32767).astype(F32) - 16384.0) * scale for w in words]
    return re, im


def kernel(
    q_hbm, target_hbm, stencil_hbm, near_hbm, green_hbm, dest_hbm, tile_hbm, offset_hbm, table_hbm,
    out_ref,
    q_ref, target_ref, green_ref, dest_ref, tile_ref, offset_ref, table,
    stencil, near_mat, sbuf, rbuf, sback, rback, swords, rwords, gsend, grecv, ga, gb5, t5, val, charge, goal, tv,
    wf, wi, mats, xs, acc, near, ext, halo, rim,
    send_sem, recv_sem, gsend_sem, grecv_sem, load_sem, near_sem, halo_sem, rim_sem,
):
    panel = lax.axis_index("panel")
    slab = lax.axis_index("slab")
    me = panel * SLABS + slab
    pz, px, pc = panel // 8, (panel // 2) % 4, panel % 2

    loads = {}
    for i, (name, src, dst) in enumerate((
        ("q", q_hbm, q_ref), ("dest", dest_hbm, dest_ref), ("tile", tile_hbm, tile_ref),
        ("stencil", stencil_hbm, stencil), ("table", table_hbm, table),
        ("green", green_hbm, green_ref), ("offset", offset_hbm, offset_ref),
        ("target", target_hbm, target_ref),
    )):
        loads[name] = pltpu.make_async_copy(src, dst, load_sem.at[i])
        loads[name].start()

    def rows_at(name):
        n = dict(TABLES)[name]
        return table[START[name]:START[name] + n, :]

    def half_at(name, half):
        n = dict(TABLES)[name]
        return table[START[name]:START[name] + n, half * LANES:(half + 1) * LANES]

    def others(visit):
        def body(g, carry):
            z = (pz + ((Z_DIGITS >> (2 * g)) & 3)) % 4
            x = (px + ((X_DIGITS >> (2 * g)) & 3)) % 4
            for dy in (2, 1, 3, 0):
                for dc in (1, 0):
                    def go(z=z, x=x, dy=dy, dc=dc):
                        visit(z * 8 + x * 2 + (pc + dc) % 2, (slab + dy) % 4)

                    if dy == 0 and dc == 0:
                        pl.when(g != 15)(go)
                    else:
                        go()
            return carry

        lax.fori_loop(0, 16, body, 0)

    barrier = pltpu.get_barrier_semaphore()
    others(
        lambda p, y: pl.semaphore_signal(barrier, inc=1, device_id=(p, y), device_id_type=MESH)
    )

    def near_load(b, carry):
        pltpu.make_async_copy(
            near_hbm.at[b], near_mat.at[pl.ds(pl.multiple_of(b * 4, 4), 4)], near_sem
        ).start()
        return carry

    rows128, lanes128 = iota((128, 128), 0), iota((128, 128), 1)

    def unfold(ref, out):
        x = ref[...].astype(F32)
        y = pltpu.roll(x, 64, 1)
        low = iota((64, 128), 1) < 64
        out[pl.ds(0, 64, stride=2), :] = jnp.where(low, x, y)
        out[pl.ds(1, 64, stride=2), :] = jnp.where(low, y, x)

    def fold(row, value):
        goal[...] = value
        low = iota((64, 128), 1) < 64
        out_ref[row:row + 64, :] = jnp.where(
            low, goal[pl.ds(0, 64, stride=2), :], goal[pl.ds(1, 64, stride=2), :]
        )

    loads["q"].wait()
    unfold(q_ref, charge)
    val[...] = charge[...]

    def pair(slot, value):
        hi, lo = split(value)
        mats[2 * slot] = hi
        mats[2 * slot + 1] = lo

    def mat(slot):
        return mats[2 * slot], mats[2 * slot + 1]

    every16 = lanes128 % 16 == 0

    def squeeze(tiles):
        total = jnp.where(every16, tiles[0], 0.0)
        for j in range(1, 4):
            total = total + pltpu.roll(jnp.where(every16, tiles[j], 0.0), j, 1)
        return total

    def split_tables():
        def circle(name):
            return half_at(name, 0), half_at(name, 1)

        pair(0, rows_at("w1"))
        c, s = circle("w2")
        pair(1, cat([cat([c, -s], 1), cat([s, c], 1)], 0))
        pair(2, cat([cat([c, s], 1), cat([-s, c], 1)], 0))
        pair(3, rows_at("m0"))
        pair(4, rows_at("m0i"))
        c, s = circle("a1")
        pair(5, cat([cat([c, s], 1), cat([-s, c], 1)], 0))
        pair(6, cat([cat([c, -s], 1), cat([s, c], 1)], 0))
        for m in range(4):
            base = START["w3"] + 128 * m
            c, s = table[base:base + 128, :LANES], table[base:base + 128, LANES:]
            pair(7 + m, cat([cat([c, -s], 1), cat([s, c], 1)], 0))
            c, s = c.T, s.T
            pair(11 + m, cat([cat([c, s], 1), cat([-s, c], 1)], 0))
        c, s = circle("w5")
        pair(15, cat([cat([c, s], 1), cat([-s, c], 1)], 0))
        t5[:, :LANES] = squeeze([half_at("c%d" % (j // 2), j % 2) for j in range(4)])
        t5[:, LANES:] = squeeze([half_at("s%d" % (j // 2), j % 2) for j in range(4)])

    loads["dest"].wait()
    loads["tile"].wait()
    dest_row = dest_ref[...]
    tile_row = tile_ref[...]

    def column(row):
        return jnp.sum(jnp.where(rows128 == lanes128, row, 0), axis=1, keepdims=True)

    dest_col = column(dest_row)
    same = dest_col == dest_row
    rank_row = jnp.sum(jnp.where(same & (rows128 < lanes128), 1, 0), axis=0, keepdims=True)
    rank_col = jnp.sum(jnp.where(same & (lanes128 < rows128), 1, 0), axis=1, keepdims=True)
    one, zero = F32(1.0), F32(0.0)
    out_pick = cat(
        [jnp.where((dest_row == rows128) & (rank_row == k), one, zero) for k in range(2)], 0
    )
    wanted = iota((128, 512), 1) - 4 * dest_col - 2 * rank_col
    in_pick = [jnp.where(wanted == h, one, zero).astype(BF16) for h in range(2)]
    ids = jnp.sum(out_pick * (tile_row + 1).astype(F32), axis=1, keepdims=True)
    id_rows = jnp.where(lanes128 == 0, ids[:128], jnp.where(lanes128 == 1, ids[128:], 0.0))
    out_pick = out_pick.astype(BF16)

    def exchange(step, src, dst, stride, count):
        mine = pl.ds(pl.multiple_of(me * stride, stride), count)

        def send(p, y):
            theirs = pl.ds(pl.multiple_of((p * SLABS + y) * stride, stride), count)
            pltpu.make_async_remote_copy(
                src_ref=src.at[theirs],
                dst_ref=dst.at[mine],
                send_sem=send_sem.at[step],
                recv_sem=recv_sem.at[step],
                device_id=(p, y),
                device_id_type=MESH,
            ).start()

        others(send)
        pltpu.make_async_copy(src.at[mine], dst.at[mine], recv_sem.at[step]).start()

    def arrived(step, src, dst, count):
        part = pl.ds(0, NDEV * count)
        pltpu.make_async_copy(src.at[part], dst.at[part], recv_sem.at[step]).wait()

    def sent(step, src, dst, count):
        part = pl.ds(0, (NDEV - 1) * count)
        pltpu.make_async_copy(src.at[part], dst.at[part], send_sem.at[step]).wait()

    def put(slot, row, value):
        sbuf[slot, pl.ds(row, NDEV, stride=MSG), :] = value

    def get(slot, row):
        return rbuf[slot, pl.ds(row, NDEV, stride=MSG), :]

    def put_words(slot, re, im):
        for j, w in enumerate(encode(re, im)):
            swords[slot, pl.ds(j, NDEV, stride=4), :] = w

    def get_words(slot):
        return decode([rwords[slot, pl.ds(j, NDEV, stride=4), :] for j in range(4)])

    def next_to(shift):
        other = (me + shift + NDEV) % NDEV
        return (other // SLABS, other % SLABS)

    def edge_copies(src, rows_prev, rows_next, dst, sem):
        for way, (shift, rows) in enumerate(((-1, rows_prev), (1, rows_next))):
            yield pltpu.make_async_remote_copy(
                src_ref=src.at[pl.ds(rows, REACH)],
                dst_ref=dst.at[1 - way],
                send_sem=sem.at[way],
                recv_sem=sem.at[3 - way],
                device_id=next_to(shift),
                device_id_type=MESH,
            )

    halo_copies = list(edge_copies(charge, 0, BLOCKS - REACH, halo, halo_sem))
    rim_copies = list(edge_copies(ext, BLOCKS, BLOCKS + REACH, rim, rim_sem))

    def place(index):
        return jnp.where(index < 128, index, jnp.where(index < 136, index - 136, index - 8))

    def near_forward():
        loads["offset"].wait()
        for copy in halo_copies:
            copy.wait_recv()
        before = jnp.where(me == 0, 0.0, halo[0])
        after = jnp.where(me == NDEV - 1, 0.0, halo[1])
        source = cat([charge[...], before, after], 0).astype(BF16)
        spot = place(iota((128, 144), 1)) - iota((128, 144), 0)
        for k in range(4):
            pick = jnp.where(spot == column(offset_ref[k:k + 1, :]), one, zero).astype(BF16)
            xs[pl.ds(k, 128, stride=4), :] = dot(pick, source)
        pltpu.make_async_copy(near_mat, near_mat, near_sem).wait()
        acc[...] = jnp.zeros((512, 128), F32)

        def body(c, carry):
            col = pl.ds(pl.multiple_of(c * 256, 256), 256)
            gather = jnp.where(
                iota((256, 128), 1) % 64 == c * 4 + iota((256, 128), 0) // 64, one, zero
            ).astype(BF16)
            for r in range(4):
                row = pl.ds(128 * r, 128)
                x = xs[row, :]
                hi, lo = split(near_mat[row, col].astype(F32) * cat([x, x], 1))
                acc[row, :] = acc[row, :] + (dot(hi, gather) + dot(lo, gather))
            return carry

        lax.fori_loop(0, 16, body, 0)
        near[...] = sum(acc[pl.ds(k, 128, stride=4), :] for k in range(4))

    def near_adjoint():
        for k in range(4):
            xs[pl.ds(k, 128, stride=4), :] = val[...]
        acc[...] = jnp.zeros((512, 128), F32)

        def body(c, carry):
            col = pl.ds(pl.multiple_of(c * 256, 256), 256)
            spread = jnp.where(
                iota((128, 256), 0) == c * 4 + iota((128, 256), 1) // 64, one, zero
            ).astype(BF16)
            for r in range(4):
                row = pl.ds(128 * r, 128)
                p = near_mat[row, col].astype(F32) * dot(xs[row, :].astype(BF16), spread)
                acc[row, :] = acc[row, :] + (p[:, :128] + p[:, 128:])
            return carry

        lax.fori_loop(0, 16, body, 0)

    def near_scatter():
        acc[...] = acc[...] + pltpu.roll(acc[...], 64, 1)
        total = jnp.zeros((144, 128), F32)
        spot = place(iota((144, 128), 0)) - iota((144, 128), 1)
        for k in range(4):
            pick = jnp.where(spot == offset_ref[k:k + 1, :], one, zero).astype(BF16)
            hi, lo = split(acc[pl.ds(k, 128, stride=4), :])
            total = total + (dot(pick, hi) + dot(pick, lo))
        ext[...] = total
        for copy in rim_copies:
            copy.start()

    def pack(kk, carry):
        def code(at):
            x = green_ref[:, pl.ds(pl.multiple_of(at * LANES, LANES), LANES)]
            return (x * GREEN_UNIT + 0.5).astype(jnp.int32)

        gsend[pl.ds(kk, 32, stride=16), :] = (code(kk + 16) << 16) | code(kk)
        return carry

    def green_copies():
        k2 = me // 8

        def body(j, carry):
            k1 = (me % 8) * 32 + j
            low = jnp.where(k1 < 128, 1, 0)
            is_mid = jnp.where(k1 == 128, 1, 0)
            is_zero = jnp.where(k1 == 0, 1, 0)
            high = 1 - low - is_mid
            target_dev = low * k1 + high * (256 - k1)
            upper = k2 // 8
            beyond = jnp.where(k2 > 8, 1, 0)
            slot_zero = (1 - upper) * k2 + upper * (1 - beyond) * 16 + beyond * (32 - k2)
            slot_mid = (1 - upper) * (8 + k2) + upper * (39 - k2)
            slot = (low - is_zero) * k2 + is_zero * slot_zero + is_mid * slot_mid + high * (31 - k2)
            src = gsend.at[pl.ds(pl.multiple_of(j * 16, 16), 16)]
            dst = grecv.at[pl.ds(pl.multiple_of(slot * 16, 16), 16)]

            @pl.when(target_dev != me)
            def _():
                pltpu.make_async_remote_copy(
                    src_ref=src, dst_ref=dst, send_sem=gsend_sem.at[j], recv_sem=grecv_sem,
                    device_id=(target_dev // SLABS, target_dev % SLABS), device_id_type=MESH,
                ).start()

            @pl.when(target_dev == me)
            def _():
                pltpu.make_async_copy(src, dst, grecv_sem).start()

            return carry

        lax.fori_loop(0, 32, body, 0)

    def green_sent():
        def body(j, carry):
            k1 = (me % 8) * 32 + j
            low = jnp.where(k1 < 128, 1, 0)
            high = jnp.where(k1 > 128, 1, 0)
            target_dev = low * k1 + high * (256 - k1)

            @pl.when(target_dev != me)
            def _():
                part = pl.ds(pl.multiple_of(j * 16, 16), 16)
                pltpu.make_async_copy(gsend.at[part], grecv.at[part], gsend_sem.at[j]).wait()

            return carry

        lax.fori_loop(0, 32, body, 0)

    def green_ready():
        pltpu.make_async_copy(gsend, grecv, grecv_sem).wait()
        scale = 2.0 ** -24 / GREEN_UNIT
        flip = jnp.where((rows128 + lanes128 == 128) & (rows128 > 0), one, zero).astype(BF16)
        first = jnp.where((rows128 == 0) & (lanes128 == 0), one, zero).astype(BF16)
        eye = jnp.where(rows128 == lanes128, one, zero).astype(BF16)
        turn = cat([flip, first], 1)
        special = every16 & (me == 0)

        def rows_of(base, kappa):
            rows = []
            for n in range(8):
                k = kappa(n)
                words = grecv[pl.ds(base * 16 + k % 16, 16, stride=16), :]
                rows.append(((words >> 16 if k >= 16 else words) & 65535).astype(F32))
            return cat(rows, 0)

        nyquist = []

        for m in range(4):
            def plain(base):
                hi, lo = split(rows_of(base, lambda n: m + 4 * n))
                return dot_nt(eye, hi) + dot_nt(eye, lo)

            def turned(base):
                one_ = rows_of(base, lambda n: 31 - m - 4 * n)
                two_ = rows_of(base, lambda n: (32 - m - 4 * n) % 32)
                hi, lo = split(cat([one_, two_], 1))
                return dot_nt(turn, hi) + dot_nt(turn, lo)

            d, dr, o, orr = plain(0), turned(0), plain(16), turned(16)
            ga[:, m * LANES:(m + 1) * LANES] = (d + jnp.where(special, dr, orr)) * scale
            nyquist.append((o + orr) * scale)
        gb5[...] = squeeze(nyquist)

    lane64 = iota((128, 128), 1) // 64
    row16 = iota((128, 128), 0) % 16

    def project():
        v = val[...]
        spread = cat(
            [jnp.where(lane64 + 2 * i == row16, v, 0.0).astype(BF16) for i in range(8)], 1
        )
        for g in range(8):
            part = stencil[g * 1024:(g + 1) * 1024, :]
            tv[g * 16:(g + 1) * 16, :] = dot(spread[g * 16:(g + 1) * 16, :], part)
        hi, lo = split(tv[...])
        return dot(out_pick, hi) + dot(out_pick, lo)

    def interpolate(own_tiles):
        rows = []
        l64, r16 = iota((16, 128), 1) // 64, iota((16, 128), 0)
        for g in range(8):
            part = stencil[g * 1024:(g + 1) * 1024, :]
            r = dot_nt(own_tiles[g * 16:(g + 1) * 16, :], part)
            acc = jnp.zeros((16, 128), F32)
            for i in range(8):
                acc = acc + jnp.where(l64 + 2 * i == r16, r[:, i * LANES:(i + 1) * LANES], 0.0)
            rows.append(acc)
        far = cat(rows, 0)
        return far + pltpu.roll(far, 64, 1)

    def cmul(re, im, c, s):
        return re * c + im * s, im * c - re * s

    def cmul_conj(re, im, c, s):
        return re * c - im * s, im * c + re * s

    def lane_tile(x, j):
        return x[:, j * LANES:(j + 1) * LANES]

    head = iota((8, 128), 0) == 0

    def special_rows(parts, slot, outs):
        small = dot3(split(cat([p[:8] for p in parts], 0)), mat(slot))
        fixed = []
        for j in range(4):
            out = outs[j]
            h2 = iota((8, 256), 0) == 0
            fixed.append(cat([jnp.where(h2, small[8 * j:8 * j + 8], out[:8]), out[8:]], 0))
        return fixed

    def evaluate(which):
        step0 = which * 4
        first, last = which == 0, which == 1
        fwd, inv_ = which * 2, which * 2 + 1
        out = project()
        for k in range(2):
            for h in range(2):
                put(which, 2 * k + h, lane_tile(out[128 * k:128 * k + 128], h))

        @pl.when(first)
        def _():
            put(0, 4, id_rows)
            pl.semaphore_wait(barrier, NDEV - 1)
            exchange(0, sbuf.at[0], rbuf.at[0], MSG, 5)
            for copy in halo_copies:
                copy.start()
            loads["green"].wait()
            lax.fori_loop(0, 16, pack, 0)
            green_copies()
            lax.fori_loop(0, BLOCKS, near_load, 0)
            loads["table"].wait()
            split_tables()
            loads["target"].wait()
            unfold(target_ref, goal)
            arrived(0, sbuf.at[0], rbuf.at[0], 5)
            idm = get(0, 4)
            tc = iota((128, 256), 1)
            for k in range(2):
                xs[pl.ds(k, 128, stride=2), :] = jnp.broadcast_to(idm[:, k:k + 1], (128, 128))
            ordered = xs[:256, :1].astype(jnp.int32)
            for tr in range(2):
                pick = cat(
                    [
                        jnp.where(idm[:, k:k + 1].astype(jnp.int32) == tc + (tr * 256 + 1), one, zero)
                        for k in range(2)
                    ],
                    0,
                ).astype(BF16)
                back_pick = jnp.where(
                    ordered == iota((256, 256), 1) + (tr * 256 + 1), one, zero
                ).astype(BF16)
                for t in range(2):
                    wf[2 * tr + t] = dot_nt(mats[t], pick).astype(BF16)
                    wi[t, :, tr * 256:(tr + 1) * 256] = dot_nt(back_pick, mats[t]).astype(BF16)

        @pl.when(last)
        def _():
            exchange(4, sbuf.at[1], rbuf.at[1], MSG, 4)
            near_adjoint()
            arrived(4, sbuf.at[1], rbuf.at[1], 4)

        tiles = split(
            cat([cat([get(which, 2 * k + h) for h in range(2)], 1) for k in range(2)], 0)
        )
        c2, s2 = half_at("t2", 0), half_at("t2", 1)
        c1 = cat([rows_at("c0"), rows_at("c1")], 1)
        s1 = cat([rows_at("s0"), rows_at("s1")], 1)
        parts = []
        for tr in range(2):
            y = dot3((wf[2 * tr], wf[2 * tr + 1]), tiles)
            for h in range(2):
                re, im = cmul(lane_tile(y[:128], h), lane_tile(y[128:], h), c2, s2)
                parts.append(cat([re, im], 1))
        prod = dot3(split(cat(parts, 0)), mat(1))
        outs = special_rows(parts, 3, [prod[128 * j:128 * j + 128] for j in range(4)])
        put_words(fwd, [o[:, :LANES] for o in outs], [o[:, LANES:] for o in outs])
        exchange(step0 + 1, swords.at[fwd], rwords.at[fwd], 4, 4)

        @pl.when(first)
        def _():
            green_ready()

        @pl.when(last)
        def _():
            near_scatter()

        arrived(step0 + 1, swords.at[fwd], rwords.at[fwd], 4)
        re, im = get_words(fwd)
        y = dot3(mat(5), split(cat([cat(re, 1), cat(im, 1)], 0)))
        re, im = cmul(y[:128], y[128:], c1, s1)
        r = [lane_tile(re, j) for j in range(4)]
        i = [lane_tile(im, j) for j in range(4)]
        er, ei, dr, di = r[0] + r[2], i[0] + i[2], r[0] - r[2], i[0] - i[2]
        fr, fi, hr, hi_ = r[1] + r[3], i[1] + i[3], r[1] - r[3], i[1] - i[3]
        vs = [(er + fr, ei + fi), (dr + hi_, di - hr), (er - fr, ei - fi), (dr - hi_, di + hr)]
        spectrum = [dot3(split(cat(list(vs[m]), 1)), mat(7 + m)) for m in range(4)]
        vs = []
        for m in range(4):
            gm = ga[:, m * LANES:(m + 1) * LANES]
            p = dot3(split(spectrum[m] * cat([gm, gm], 1)), mat(11 + m))
            vs.append((p[:, :LANES], p[:, LANES:]))
        r = [v[0] for v in vs]
        i = [v[1] for v in vs]
        er, ei, dr, di = r[0] + r[2], i[0] + i[2], r[0] - r[2], i[0] - i[2]
        fr, fi, hr, hi_ = r[1] + r[3], i[1] + i[3], r[1] - r[3], i[1] - i[3]
        zs = [(er + fr, ei + fi), (dr - hi_, di + hr), (er - fr, ei - fi), (dr + hi_, di - hr)]
        re, im = cmul_conj(cat([z[0] for z in zs], 1), cat([z[1] for z in zs], 1), c1, s1)
        y = dot3(mat(6), split(cat([re, im], 0)))
        g5 = gb5[...]
        p = dot3(
            split(cat([squeeze([f[:, :LANES] for f in spectrum]) * g5,
                       squeeze([f[:, LANES:] for f in spectrum]) * g5], 1)),
            mat(15),
        )
        re, im = cmul_conj(p[:, :LANES], p[:, LANES:], t5[:, :LANES], t5[:, LANES:])
        y5 = dot3((mats[12, 128:, :], mats[13, 128:, :]), split(cat([re, im], 0)))
        here = every16 & (me == 0)
        yr = [lane_tile(y[:128], j) for j in range(4)]
        yi = [
            jnp.where(here, pltpu.roll(y5, LANES - j, 1) if j else y5, lane_tile(y[128:], j))
            for j in range(4)
        ]
        put_words(inv_, yr, yi)
        exchange(step0 + 2, swords.at[inv_], rwords.at[inv_], 4, 4)

        @pl.when(first)
        def _():
            near_forward()

        arrived(step0 + 2, swords.at[inv_], rwords.at[inv_], 4)
        re, im = get_words(inv_)
        parts = [cat([re[j], im[j]], 1) for j in range(4)]
        prod = dot3(split(cat(parts, 0)), mat(2))
        outs = special_rows(parts, 4, [prod[128 * j:128 * j + 128] for j in range(4)])
        zs = [cmul_conj(o[:, :LANES], o[:, LANES:], c2, s2) for o in outs]
        y = cat(
            [
                cat([cat([zs[2 * tr][0], zs[2 * tr + 1][0]], 1), cat([zs[2 * tr][1], zs[2 * tr + 1][1]], 1)], 0)
                for tr in range(2)
            ],
            0,
        )
        back = dot3((wi[0], wi[1]), split(y))
        for h in range(2):
            xs[pl.ds(h, 256, stride=2), :] = lane_tile(back, h)
        sback[which] = xs[...].astype(BF16)
        exchange(step0 + 3, sback.at[which], rback.at[which], 4, 4)
        arrived(step0 + 3, sback.at[which], rback.at[which], 4)
        tiles = rback[which]
        far = interpolate(cat([dot(in_pick[h], tiles) for h in range(2)], 1).astype(BF16))

        @pl.when(first)
        def _():
            pot = far + near[...]
            val[...] = (pot - goal[...]).astype(BF16).astype(F32)
            fold(0, pot)

        @pl.when(last)
        def _():
            for copy in rim_copies:
                copy.wait_recv()
            before = jnp.where(me == 0, 0.0, rim[0])
            after = jnp.where(me == NDEV - 1, 0.0, rim[1])
            grad = far + ext[:BLOCKS, :]
            grad = cat(
                [grad[:REACH] + before, grad[REACH:BLOCKS - REACH], grad[BLOCKS - REACH:] + after], 0
            )
            fold(64, grad)

    loads["stencil"].wait()

    def both_passes(which, carry):
        evaluate(which)
        return carry

    lax.fori_loop(0, 2, both_passes, 0)
    for p in range(2):
        sent(4 * p, sbuf.at[p], rbuf.at[p], 5 - p)
        sent(4 * p + 1, swords.at[2 * p], rwords.at[2 * p], 4)
        sent(4 * p + 2, swords.at[2 * p + 1], rwords.at[2 * p + 1], 4)
        sent(4 * p + 3, sback.at[p], rback.at[p], 4)
    green_sent()
    for copy in halo_copies + rim_copies:
        copy.wait_send()


def local(table, charges, target, stencil, near_matrix, green, block_dest, block_tile, near_offset):
    out = pl.pallas_call(
        kernel,
        out_shape=jax.ShapeDtypeStruct((128, LANES), F32),
        in_specs=[pl.BlockSpec(memory_space=pltpu.HBM)] * 9,
        out_specs=pl.BlockSpec(memory_space=pltpu.VMEM),
        scratch_shapes=[
            pltpu.VMEM((64, LANES), BF16),
            pltpu.VMEM((64, LANES), F32),
            pltpu.VMEM((32, GRID), F32),
            pltpu.VMEM((1, LANES), jnp.int32),
            pltpu.VMEM((1, LANES), jnp.int32),
            pltpu.VMEM((4, LANES), jnp.int32),
            pltpu.VMEM((TABLE_ROWS, 256), F32),
            pltpu.VMEM((BLOCKS * PANEL, CELLS), BF16),
            pltpu.VMEM((4 * BLOCKS, PANEL * PANEL), BF16),
            pltpu.VMEM((2, ROWS, LANES), F32),
            pltpu.VMEM((2, ROWS, LANES), F32),
            pltpu.VMEM((2, 4 * NDEV, LANES), BF16),
            pltpu.VMEM((2, 4 * NDEV, LANES), BF16),
            pltpu.VMEM((4, 4 * NDEV, LANES), jnp.int32),
            pltpu.VMEM((4, 4 * NDEV, LANES), jnp.int32),
            pltpu.VMEM((512, LANES), jnp.int32),
            pltpu.VMEM((512, LANES), jnp.int32),
            pltpu.VMEM((128, 512), F32),
            pltpu.VMEM((128, LANES), F32),
            pltpu.VMEM((128, 256), F32),
            pltpu.VMEM((128, 128), F32),
            pltpu.VMEM((128, 128), F32),
            pltpu.VMEM((128, 128), F32),
            pltpu.VMEM((128, 256), F32),
            pltpu.VMEM((4, 256, 256), BF16),
            pltpu.VMEM((2, 256, 512), BF16),
            pltpu.VMEM((32, 256, 256), BF16),
            pltpu.VMEM((512, LANES), F32),
            pltpu.VMEM((512, LANES), F32),
            pltpu.VMEM((128, LANES), F32),
            pltpu.VMEM((144, LANES), F32),
            pltpu.VMEM((2, REACH, LANES), F32),
            pltpu.VMEM((2, REACH, LANES), F32),
            pltpu.SemaphoreType.DMA((8,)),
            pltpu.SemaphoreType.DMA((8,)),
            pltpu.SemaphoreType.DMA((32,)),
            pltpu.SemaphoreType.DMA,
            pltpu.SemaphoreType.DMA((8,)),
            pltpu.SemaphoreType.DMA,
            pltpu.SemaphoreType.DMA((4,)),
            pltpu.SemaphoreType.DMA((4,)),
        ],
        compiler_params=pltpu.CompilerParams(
            collective_id=0, has_side_effects=True, vmem_limit_bytes=44 << 20
        ),
        name="panel_solver",
    )(
        charges.reshape(64, LANES), target.reshape(64, LANES),
        stencil.reshape(BLOCKS * PANEL, CELLS), near_matrix, green.T,
        block_dest.reshape(1, BLOCKS), block_tile.reshape(1, BLOCKS), near_offset.T, table,
    )
    return (out[:64].reshape(-1), out[64:].reshape(-1))


def solution(mesh):
    table = jnp.asarray(make_tables())
    return jax.shard_map(
        functools.partial(local, table),
        mesh=mesh,
        in_specs=(
            P(("panel", "slab")),
            P(("panel", "slab")),
            P(("panel", "slab"), None, None),
            P(("panel", "slab"), None, None),
            P(None, ("panel", "slab")),
            P(("panel", "slab"), None),
            P(("panel", "slab")),
            P(("panel", "slab"), None),
        ),
        out_specs=(P(("panel", "slab")), P(("panel", "slab"))),
        check_vma=False,
    )
```

```python
import functools
import math

import jax
import jax.numpy as jnp
import numpy as np
from jax import lax
from jax.experimental import pallas as pl
from jax.experimental.pallas import tpu as pltpu
from jax.sharding import PartitionSpec as P

GRID = 4096
TILE = 16
REACH = 8
NDEV = 128
SLABS = 4
BLOCKS = 128
PANEL = 64
CELLS = 256
LANES = 128
MSG = 8
GREEN_UNIT = 8191.0
ROWS = NDEV * MSG
MESH = pl.DeviceIdType.MESH
F32 = jnp.float32
BF16 = jnp.bfloat16
TABLES = (("w1", 256), ("m0", 256), ("m0i", 256), ("w2", 128), ("a1", 128), ("w3", 512), ("w5", 128), ("t2", 128),
          ("c0", 128), ("c1", 128), ("s0", 128), ("s1", 128))
START = {name: sum(n for _, n in TABLES[:i]) for i, (name, _) in enumerate(TABLES)}
TABLE_ROWS = sum(n for _, n in TABLES)


def make_tables():
    def angle(rows, cols, modulus):
        return 2.0 * math.pi / modulus * ((np.outer(rows, cols)) % modulus)

    out = {}
    th = angle(np.arange(128), np.arange(256), 256)
    w1 = np.concatenate([np.cos(th), -np.sin(th)], 0)
    w1[128] = (-1.0) ** np.arange(256)
    out["w1"] = w1
    th = angle(np.arange(16), np.arange(16), 16)
    c, s = np.kron(np.eye(8), np.cos(th)), np.kron(np.eye(8), np.sin(th))
    out["w2"] = np.concatenate([c, s], 1)
    m0 = np.zeros((2, 16, 2, 16))
    idx = np.arange(16)
    m0[0, :, 0, 0] = 1.0
    m0[0, :, 1, 0] = (-1.0) ** idx
    for k in range(1, 8):
        t = 2 * math.pi * ((idx * k) % 16) / 16
        m0[0, :, 0, k], m0[0, :, 1, k] = np.cos(t), -np.sin(t)
    for n in range(8):
        t = 2 * math.pi * ((idx * (1 + 2 * n)) % 32) / 32
        m0[1, :, 0, 8 + n], m0[1, :, 1, 8 + n] = np.cos(t), -np.sin(t)
    big = np.zeros((2, 8, 16, 2, 8, 16))
    for a in range(8):
        big[:, a, :, :, a, :] = m0
    out["m0"] = big.reshape(256, 256)
    inv = m0.copy()
    inv[:, :, :, 0] *= 0.5
    big = np.zeros((2, 8, 16, 2, 8, 16))
    for a in range(8):
        big[:, a, :, :, a, :] = inv
    out["m0i"] = big.reshape(256, 256).T
    th = angle(np.arange(128), np.arange(128), 128)
    out["a1"] = np.concatenate([np.cos(th), np.sin(th)], 1)
    parts = []
    for m in range(4):
        th = angle(np.arange(8), m + 4 * np.arange(8), 32)
        parts.append(
            np.concatenate([np.kron(np.cos(th), np.eye(16)), np.kron(np.sin(th), np.eye(16))], 1)
        )
    out["w3"] = np.concatenate(parts, 0)
    w5 = np.zeros((2, 8, 16, 8, 16))
    for m in range(4):
        for j in range(4):
            th = angle(m + 4 * np.arange(8), 8 * j + np.arange(8), 32)
            w5[0, :, m, :, j], w5[1, :, m, :, j] = np.cos(th), np.sin(th)
    out["w5"] = np.concatenate([w5[0].reshape(128, 128), w5[1].reshape(128, 128)], 1)
    th = np.tile(angle(np.arange(128), np.arange(16), GRID), (1, 8))
    th[0] = 0.0
    out["t2"] = np.concatenate([np.cos(th), np.sin(th)], 1)
    th = np.repeat(angle(np.arange(128), np.arange(32), GRID), 16, axis=1)
    out["c0"], out["c1"] = np.cos(th[:, :256]), np.cos(th[:, 256:])
    out["s0"], out["s1"] = np.sin(th[:, :256]), np.sin(th[:, 256:])
    return np.concatenate([out[name] for name, _ in TABLES], 0).astype(np.float32)


def dot(a, b):
    return lax.dot_general(a, b, (((1,), (0,)), ((), ())), preferred_element_type=F32)


def dot_nt(a, b):
    return lax.dot_general(a, b, (((1,), (1,)), ((), ())), preferred_element_type=F32)


def split(x):
    hi = x.astype(BF16)
    return hi, (x - hi.astype(F32)).astype(BF16)


def dot3(a, b):
    return dot(a[0], b[0]) + (dot(a[0], b[1]) + dot(a[1], b[0]))


def iota(shape, dim):
    return lax.broadcasted_iota(jnp.int32, shape, dim)


def cat(parts, axis):
    return jnp.concatenate(parts, axis=axis)


COMBOS = sorted(
    ((dz, dx) for dz in range(4) for dx in range(4)),
    key=lambda c: -(min(c[0], 4 - c[0]) + min(c[1], 4 - c[1])),
)
Z_DIGITS = sum(c[0] << (2 * i) for i, c in enumerate(COMBOS))
X_DIGITS = sum(c[1] << (2 * i) for i, c in enumerate(COMBOS))


def encode(re, im):
    top = jnp.abs(re[0])
    for x in list(re[1:]) + list(im):
        top = jnp.maximum(top, jnp.abs(x))
    top = jnp.maximum(top, 2.0 ** -100)
    power = jnp.floor(jnp.log2(top)) + 1.0
    scale = jnp.exp2(14.0 - power)
    code = power.astype(jnp.int32) + 128

    def mantissa(x):
        return jnp.minimum(x * scale + 16384.5, 32767.5).astype(jnp.int32)

    return [
        (((code >> (2 * j)) & 3) << 30) | (mantissa(re[j]) << 15) | mantissa(im[j])
        for j in range(4)
    ]


def decode(words):
    code = words[0] >> 30 & 3
    for j in range(1, 4):
        code = code | ((words[j] >> 30 & 3) << (2 * j))
    scale = jnp.exp2(code.astype(F32) - 142.0)
    re = [((w >> 15 & 32767).astype(F32) - 16384.0) * scale for w in words]
    im = [((w & 32767).astype(F32) - 16384.0) * scale for w in words]
    return re, im


def kernel(
    q_hbm, target_hbm, stencil_hbm, near_hbm, green_hbm, dest_hbm, tile_hbm, offset_hbm, table_hbm,
    out_ref,
    q_ref, target_ref, green_ref, dest_ref, tile_ref, offset_ref, table,
    stencil, near_mat, sbuf, rbuf, sback, rback, swords, rwords, gsend, grecv, ga, gb5, t5, val, charge, goal, tv,
    wf, wi, mats, xs, acc, near, ext, halo, rim,
    send_sem, recv_sem, gsend_sem, grecv_sem, load_sem, near_sem, halo_sem, rim_sem,
):
    panel = lax.axis_index("panel")
    slab = lax.axis_index("slab")
    me = panel * SLABS + slab
    pz, px, pc = panel // 8, (panel // 2) % 4, panel % 2

    loads = {}
    for i, (name, src, dst) in enumerate((
        ("q", q_hbm, q_ref), ("dest", dest_hbm, dest_ref), ("tile", tile_hbm, tile_ref),
        ("stencil", stencil_hbm, stencil), ("table", table_hbm, table),
        ("green", green_hbm, green_ref), ("offset", offset_hbm, offset_ref),
        ("target", target_hbm, target_ref),
    )):
        loads[name] = pltpu.make_async_copy(src, dst, load_sem.at[i])
        loads[name].start()

    def rows_at(name):
        n = dict(TABLES)[name]
        return table[START[name]:START[name] + n, :]

    def half_at(name, half):
        n = dict(TABLES)[name]
        return table[START[name]:START[name] + n, half * LANES:(half + 1) * LANES]

    def others(visit):
        def body(g, carry):
            z = (pz + ((Z_DIGITS >> (2 * g)) & 3)) % 4
            x = (px + ((X_DIGITS >> (2 * g)) & 3)) % 4
            for dy in (2, 1, 3, 0):
                for dc in (1, 0):
                    def go(z=z, x=x, dy=dy, dc=dc):
                        visit(z * 8 + x * 2 + (pc + dc) % 2, (slab + dy) % 4)

                    if dy == 0 and dc == 0:
                        pl.when(g != 15)(go)
                    else:
                        go()
            return carry

        lax.fori_loop(0, 16, body, 0)

    barrier = pltpu.get_barrier_semaphore()
    others(
        lambda p, y: pl.semaphore_signal(barrier, inc=1, device_id=(p, y), device_id_type=MESH)
    )

    def near_load(b, carry):
        pltpu.make_async_copy(
            near_hbm.at[b], near_mat.at[pl.ds(pl.multiple_of(b * 4, 4), 4)], near_sem
        ).start()
        return carry

    rows128, lanes128 = iota((128, 128), 0), iota((128, 128), 1)

    def unfold(ref, out):
        x = ref[...].astype(F32)
        y = pltpu.roll(x, 64, 1)
        low = iota((64, 128), 1) < 64
        out[pl.ds(0, 64, stride=2), :] = jnp.where(low, x, y)
        out[pl.ds(1, 64, stride=2), :] = jnp.where(low, y, x)

    def fold(row, value):
        goal[...] = value
        low = iota((64, 128), 1) < 64
        out_ref[row:row + 64, :] = jnp.where(
            low, goal[pl.ds(0, 64, stride=2), :], goal[pl.ds(1, 64, stride=2), :]
        )

    loads["q"].wait()
    unfold(q_ref, charge)
    val[...] = charge[...]

    def pair(slot, value):
        hi, lo = split(value)
        mats[2 * slot] = hi
        mats[2 * slot + 1] = lo

    def mat(slot):
        return mats[2 * slot], mats[2 * slot + 1]

    every16 = lanes128 % 16 == 0

    def squeeze(tiles):
        total = jnp.where(every16, tiles[0], 0.0)
        for j in range(1, 4):
            total = total + pltpu.roll(jnp.where(every16, tiles[j], 0.0), j, 1)
        return total

    def split_tables():
        def circle(name):
            return half_at(name, 0), half_at(name, 1)

        pair(0, rows_at("w1"))
        c, s = circle("w2")
        pair(1, cat([cat([c, -s], 1), cat([s, c], 1)], 0))
        pair(2, cat([cat([c, s], 1), cat([-s, c], 1)], 0))
        pair(3, rows_at("m0"))
        pair(4, rows_at("m0i"))
        c, s = circle("a1")
        pair(5, cat([cat([c, s], 1), cat([-s, c], 1)], 0))
        pair(6, cat([cat([c, -s], 1), cat([s, c], 1)], 0))
        for m in range(4):
            base = START["w3"] + 128 * m
            c, s = table[base:base + 128, :LANES], table[base:base + 128, LANES:]
            pair(7 + m, cat([cat([c, -s], 1), cat([s, c], 1)], 0))
            c, s = c.T, s.T
            pair(11 + m, cat([cat([c, s], 1), cat([-s, c], 1)], 0))
        c, s = circle("w5")
        pair(15, cat([cat([c, s], 1), cat([-s, c], 1)], 0))
        t5[:, :LANES] = squeeze([half_at("c%d" % (j // 2), j % 2) for j in range(4)])
        t5[:, LANES:] = squeeze([half_at("s%d" % (j // 2), j % 2) for j in range(4)])

    loads["dest"].wait()
    loads["tile"].wait()
    dest_row = dest_ref[...]
    tile_row = tile_ref[...]

    def column(row):
        return jnp.sum(jnp.where(rows128 == lanes128, row, 0), axis=1, keepdims=True)

    dest_col = column(dest_row)
    same = dest_col == dest_row
    rank_row = jnp.sum(jnp.where(same & (rows128 < lanes128), 1, 0), axis=0, keepdims=True)
    rank_col = jnp.sum(jnp.where(same & (lanes128 < rows128), 1, 0), axis=1, keepdims=True)
    one, zero = F32(1.0), F32(0.0)
    out_pick = cat(
        [jnp.where((dest_row == rows128) & (rank_row == k), one, zero) for k in range(2)], 0
    )
    wanted = iota((128, 512), 1) - 4 * dest_col - 2 * rank_col
    in_pick = [jnp.where(wanted == h, one, zero).astype(BF16) for h in range(2)]
    ids = jnp.sum(out_pick * (tile_row + 1).astype(F32), axis=1, keepdims=True)
    id_rows = jnp.where(lanes128 == 0, ids[:128], jnp.where(lanes128 == 1, ids[128:], 0.0))
    out_pick = out_pick.astype(BF16)

    def exchange(step, src, dst, stride, count):
        mine = pl.ds(pl.multiple_of(me * stride, stride), count)

        def send(p, y):
            theirs = pl.ds(pl.multiple_of((p * SLABS + y) * stride, stride), count)
            pltpu.make_async_remote_copy(
                src_ref=src.at[theirs],
                dst_ref=dst.at[mine],
                send_sem=send_sem.at[step],
                recv_sem=recv_sem.at[step],
                device_id=(p, y),
                device_id_type=MESH,
            ).start()

        others(send)
        pltpu.make_async_copy(src.at[mine], dst.at[mine], recv_sem.at[step]).start()

    def arrived(step, src, dst, count):
        part = pl.ds(0, NDEV * count)
        pltpu.make_async_copy(src.at[part], dst.at[part], recv_sem.at[step]).wait()

    def sent(step, src, dst, count):
        part = pl.ds(0, (NDEV - 1) * count)
        pltpu.make_async_copy(src.at[part], dst.at[part], send_sem.at[step]).wait()

    def put(slot, row, value):
        sbuf[slot, pl.ds(row, NDEV, stride=MSG), :] = value

    def get(slot, row):
        return rbuf[slot, pl.ds(row, NDEV, stride=MSG), :]

    def put_words(slot, re, im):
        for j, w in enumerate(encode(re, im)):
            swords[slot, pl.ds(j, NDEV, stride=4), :] = w

    def get_words(slot):
        return decode([rwords[slot, pl.ds(j, NDEV, stride=4), :] for j in range(4)])

    def next_to(shift):
        other = (me + shift + NDEV) % NDEV
        return (other // SLABS, other % SLABS)

    def edge_copies(src, rows_prev, rows_next, dst, sem):
        for way, (shift, rows) in enumerate(((-1, rows_prev), (1, rows_next))):
            yield pltpu.make_async_remote_copy(
                src_ref=src.at[pl.ds(rows, REACH)],
                dst_ref=dst.at[1 - way],
                send_sem=sem.at[way],
                recv_sem=sem.at[3 - way],
                device_id=next_to(shift),
                device_id_type=MESH,
            )

    halo_copies = list(edge_copies(charge, 0, BLOCKS - REACH, halo, halo_sem))
    rim_copies = list(edge_copies(ext, BLOCKS, BLOCKS + REACH, rim, rim_sem))

    def place(index):
        return jnp.where(index < 128, index, jnp.where(index < 136, index - 136, index - 8))

    def near_forward():
        loads["offset"].wait()
        for copy in halo_copies:
            copy.wait_recv()
        before = jnp.where(me == 0, 0.0, halo[0])
        after = jnp.where(me == NDEV - 1, 0.0, halo[1])
        source = cat([charge[...], before, after], 0).astype(BF16)
        spot = place(iota((128, 144), 1)) - iota((128, 144), 0)
        for k in range(4):
            pick = jnp.where(spot == column(offset_ref[k:k + 1, :]), one, zero).astype(BF16)
            xs[pl.ds(k, 128, stride=4), :] = dot(pick, source)
        pltpu.make_async_copy(near_mat, near_mat, near_sem).wait()
        acc[...] = jnp.zeros((512, 128), F32)

        def body(c, carry):
            col = pl.ds(pl.multiple_of(c * 256, 256), 256)
            gather = jnp.where(
                iota((256, 128), 1) % 64 == c * 4 + iota((256, 128), 0) // 64, one, zero
            ).astype(BF16)
            for r in range(4):
                row = pl.ds(128 * r, 128)
                x = xs[row, :]
                hi, lo = split(near_mat[row, col].astype(F32) * cat([x, x], 1))
                acc[row, :] = acc[row, :] + (dot(hi, gather) + dot(lo, gather))
            return carry

        lax.fori_loop(0, 16, body, 0)
        near[...] = sum(acc[pl.ds(k, 128, stride=4), :] for k in range(4))

    def near_adjoint():
        for k in range(4):
            xs[pl.ds(k, 128, stride=4), :] = val[...]
        acc[...] = jnp.zeros((512, 128), F32)

        def body(c, carry):
            col = pl.ds(pl.multiple_of(c * 256, 256), 256)
            spread = jnp.where(
                iota((128, 256), 0) == c * 4 + iota((128, 256), 1) // 64, one, zero
            ).astype(BF16)
            for r in range(4):
                row = pl.ds(128 * r, 128)
                p = near_mat[row, col].astype(F32) * dot(xs[row, :].astype(BF16), spread)
                acc[row, :] = acc[row, :] + (p[:, :128] + p[:, 128:])
            return carry

        lax.fori_loop(0, 16, body, 0)

    def near_scatter():
        acc[...] = acc[...] + pltpu.roll(acc[...], 64, 1)
        total = jnp.zeros((144, 128), F32)
        spot = place(iota((144, 128), 0)) - iota((144, 128), 1)
        for k in range(4):
            pick = jnp.where(spot == offset_ref[k:k + 1, :], one, zero).astype(BF16)
            hi, lo = split(acc[pl.ds(k, 128, stride=4), :])
            total = total + (dot(pick, hi) + dot(pick, lo))
        ext[...] = total
        for copy in rim_copies:
            copy.start()

    def pack(kk, carry):
        def code(at):
            x = green_ref[:, pl.ds(pl.multiple_of(at * LANES, LANES), LANES)]
            return (x * GREEN_UNIT + 0.5).astype(jnp.int32)

        gsend[pl.ds(kk, 32, stride=16), :] = (code(kk + 16) << 16) | code(kk)
        return carry

    def green_copies():
        k2 = me // 8

        def body(j, carry):
            k1 = (me % 8) * 32 + j
            low = jnp.where(k1 < 128, 1, 0)
            is_mid = jnp.where(k1 == 128, 1, 0)
            is_zero = jnp.where(k1 == 0, 1, 0)
            high = 1 - low - is_mid
            target_dev = low * k1 + high * (256 - k1)
            upper = k2 // 8
            beyond = jnp.where(k2 > 8, 1, 0)
            slot_zero = (1 - upper) * k2 + upper * (1 - beyond) * 16 + beyond * (32 - k2)
            slot_mid = (1 - upper) * (8 + k2) + upper * (39 - k2)
            slot = (low - is_zero) * k2 + is_zero * slot_zero + is_mid * slot_mid + high * (31 - k2)
            src = gsend.at[pl.ds(pl.multiple_of(j * 16, 16), 16)]
            dst = grecv.at[pl.ds(pl.multiple_of(slot * 16, 16), 16)]

            @pl.when(target_dev != me)
            def _():
                pltpu.make_async_remote_copy(
                    src_ref=src, dst_ref=dst, send_sem=gsend_sem.at[j], recv_sem=grecv_sem,
                    device_id=(target_dev // SLABS, target_dev % SLABS), device_id_type=MESH,
                ).start()

            @pl.when(target_dev == me)
            def _():
                pltpu.make_async_copy(src, dst, grecv_sem).start()

            return carry

        lax.fori_loop(0, 32, body, 0)

    def green_sent():
        def body(j, carry):
            k1 = (me % 8) * 32 + j
            low = jnp.where(k1 < 128, 1, 0)
            high = jnp.where(k1 > 128, 1, 0)
            target_dev = low * k1 + high * (256 - k1)

            @pl.when(target_dev != me)
            def _():
                part = pl.ds(pl.multiple_of(j * 16, 16), 16)
                pltpu.make_async_copy(gsend.at[part], grecv.at[part], gsend_sem.at[j]).wait()

            return carry

        lax.fori_loop(0, 32, body, 0)

    def green_ready():
        pltpu.make_async_copy(gsend, grecv, grecv_sem).wait()
        scale = 2.0 ** -24 / GREEN_UNIT
        flip = jnp.where((rows128 + lanes128 == 128) & (rows128 > 0), one, zero).astype(BF16)
        first = jnp.where((rows128 == 0) & (lanes128 == 0), one, zero).astype(BF16)
        eye = jnp.where(rows128 == lanes128, one, zero).astype(BF16)
        turn = cat([flip, first], 1)
        special = every16 & (me == 0)

        def rows_of(base, kappa):
            rows = []
            for n in range(8):
                k = kappa(n)
                words = grecv[pl.ds(base * 16 + k % 16, 16, stride=16), :]
                rows.append(((words >> 16 if k >= 16 else words) & 65535).astype(F32))
            return cat(rows, 0)

        nyquist = []

        for m in range(4):
            def plain(base):
                hi, lo = split(rows_of(base, lambda n: m + 4 * n))
                return dot_nt(eye, hi) + dot_nt(eye, lo)

            def turned(base):
                one_ = rows_of(base, lambda n: 31 - m - 4 * n)
                two_ = rows_of(base, lambda n: (32 - m - 4 * n) % 32)
                hi, lo = split(cat([one_, two_], 1))
                return dot_nt(turn, hi) + dot_nt(turn, lo)

            d, dr, o, orr = plain(0), turned(0), plain(16), turned(16)
            ga[:, m * LANES:(m + 1) * LANES] = (d + jnp.where(special, dr, orr)) * scale
            nyquist.append((o + orr) * scale)
        gb5[...] = squeeze(nyquist)

    lane64 = iota((128, 128), 1) // 64
    row16 = iota((128, 128), 0) % 16

    def project():
        v = val[...]
        spread = cat(
            [jnp.where(lane64 + 2 * i == row16, v, 0.0).astype(BF16) for i in range(8)], 1
        )
        for g in range(8):
            part = stencil[g * 1024:(g + 1) * 1024, :]
            tv[g * 16:(g + 1) * 16, :] = dot(spread[g * 16:(g + 1) * 16, :], part)
        hi, lo = split(tv[...])
        return dot(out_pick, hi) + dot(out_pick, lo)

    def interpolate(own_tiles):
        rows = []
        l64, r16 = iota((16, 128), 1) // 64, iota((16, 128), 0)
        for g in range(8):
            part = stencil[g * 1024:(g + 1) * 1024, :]
            r = dot_nt(own_tiles[g * 16:(g + 1) * 16, :], part)
            acc = jnp.zeros((16, 128), F32)
            for i in range(8):
                acc = acc + jnp.where(l64 + 2 * i == r16, r[:, i * LANES:(i + 1) * LANES], 0.0)
            rows.append(acc)
        far = cat(rows, 0)
        return far + pltpu.roll(far, 64, 1)

    def cmul(re, im, c, s):
        return re * c + im * s, im * c - re * s

    def cmul_conj(re, im, c, s):
        return re * c - im * s, im * c + re * s

    def lane_tile(x, j):
        return x[:, j * LANES:(j + 1) * LANES]

    head = iota((8, 128), 0) == 0

    def special_rows(parts, slot, outs):
        small = dot3(split(cat([p[:8] for p in parts], 0)), mat(slot))
        fixed = []
        for j in range(4):
            out = outs[j]
            h2 = iota((8, 256), 0) == 0
            fixed.append(cat([jnp.where(h2, small[8 * j:8 * j + 8], out[:8]), out[8:]], 0))
        return fixed

    def evaluate(which):
        step0 = which * 4
        first, last = which == 0, which == 1
        fwd, inv_ = which * 2, which * 2 + 1
        out = project()
        for k in range(2):
            for h in range(2):
                put(which, 2 * k + h, lane_tile(out[128 * k:128 * k + 128], h))

        @pl.when(first)
        def _():
            put(0, 4, id_rows)
            pl.semaphore_wait(barrier, NDEV - 1)
            exchange(0, sbuf.at[0], rbuf.at[0], MSG, 5)
            for copy in halo_copies:
                copy.start()
            loads["green"].wait()
            lax.fori_loop(0, 16, pack, 0)
            green_copies()
            lax.fori_loop(0, BLOCKS, near_load, 0)
            loads["table"].wait()
            split_tables()
            loads["target"].wait()
            unfold(target_ref, goal)
            arrived(0, sbuf.at[0], rbuf.at[0], 5)
            idm = get(0, 4)
            tc = iota((128, 256), 1)
            for k in range(2):
                xs[pl.ds(k, 128, stride=2), :] = jnp.broadcast_to(idm[:, k:k + 1], (128, 128))
            ordered = xs[:256, :1].astype(jnp.int32)
            for tr in range(2):
                pick = cat(
                    [
                        jnp.where(idm[:, k:k + 1].astype(jnp.int32) == tc + (tr * 256 + 1), one, zero)
                        for k in range(2)
                    ],
                    0,
                ).astype(BF16)
                back_pick = jnp.where(
                    ordered == iota((256, 256), 1) + (tr * 256 + 1), one, zero
                ).astype(BF16)
                for t in range(2):
                    wf[2 * tr + t] = dot_nt(mats[t], pick).astype(BF16)
                    wi[t, :, tr * 256:(tr + 1) * 256] = dot_nt(back_pick, mats[t]).astype(BF16)

        @pl.when(last)
        def _():
            exchange(4, sbuf.at[1], rbuf.at[1], MSG, 4)
            near_adjoint()
            arrived(4, sbuf.at[1], rbuf.at[1], 4)

        tiles = split(
            cat([cat([get(which, 2 * k + h) for h in range(2)], 1) for k in range(2)], 0)
        )
        c2, s2 = half_at("t2", 0), half_at("t2", 1)
        c1 = cat([rows_at("c0"), rows_at("c1")], 1)
        s1 = cat([rows_at("s0"), rows_at("s1")], 1)
        parts = []
        for tr in range(2):
            y = dot3((wf[2 * tr], wf[2 * tr + 1]), tiles)
            for h in range(2):
                re, im = cmul(lane_tile(y[:128], h), lane_tile(y[128:], h), c2, s2)
                parts.append(cat([re, im], 1))
        prod = dot3(split(cat(parts, 0)), mat(1))
        outs = special_rows(parts, 3, [prod[128 * j:128 * j + 128] for j in range(4)])
        put_words(fwd, [o[:, :LANES] for o in outs], [o[:, LANES:] for o in outs])
        exchange(step0 + 1, swords.at[fwd], rwords.at[fwd], 4, 4)

        @pl.when(first)
        def _():
            green_ready()

        @pl.when(last)
        def _():
            near_scatter()

        arrived(step0 + 1, swords.at[fwd], rwords.at[fwd], 4)
        re, im = get_words(fwd)
        y = dot3(mat(5), split(cat([cat(re, 1), cat(im, 1)], 0)))
        re, im = cmul(y[:128], y[128:], c1, s1)
        r = [lane_tile(re, j) for j in range(4)]
        i = [lane_tile(im, j) for j in range(4)]
        er, ei, dr, di = r[0] + r[2], i[0] + i[2], r[0] - r[2], i[0] - i[2]
        fr, fi, hr, hi_ = r[1] + r[3], i[1] + i[3], r[1] - r[3], i[1] - i[3]
        vs = [(er + fr, ei + fi), (dr + hi_, di - hr), (er - fr, ei - fi), (dr - hi_, di + hr)]
        spectrum = [dot3(split(cat(list(vs[m]), 1)), mat(7 + m)) for m in range(4)]
        vs = []
        for m in range(4):
            gm = ga[:, m * LANES:(m + 1) * LANES]
            p = dot3(split(spectrum[m] * cat([gm, gm], 1)), mat(11 + m))
            vs.append((p[:, :LANES], p[:, LANES:]))
        r = [v[0] for v in vs]
        i = [v[1] for v in vs]
        er, ei, dr, di = r[0] + r[2], i[0] + i[2], r[0] - r[2], i[0] - i[2]
        fr, fi, hr, hi_ = r[1] + r[3], i[1] + i[3], r[1] - r[3], i[1] - i[3]
        zs = [(er + fr, ei + fi), (dr - hi_, di + hr), (er - fr, ei - fi), (dr + hi_, di - hr)]
        re, im = cmul_conj(cat([z[0] for z in zs], 1), cat([z[1] for z in zs], 1), c1, s1)
        y = dot3(mat(6), split(cat([re, im], 0)))
        g5 = gb5[...]
        p = dot3(
            split(cat([squeeze([f[:, :LANES] for f in spectrum]) * g5,
                       squeeze([f[:, LANES:] for f in spectrum]) * g5], 1)),
            mat(15),
        )
        re, im = cmul_conj(p[:, :LANES], p[:, LANES:], t5[:, :LANES], t5[:, LANES:])
        y5 = dot3((mats[12, 128:, :], mats[13, 128:, :]), split(cat([re, im], 0)))
        here = every16 & (me == 0)
        yr = [lane_tile(y[:128], j) for j in range(4)]
        yi = [
            jnp.where(here, pltpu.roll(y5, LANES - j, 1) if j else y5, lane_tile(y[128:], j))
            for j in range(4)
        ]
        put_words(inv_, yr, yi)
        exchange(step0 + 2, swords.at[inv_], rwords.at[inv_], 4, 4)

        @pl.when(first)
        def _():
            near_forward()

        arrived(step0 + 2, swords.at[inv_], rwords.at[inv_], 4)
        re, im = get_words(inv_)
        parts = [cat([re[j], im[j]], 1) for j in range(4)]
        prod = dot3(split(cat(parts, 0)), mat(2))
        outs = special_rows(parts, 4, [prod[128 * j:128 * j + 128] for j in range(4)])
        zs = [cmul_conj(o[:, :LANES], o[:, LANES:], c2, s2) for o in outs]
        y = cat(
            [
                cat([cat([zs[2 * tr][0], zs[2 * tr + 1][0]], 1), cat([zs[2 * tr][1], zs[2 * tr + 1][1]], 1)], 0)
                for tr in range(2)
            ],
            0,
        )
        back = dot3((wi[0], wi[1]), split(y))
        for h in range(2):
            xs[pl.ds(h, 256, stride=2), :] = lane_tile(back, h)
        sback[which] = xs[...].astype(BF16)
        exchange(step0 + 3, sback.at[which], rback.at[which], 4, 4)
        arrived(step0 + 3, sback.at[which], rback.at[which], 4)
        tiles = rback[which]
        far = interpolate(cat([dot(in_pick[h], tiles) for h in range(2)], 1).astype(BF16))

        @pl.when(first)
        def _():
            pot = far + near[...]
            val[...] = (pot - goal[...]).astype(BF16).astype(F32)
            fold(0, pot)

        @pl.when(last)
        def _():
            for copy in rim_copies:
                copy.wait_recv()
            before = jnp.where(me == 0, 0.0, rim[0])
            after = jnp.where(me == NDEV - 1, 0.0, rim[1])
            grad = far + ext[:BLOCKS, :]
            grad = cat(
                [grad[:REACH] + before, grad[REACH:BLOCKS - REACH], grad[BLOCKS - REACH:] + after], 0
            )
            fold(64, grad)

    loads["stencil"].wait()

    def both_passes(which, carry):
        evaluate(which)
        return carry

    lax.fori_loop(0, 2, both_passes, 0)
    for p in range(2):
        sent(4 * p, sbuf.at[p], rbuf.at[p], 5 - p)
        sent(4 * p + 1, swords.at[2 * p], rwords.at[2 * p], 4)
        sent(4 * p + 2, swords.at[2 * p + 1], rwords.at[2 * p + 1], 4)
        sent(4 * p + 3, sback.at[p], rback.at[p], 4)
    green_sent()
    for copy in halo_copies + rim_copies:
        copy.wait_send()


def local(table, charges, target, stencil, near_matrix, green, block_dest, block_tile, near_offset):
    out = pl.pallas_call(
        kernel,
        out_shape=jax.ShapeDtypeStruct((128, LANES), F32),
        in_specs=[pl.BlockSpec(memory_space=pl.ANY)] * 9,
        out_specs=pl.BlockSpec(memory_space=pltpu.VMEM),
        scratch_shapes=[
            pltpu.VMEM((64, LANES), BF16),
            pltpu.VMEM((64, LANES), F32),
            pltpu.VMEM((32, GRID), F32),
            pltpu.VMEM((1, LANES), jnp.int32),
            pltpu.VMEM((1, LANES), jnp.int32),
            pltpu.VMEM((4, LANES), jnp.int32),
            pltpu.VMEM((TABLE_ROWS, 256), F32),
            pltpu.VMEM((BLOCKS * PANEL, CELLS), BF16),
            pltpu.VMEM((4 * BLOCKS, PANEL * PANEL), BF16),
            pltpu.VMEM((2, ROWS, LANES), F32),
            pltpu.VMEM((2, ROWS, LANES), F32),
            pltpu.VMEM((2, 4 * NDEV, LANES), BF16),
            pltpu.VMEM((2, 4 * NDEV, LANES), BF16),
            pltpu.VMEM((4, 4 * NDEV, LANES), jnp.int32),
            pltpu.VMEM((4, 4 * NDEV, LANES), jnp.int32),
            pltpu.VMEM((512, LANES), jnp.int32),
            pltpu.VMEM((512, LANES), jnp.int32),
            pltpu.VMEM((128, 512), F32),
            pltpu.VMEM((128, LANES), F32),
            pltpu.VMEM((128, 256), F32),
            pltpu.VMEM((128, 128), F32),
            pltpu.VMEM((128, 128), F32),
            pltpu.VMEM((128, 128), F32),
            pltpu.VMEM((128, 256), F32),
            pltpu.VMEM((4, 256, 256), BF16),
            pltpu.VMEM((2, 256, 512), BF16),
            pltpu.VMEM((32, 256, 256), BF16),
            pltpu.VMEM((512, LANES), F32),
            pltpu.VMEM((512, LANES), F32),
            pltpu.VMEM((128, LANES), F32),
            pltpu.VMEM((144, LANES), F32),
            pltpu.VMEM((2, REACH, LANES), F32),
            pltpu.VMEM((2, REACH, LANES), F32),
            pltpu.SemaphoreType.DMA((8,)),
            pltpu.SemaphoreType.DMA((8,)),
            pltpu.SemaphoreType.DMA((32,)),
            pltpu.SemaphoreType.DMA,
            pltpu.SemaphoreType.DMA((8,)),
            pltpu.SemaphoreType.DMA,
            pltpu.SemaphoreType.DMA((4,)),
            pltpu.SemaphoreType.DMA((4,)),
        ],
        compiler_params=pltpu.CompilerParams(collective_id=0, has_side_effects=True),
        name="panel_solver",
    )(
        charges.reshape(64, LANES), target.reshape(64, LANES),
        stencil.reshape(BLOCKS * PANEL, CELLS), near_matrix, green.T,
        block_dest.reshape(1, BLOCKS), block_tile.reshape(1, BLOCKS), near_offset.T, table,
    )
    return (out[:64].reshape(-1), out[64:].reshape(-1))


def solution(mesh):
    table = jnp.asarray(make_tables())
    return jax.shard_map(
        functools.partial(local, table),
        mesh=mesh,
        in_specs=(
            P(("panel", "slab")),
            P(("panel", "slab")),
            P(("panel", "slab"), None, None),
            P(("panel", "slab"), None, None),
            P(None, ("panel", "slab")),
            P(("panel", "slab"), None),
            P(("panel", "slab")),
            P(("panel", "slab"), None),
        ),
        out_specs=(P(("panel", "slab")), P(("panel", "slab"))),
        check_vma=False,
    )
```

```python
import functools
import math

import jax
import jax.numpy as jnp
import numpy as np
from jax import lax
from jax.experimental import pallas as pl
from jax.experimental.pallas import tpu as pltpu
from jax.sharding import PartitionSpec as P

GRID = 4096
TILE = 16
REACH = 8
NDEV = 128
SLABS = 4
BLOCKS = 128
PANEL = 64
CELLS = 256
LANES = 128
GREEN_UNIT = 8191.0
MESH = pl.DeviceIdType.MESH
F32 = jnp.float32
BF16 = jnp.bfloat16
TABLES = (("w1", 256), ("m0", 256), ("m0i", 256), ("w2", 128), ("a1", 128), ("w3", 512), ("w5", 128), ("t2", 128),
          ("c0", 128), ("c1", 128), ("s0", 128), ("s1", 128))
START = {name: sum(n for _, n in TABLES[:i]) for i, (name, _) in enumerate(TABLES)}
TABLE_ROWS = sum(n for _, n in TABLES)


def make_tables():
    def angle(rows, cols, modulus):
        return 2.0 * math.pi / modulus * ((np.outer(rows, cols)) % modulus)

    out = {}
    th = angle(np.arange(128), np.arange(256), 256)
    w1 = np.concatenate([np.cos(th), -np.sin(th)], 0)
    w1[128] = (-1.0) ** np.arange(256)
    out["w1"] = w1
    th = angle(np.arange(16), np.arange(16), 16)
    c, s = np.kron(np.eye(8), np.cos(th)), np.kron(np.eye(8), np.sin(th))
    out["w2"] = np.concatenate([c, s], 1)
    m0 = np.zeros((2, 16, 2, 16))
    idx = np.arange(16)
    m0[0, :, 0, 0] = 1.0
    m0[0, :, 1, 0] = (-1.0) ** idx
    for k in range(1, 8):
        t = 2 * math.pi * ((idx * k) % 16) / 16
        m0[0, :, 0, k], m0[0, :, 1, k] = np.cos(t), -np.sin(t)
    for n in range(8):
        t = 2 * math.pi * ((idx * (1 + 2 * n)) % 32) / 32
        m0[1, :, 0, 8 + n], m0[1, :, 1, 8 + n] = np.cos(t), -np.sin(t)
    big = np.zeros((2, 8, 16, 2, 8, 16))
    for a in range(8):
        big[:, a, :, :, a, :] = m0
    out["m0"] = big.reshape(256, 256)
    inv = m0.copy()
    inv[:, :, :, 0] *= 0.5
    big = np.zeros((2, 8, 16, 2, 8, 16))
    for a in range(8):
        big[:, a, :, :, a, :] = inv
    out["m0i"] = big.reshape(256, 256).T
    th = angle(np.arange(128), np.arange(128), 128)
    out["a1"] = np.concatenate([np.cos(th), np.sin(th)], 1)
    parts = []
    for m in range(4):
        th = angle(np.arange(8), m + 4 * np.arange(8), 32)
        parts.append(
            np.concatenate([np.kron(np.cos(th), np.eye(16)), np.kron(np.sin(th), np.eye(16))], 1)
        )
    out["w3"] = np.concatenate(parts, 0)
    w5 = np.zeros((2, 8, 16, 8, 16))
    for m in range(4):
        for j in range(4):
            th = angle(m + 4 * np.arange(8), 8 * j + np.arange(8), 32)
            w5[0, :, m, :, j], w5[1, :, m, :, j] = np.cos(th), np.sin(th)
    out["w5"] = np.concatenate([w5[0].reshape(128, 128), w5[1].reshape(128, 128)], 1)
    th = np.tile(angle(np.arange(128), np.arange(16), GRID), (1, 8))
    th[0] = 0.0
    out["t2"] = np.concatenate([np.cos(th), np.sin(th)], 1)
    th = np.repeat(angle(np.arange(128), np.arange(32), GRID), 16, axis=1)
    out["c0"], out["c1"] = np.cos(th[:, :256]), np.cos(th[:, 256:])
    out["s0"], out["s1"] = np.sin(th[:, :256]), np.sin(th[:, 256:])
    return np.concatenate([out[name] for name, _ in TABLES], 0).astype(np.float32)


def dot(a, b):
    return lax.dot_general(a, b, (((1,), (0,)), ((), ())), preferred_element_type=F32)


def dot_nt(a, b):
    return lax.dot_general(a, b, (((1,), (1,)), ((), ())), preferred_element_type=F32)


def split(x):
    hi = x.astype(BF16)
    return hi, (x - hi.astype(F32)).astype(BF16)


def dot3(a, b):
    n = a[0].shape[0]
    both = dot(jnp.concatenate(a, 0), b[0])
    return both[:n] + (both[n:] + dot(a[0], b[1]))


def iota(shape, dim):
    return lax.broadcasted_iota(jnp.int32, shape, dim)


def cat(parts, axis):
    return jnp.concatenate(parts, axis=axis)


COMBOS = sorted(
    ((dz, dx) for dz in range(4) for dx in range(4)),
    key=lambda c: -(min(c[0], 4 - c[0]) + min(c[1], 4 - c[1])),
)
Z_DIGITS = sum(c[0] << (2 * i) for i, c in enumerate(COMBOS))
X_DIGITS = sum(c[1] << (2 * i) for i, c in enumerate(COMBOS))


def encode(re, im):
    top = jnp.abs(re[0])
    for x in list(re[1:]) + list(im):
        top = jnp.maximum(top, jnp.abs(x))
    top = jnp.maximum(top, 2.0 ** -100)
    power = jnp.floor(jnp.log2(top)) + 1.0
    scale = jnp.exp2(14.0 - power)
    code = power.astype(jnp.int32) + 128

    def mantissa(x):
        return jnp.minimum(x * scale + 16384.5, 32767.5).astype(jnp.int32)

    return [
        (((code >> (2 * j)) & 3) << 30) | (mantissa(re[j]) << 15) | mantissa(im[j])
        for j in range(4)
    ]


def decode(words):
    code = words[0] >> 30 & 3
    for j in range(1, 4):
        code = code | ((words[j] >> 30 & 3) << (2 * j))
    scale = jnp.exp2(code.astype(F32) - 142.0)
    re = [((w >> 15 & 32767).astype(F32) - 16384.0) * scale for w in words]
    im = [((w & 32767).astype(F32) - 16384.0) * scale for w in words]
    return re, im


def encode_pairs(values):
    flat = [x for pair in values for x in pair]
    top = jnp.abs(flat[0])
    for x in flat[1:]:
        top = jnp.maximum(top, jnp.abs(x))
    power = jnp.floor(jnp.log2(jnp.maximum(top, 2.0 ** -100))) + 1.0
    scale = jnp.exp2(13.0 - power)
    code = power.astype(jnp.int32) + 128

    def mantissa(x):
        return jnp.minimum(x * scale + 8192.5, 16383.5).astype(jnp.int32)

    return [
        (((code >> (4 * k)) & 15) << 28) | (mantissa(a) << 14) | mantissa(b)
        for k, (a, b) in enumerate(values)
    ]


def decode_pairs(words):
    code = (words[0] >> 28 & 15) | ((words[1] >> 28 & 15) << 4)
    scale = jnp.exp2(code.astype(F32) - 141.0)
    return [
        [((w >> at & 16383).astype(F32) - 8192.0) * scale for at in (14, 0)] for w in words
    ]


def kernel(
    q_hbm, target_hbm, stencil_hbm, near_hbm, green_hbm, dest_hbm, tile_hbm, offset_hbm, table_hbm,
    out_ref,
    q_ref, target_ref, green_ref, dest_ref, tile_ref, offset_ref, table,
    stencil, near_mat, sback, rback, swords, rwords, gsend, grecv, ga, gb5, t5, val, charge, goal, tv,
    wf, wi, mats, xs, acc, near, ext, halo, rim,
    send_sem, recv_sem, gsend_sem, grecv_sem, load_sem, near_sem, halo_sem, rim_sem,
):
    panel = lax.axis_index("panel")
    slab = lax.axis_index("slab")
    me = panel * SLABS + slab
    pz, px, pc = panel // 8, (panel // 2) % 4, panel % 2

    def rows_at(name):
        n = dict(TABLES)[name]
        return table[START[name]:START[name] + n, :]

    def half_at(name, half):
        n = dict(TABLES)[name]
        return table[START[name]:START[name] + n, half * LANES:(half + 1) * LANES]

    def others(visit):
        def body(g, carry):
            z = (pz + ((Z_DIGITS >> (2 * g)) & 3)) % 4
            x = (px + ((X_DIGITS >> (2 * g)) & 3)) % 4
            for dy in (2, 1, 3, 0):
                for dc in (1, 0):
                    def go(z=z, x=x, dy=dy, dc=dc):
                        visit(z * 8 + x * 2 + (pc + dc) % 2, (slab + dy) % 4)

                    if dy == 0 and dc == 0:
                        pl.when(g != 15)(go)
                    else:
                        go()
            return carry

        lax.fori_loop(0, 16, body, 0)

    barrier = pltpu.get_barrier_semaphore()
    others(
        lambda p, y: pl.semaphore_signal(barrier, inc=1, device_id=(p, y), device_id_type=MESH)
    )

    loads = {}
    for i, (name, src, dst) in enumerate((
        ("q", q_hbm, q_ref), ("dest", dest_hbm, dest_ref), ("tile", tile_hbm, tile_ref),
        ("stencil", stencil_hbm, stencil), ("table", table_hbm, table),
        ("green", green_hbm, green_ref), ("offset", offset_hbm, offset_ref),
        ("target", target_hbm, target_ref),
    )):
        loads[name] = pltpu.make_async_copy(src, dst, load_sem.at[i])
        loads[name].start()

    def near_load(b, carry):
        pltpu.make_async_copy(
            near_hbm.at[b], near_mat.at[pl.ds(pl.multiple_of(b * 4, 4), 4)], near_sem
        ).start()
        return carry

    rows128, lanes128 = iota((128, 128), 0), iota((128, 128), 1)

    def unfold(ref, out):
        x = ref[...].astype(F32)
        y = pltpu.roll(x, 64, 1)
        low = iota((64, 128), 1) < 64
        out[pl.ds(0, 64, stride=2), :] = jnp.where(low, x, y)
        out[pl.ds(1, 64, stride=2), :] = jnp.where(low, y, x)

    def fold(row, value):
        goal[...] = value
        low = iota((64, 128), 1) < 64
        out_ref[row:row + 64, :] = jnp.where(
            low, goal[pl.ds(0, 64, stride=2), :], goal[pl.ds(1, 64, stride=2), :]
        )

    loads["q"].wait()
    unfold(q_ref, charge)
    val[...] = charge[...]

    def pair(slot, value):
        hi, lo = split(value)
        mats[2 * slot] = hi
        mats[2 * slot + 1] = lo

    def mat(slot):
        return mats[2 * slot], mats[2 * slot + 1]

    every16 = lanes128 % 16 == 0

    def squeeze(tiles):
        total = jnp.where(every16, tiles[0], 0.0)
        for j in range(1, 4):
            total = total + pltpu.roll(jnp.where(every16, tiles[j], 0.0), j, 1)
        return total

    def split_tables():
        def circle(name):
            return half_at(name, 0), half_at(name, 1)

        pair(0, rows_at("w1"))
        c, s = circle("w2")
        pair(1, cat([cat([c, -s], 1), cat([s, c], 1)], 0))
        pair(2, cat([cat([c, s], 1), cat([-s, c], 1)], 0))
        pair(3, rows_at("m0"))
        pair(4, rows_at("m0i"))
        c, s = circle("a1")
        pair(5, cat([cat([c, s], 1), cat([-s, c], 1)], 0))
        pair(6, cat([cat([c, -s], 1), cat([s, c], 1)], 0))
        for m in range(4):
            base = START["w3"] + 128 * m
            c, s = table[base:base + 128, :LANES], table[base:base + 128, LANES:]
            pair(7 + m, cat([cat([c, -s], 1), cat([s, c], 1)], 0))
            c, s = c.T, s.T
            pair(11 + m, cat([cat([c, s], 1), cat([-s, c], 1)], 0))
        c, s = circle("w5")
        pair(15, cat([cat([c, s], 1), cat([-s, c], 1)], 0))
        t5[:, :LANES] = squeeze([half_at("c%d" % (j // 2), j % 2) for j in range(4)])
        t5[:, LANES:] = squeeze([half_at("s%d" % (j // 2), j % 2) for j in range(4)])

    loads["dest"].wait()
    loads["tile"].wait()
    dest_row = dest_ref[...]
    tile_row = tile_ref[...]

    def column(row):
        return jnp.sum(jnp.where(rows128 == lanes128, row, 0), axis=1, keepdims=True)

    dest_col = column(dest_row)
    same = dest_col == dest_row
    rank_row = jnp.sum(jnp.where(same & (rows128 < lanes128), 1, 0), axis=0, keepdims=True)
    rank_col = jnp.sum(jnp.where(same & (lanes128 < rows128), 1, 0), axis=1, keepdims=True)
    one, zero = F32(1.0), F32(0.0)
    out_pick = cat(
        [jnp.where((dest_row == rows128) & (rank_row == k), one, zero) for k in range(2)], 0
    )
    wanted = iota((128, 512), 1) - 4 * dest_col - 2 * rank_col
    in_pick = [jnp.where(wanted == h, one, zero).astype(BF16) for h in range(2)]
    ids = jnp.sum(out_pick * (tile_row + 1).astype(F32), axis=1, keepdims=True)
    id_rows = jnp.where(lanes128 == 0, ids[:128], jnp.where(lanes128 == 1, ids[128:], 0.0))
    out_pick = out_pick.astype(BF16)

    def exchange(step, src, dst, stride, count):
        mine = pl.ds(pl.multiple_of(me * stride, stride), count)

        def send(p, y):
            theirs = pl.ds(pl.multiple_of((p * SLABS + y) * stride, stride), count)
            pltpu.make_async_remote_copy(
                src_ref=src.at[theirs],
                dst_ref=dst.at[mine],
                send_sem=send_sem.at[step],
                recv_sem=recv_sem.at[step],
                device_id=(p, y),
                device_id_type=MESH,
            ).start()

        others(send)
        pltpu.make_async_copy(src.at[mine], dst.at[mine], recv_sem.at[step]).start()

    def arrived(step, src, dst, count):
        part = pl.ds(0, NDEV * count)
        pltpu.make_async_copy(src.at[part], dst.at[part], recv_sem.at[step]).wait()

    def sent(step, src, dst, count):
        part = pl.ds(0, (NDEV - 1) * count)
        pltpu.make_async_copy(src.at[part], dst.at[part], send_sem.at[step]).wait()

    def put_row(slot, row, value):
        swords[slot, pl.ds(row, NDEV, stride=4), :] = value

    def get_row(slot, row):
        return rwords[slot, pl.ds(row, NDEV, stride=4), :]

    def put_words(slot, re, im):
        for j, w in enumerate(encode(re, im)):
            put_row(slot, j, w)

    def get_words(slot):
        return decode([get_row(slot, j) for j in range(4)])

    def next_to(shift):
        other = (me + shift + NDEV) % NDEV
        return (other // SLABS, other % SLABS)

    def edge_copies(src, rows_prev, rows_next, dst, sem):
        for way, (shift, rows) in enumerate(((-1, rows_prev), (1, rows_next))):
            yield pltpu.make_async_remote_copy(
                src_ref=src.at[pl.ds(rows, REACH)],
                dst_ref=dst.at[1 - way],
                send_sem=sem.at[way],
                recv_sem=sem.at[3 - way],
                device_id=next_to(shift),
                device_id_type=MESH,
            )

    halo_copies = list(edge_copies(charge, 0, BLOCKS - REACH, halo, halo_sem))
    rim_copies = list(edge_copies(ext, BLOCKS, BLOCKS + REACH, rim, rim_sem))

    def place(index):
        return jnp.where(index < 128, index, jnp.where(index < 136, index - 136, index - 8))

    def near_forward():
        loads["offset"].wait()
        for copy in halo_copies:
            copy.wait_recv()
        before = jnp.where(me == 0, 0.0, halo[0])
        after = jnp.where(me == NDEV - 1, 0.0, halo[1])
        source = cat([charge[...], before, after], 0).astype(BF16)
        spot = place(iota((128, 144), 1)) - iota((128, 144), 0)
        for k in range(4):
            pick = jnp.where(spot == column(offset_ref[k:k + 1, :]), one, zero).astype(BF16)
            xs[pl.ds(k, 128, stride=4), :] = dot(pick, source)
        pltpu.make_async_copy(near_mat, near_mat, near_sem).wait()
        acc[...] = jnp.zeros((512, 128), F32)

        def body(c, carry):
            col = pl.ds(pl.multiple_of(c * 256, 256), 256)
            gather = jnp.where(
                iota((256, 128), 1) % 64 == c * 4 + iota((256, 128), 0) // 64, one, zero
            ).astype(BF16)
            for r in range(4):
                row = pl.ds(128 * r, 128)
                x = xs[row, :]
                hi, lo = split(near_mat[row, col].astype(F32) * cat([x, x], 1))
                acc[row, :] = acc[row, :] + (dot(hi, gather) + dot(lo, gather))
            return carry

        lax.fori_loop(0, 16, body, 0)
        near[...] = sum(acc[pl.ds(k, 128, stride=4), :] for k in range(4))

    def near_adjoint():
        for k in range(4):
            xs[pl.ds(k, 128, stride=4), :] = val[...]
        acc[...] = jnp.zeros((512, 128), F32)

        def body(c, carry):
            col = pl.ds(pl.multiple_of(c * 256, 256), 256)
            spread = jnp.where(
                iota((128, 256), 0) == c * 4 + iota((128, 256), 1) // 64, one, zero
            ).astype(BF16)
            for r in range(4):
                row = pl.ds(128 * r, 128)
                p = near_mat[row, col].astype(F32) * dot(xs[row, :].astype(BF16), spread)
                acc[row, :] = acc[row, :] + (p[:, :128] + p[:, 128:])
            return carry

        lax.fori_loop(0, 16, body, 0)

    def near_scatter():
        acc[...] = acc[...] + pltpu.roll(acc[...], 64, 1)
        total = jnp.zeros((144, 128), F32)
        spot = place(iota((144, 128), 0)) - iota((144, 128), 1)
        for k in range(4):
            pick = jnp.where(spot == offset_ref[k:k + 1, :], one, zero).astype(BF16)
            hi, lo = split(acc[pl.ds(k, 128, stride=4), :])
            total = total + (dot(pick, hi) + dot(pick, lo))
        ext[...] = total
        for copy in rim_copies:
            copy.start()

    def pack(kk, carry):
        def code(at):
            x = green_ref[:, pl.ds(pl.multiple_of(at * LANES, LANES), LANES)]
            return (x * GREEN_UNIT + 0.5).astype(jnp.int32)

        gsend[pl.ds(kk, 32, stride=16), :] = (code(kk + 16) << 16) | code(kk)
        return carry

    def green_copies():
        k2 = me // 8

        def body(j, carry):
            k1 = (me % 8) * 32 + j
            low = jnp.where(k1 < 128, 1, 0)
            is_mid = jnp.where(k1 == 128, 1, 0)
            is_zero = jnp.where(k1 == 0, 1, 0)
            high = 1 - low - is_mid
            target_dev = low * k1 + high * (256 - k1)
            upper = k2 // 8
            beyond = jnp.where(k2 > 8, 1, 0)
            slot_zero = (1 - upper) * k2 + upper * (1 - beyond) * 16 + beyond * (32 - k2)
            slot_mid = (1 - upper) * (8 + k2) + upper * (39 - k2)
            slot = (low - is_zero) * k2 + is_zero * slot_zero + is_mid * slot_mid + high * (31 - k2)
            src = gsend.at[pl.ds(pl.multiple_of(j * 16, 16), 16)]
            dst = grecv.at[pl.ds(pl.multiple_of(slot * 16, 16), 16)]

            @pl.when(target_dev != me)
            def _():
                pltpu.make_async_remote_copy(
                    src_ref=src, dst_ref=dst, send_sem=gsend_sem.at[j], recv_sem=grecv_sem,
                    device_id=(target_dev // SLABS, target_dev % SLABS), device_id_type=MESH,
                ).start()

            @pl.when(target_dev == me)
            def _():
                pltpu.make_async_copy(src, dst, grecv_sem).start()

            return carry

        lax.fori_loop(0, 32, body, 0)

    def green_sent():
        def body(j, carry):
            k1 = (me % 8) * 32 + j
            low = jnp.where(k1 < 128, 1, 0)
            high = jnp.where(k1 > 128, 1, 0)
            target_dev = low * k1 + high * (256 - k1)

            @pl.when(target_dev != me)
            def _():
                part = pl.ds(pl.multiple_of(j * 16, 16), 16)
                pltpu.make_async_copy(gsend.at[part], grecv.at[part], gsend_sem.at[j]).wait()

            return carry

        lax.fori_loop(0, 32, body, 0)

    def green_ready():
        pltpu.make_async_copy(gsend, grecv, grecv_sem).wait()
        scale = 2.0 ** -24 / GREEN_UNIT
        flip = jnp.where((rows128 + lanes128 == 128) & (rows128 > 0), one, zero).astype(BF16)
        first = jnp.where((rows128 == 0) & (lanes128 == 0), one, zero).astype(BF16)
        eye = jnp.where(rows128 == lanes128, one, zero).astype(BF16)
        turn = cat([flip, first], 1)
        special = every16 & (me == 0)

        def rows_of(base, kappa):
            rows = []
            for n in range(8):
                k = kappa(n)
                words = grecv[pl.ds(base * 16 + k % 16, 16, stride=16), :]
                rows.append(((words >> 16 if k >= 16 else words) & 65535).astype(F32))
            return cat(rows, 0)

        nyquist = []

        for m in range(4):
            def plain(base):
                hi, lo = split(rows_of(base, lambda n: m + 4 * n))
                return dot_nt(eye, hi) + dot_nt(eye, lo)

            def turned(base):
                one_ = rows_of(base, lambda n: 31 - m - 4 * n)
                two_ = rows_of(base, lambda n: (32 - m - 4 * n) % 32)
                hi, lo = split(cat([one_, two_], 1))
                return dot_nt(turn, hi) + dot_nt(turn, lo)

            d, dr, o, orr = plain(0), turned(0), plain(16), turned(16)
            ga[:, m * LANES:(m + 1) * LANES] = (d + jnp.where(special, dr, orr)) * scale
            nyquist.append((o + orr) * scale)
        gb5[...] = squeeze(nyquist)

    lane64 = iota((128, 128), 1) // 64
    row16 = iota((128, 128), 0) % 16

    def project():
        v = val[...]
        spread = cat(
            [jnp.where(lane64 + 2 * i == row16, v, 0.0).astype(BF16) for i in range(8)], 1
        )
        for g in range(8):
            part = stencil[g * 1024:(g + 1) * 1024, :]
            tv[g * 16:(g + 1) * 16, :] = dot(spread[g * 16:(g + 1) * 16, :], part)
        hi, lo = split(tv[...])
        return dot(out_pick, hi) + dot(out_pick, lo)

    def interpolate(own_tiles):
        rows = []
        l64, r16 = iota((16, 128), 1) // 64, iota((16, 128), 0)
        for g in range(8):
            part = stencil[g * 1024:(g + 1) * 1024, :]
            r = dot_nt(own_tiles[g * 16:(g + 1) * 16, :], part)
            acc = jnp.zeros((16, 128), F32)
            for i in range(8):
                acc = acc + jnp.where(l64 + 2 * i == r16, r[:, i * LANES:(i + 1) * LANES], 0.0)
            rows.append(acc)
        far = cat(rows, 0)
        return far + pltpu.roll(far, 64, 1)

    def cmul(re, im, c, s):
        return re * c + im * s, im * c - re * s

    def cmul_conj(re, im, c, s):
        return re * c - im * s, im * c + re * s

    def lane_tile(x, j):
        return x[:, j * LANES:(j + 1) * LANES]

    head = iota((8, 128), 0) == 0

    def special_rows(parts, slot, outs):
        small = dot3(split(cat([p[:8] for p in parts], 0)), mat(slot))
        fixed = []
        for j in range(4):
            out = outs[j]
            h2 = iota((8, 256), 0) == 0
            fixed.append(cat([jnp.where(h2, small[8 * j:8 * j + 8], out[:8]), out[8:]], 0))
        return fixed

    def evaluate(which):
        step0 = which * 4
        first, last = which == 0, which == 1
        fwd, inv_ = which * 2, which * 2 + 1
        out = project()
        coded = encode_pairs(
            [[lane_tile(out[128 * k:128 * k + 128], h) for h in range(2)] for k in range(2)]
        )
        for k in range(2):
            put_row(4 + which, k, coded[k])

        @pl.when(first)
        def _():
            put_row(4, 2, id_rows.astype(jnp.int32))
            pl.semaphore_wait(barrier, NDEV - 1)
            exchange(0, swords.at[4], rwords.at[4], 4, 3)
            for copy in halo_copies:
                copy.start()
            loads["green"].wait()
            lax.fori_loop(0, 16, pack, 0)
            green_copies()
            lax.fori_loop(0, BLOCKS, near_load, 0)
            loads["table"].wait()
            split_tables()
            loads["target"].wait()
            unfold(target_ref, goal)
            arrived(0, swords.at[4], rwords.at[4], 3)
            idm = get_row(4, 2)
            tc = iota((128, 256), 1)
            for k in range(2):
                xs[pl.ds(k, 128, stride=2), :] = jnp.broadcast_to(
                    idm[:, k:k + 1].astype(F32), (128, 128)
                )
            ordered = xs[:256, :1].astype(jnp.int32)
            for tr in range(2):
                pick = cat(
                    [
                        jnp.where(idm[:, k:k + 1] == tc + (tr * 256 + 1), one, zero)
                        for k in range(2)
                    ],
                    0,
                ).astype(BF16)
                back_pick = jnp.where(
                    ordered == iota((256, 256), 1) + (tr * 256 + 1), one, zero
                ).astype(BF16)
                for t in range(2):
                    wf[2 * tr + t] = dot_nt(mats[t], pick).astype(BF16)
                    wi[t, :, tr * 256:(tr + 1) * 256] = dot_nt(back_pick, mats[t]).astype(BF16)

        @pl.when(last)
        def _():
            exchange(4, swords.at[5], rwords.at[5], 4, 2)
            near_adjoint()
            arrived(4, swords.at[5], rwords.at[5], 2)

        values = decode_pairs([get_row(4 + which, k) for k in range(2)])
        tiles = split(cat([cat(v, 1) for v in values], 0))
        c2, s2 = half_at("t2", 0), half_at("t2", 1)
        c1 = cat([rows_at("c0"), rows_at("c1")], 1)
        s1 = cat([rows_at("s0"), rows_at("s1")], 1)
        parts = []
        for tr in range(2):
            y = dot3((wf[2 * tr], wf[2 * tr + 1]), tiles)
            for h in range(2):
                re, im = cmul(lane_tile(y[:128], h), lane_tile(y[128:], h), c2, s2)
                parts.append(cat([re, im], 1))
        prod = dot3(split(cat(parts, 0)), mat(1))
        outs = special_rows(parts, 3, [prod[128 * j:128 * j + 128] for j in range(4)])
        put_words(fwd, [o[:, :LANES] for o in outs], [o[:, LANES:] for o in outs])
        exchange(step0 + 1, swords.at[fwd], rwords.at[fwd], 4, 4)

        @pl.when(first)
        def _():
            green_ready()

        @pl.when(last)
        def _():
            near_scatter()

        arrived(step0 + 1, swords.at[fwd], rwords.at[fwd], 4)
        re, im = get_words(fwd)
        y = dot3(mat(5), split(cat([cat(re, 1), cat(im, 1)], 0)))
        re, im = cmul(y[:128], y[128:], c1, s1)
        r = [lane_tile(re, j) for j in range(4)]
        i = [lane_tile(im, j) for j in range(4)]
        er, ei, dr, di = r[0] + r[2], i[0] + i[2], r[0] - r[2], i[0] - i[2]
        fr, fi, hr, hi_ = r[1] + r[3], i[1] + i[3], r[1] - r[3], i[1] - i[3]
        vs = [(er + fr, ei + fi), (dr + hi_, di - hr), (er - fr, ei - fi), (dr - hi_, di + hr)]
        spectrum = [dot3(split(cat(list(vs[m]), 1)), mat(7 + m)) for m in range(4)]
        vs = []
        for m in range(4):
            gm = ga[:, m * LANES:(m + 1) * LANES]
            p = dot3(split(spectrum[m] * cat([gm, gm], 1)), mat(11 + m))
            vs.append((p[:, :LANES], p[:, LANES:]))
        r = [v[0] for v in vs]
        i = [v[1] for v in vs]
        er, ei, dr, di = r[0] + r[2], i[0] + i[2], r[0] - r[2], i[0] - i[2]
        fr, fi, hr, hi_ = r[1] + r[3], i[1] + i[3], r[1] - r[3], i[1] - i[3]
        zs = [(er + fr, ei + fi), (dr - hi_, di + hr), (er - fr, ei - fi), (dr + hi_, di - hr)]
        re, im = cmul_conj(cat([z[0] for z in zs], 1), cat([z[1] for z in zs], 1), c1, s1)
        y = dot3(mat(6), split(cat([re, im], 0)))
        g5 = gb5[...]
        p = dot3(
            split(cat([squeeze([f[:, :LANES] for f in spectrum]) * g5,
                       squeeze([f[:, LANES:] for f in spectrum]) * g5], 1)),
            mat(15),
        )
        re, im = cmul_conj(p[:, :LANES], p[:, LANES:], t5[:, :LANES], t5[:, LANES:])
        y5 = dot3((mats[12, 128:, :], mats[13, 128:, :]), split(cat([re, im], 0)))
        here = every16 & (me == 0)
        yr = [lane_tile(y[:128], j) for j in range(4)]
        yi = [
            jnp.where(here, pltpu.roll(y5, LANES - j, 1) if j else y5, lane_tile(y[128:], j))
            for j in range(4)
        ]
        put_words(inv_, yr, yi)
        exchange(step0 + 2, swords.at[inv_], rwords.at[inv_], 4, 4)

        @pl.when(first)
        def _():
            near_forward()

        arrived(step0 + 2, swords.at[inv_], rwords.at[inv_], 4)
        re, im = get_words(inv_)
        parts = [cat([re[j], im[j]], 1) for j in range(4)]
        prod = dot3(split(cat(parts, 0)), mat(2))
        outs = special_rows(parts, 4, [prod[128 * j:128 * j + 128] for j in range(4)])
        zs = [cmul_conj(o[:, :LANES], o[:, LANES:], c2, s2) for o in outs]
        y = cat(
            [
                cat([cat([zs[2 * tr][0], zs[2 * tr + 1][0]], 1), cat([zs[2 * tr][1], zs[2 * tr + 1][1]], 1)], 0)
                for tr in range(2)
            ],
            0,
        )
        back = dot3((wi[0], wi[1]), split(y))
        for h in range(2):
            xs[pl.ds(h, 256, stride=2), :] = lane_tile(back, h)
        sback[which] = xs[...].astype(BF16)
        exchange(step0 + 3, sback.at[which], rback.at[which], 4, 4)
        arrived(step0 + 3, sback.at[which], rback.at[which], 4)
        tiles = rback[which]
        far = interpolate(cat([dot(in_pick[h], tiles) for h in range(2)], 1).astype(BF16))

        @pl.when(first)
        def _():
            pot = far + near[...]
            val[...] = (pot - goal[...]).astype(BF16).astype(F32)
            fold(0, pot)

        @pl.when(last)
        def _():
            for copy in rim_copies:
                copy.wait_recv()
            before = jnp.where(me == 0, 0.0, rim[0])
            after = jnp.where(me == NDEV - 1, 0.0, rim[1])
            grad = far + ext[:BLOCKS, :]
            grad = cat(
                [grad[:REACH] + before, grad[REACH:BLOCKS - REACH], grad[BLOCKS - REACH:] + after], 0
            )
            fold(64, grad)

    loads["stencil"].wait()

    def both_passes(which, carry):
        evaluate(which)
        return carry

    lax.fori_loop(0, 2, both_passes, 0)
    for p in range(2):
        sent(4 * p, swords.at[4 + p], rwords.at[4 + p], 3 - p)
        sent(4 * p + 1, swords.at[2 * p], rwords.at[2 * p], 4)
        sent(4 * p + 2, swords.at[2 * p + 1], rwords.at[2 * p + 1], 4)
        sent(4 * p + 3, sback.at[p], rback.at[p], 4)
    green_sent()
    for copy in halo_copies + rim_copies:
        copy.wait_send()


def local(table, charges, target, stencil, near_matrix, green, block_dest, block_tile, near_offset):
    out = pl.pallas_call(
        kernel,
        out_shape=jax.ShapeDtypeStruct((128, LANES), F32),
        in_specs=[pl.BlockSpec(memory_space=pl.ANY)] * 9,
        out_specs=pl.BlockSpec(memory_space=pltpu.VMEM),
        scratch_shapes=[
            pltpu.VMEM((64, LANES), BF16),
            pltpu.VMEM((64, LANES), F32),
            pltpu.VMEM((32, GRID), F32),
            pltpu.VMEM((1, LANES), jnp.int32),
            pltpu.VMEM((1, LANES), jnp.int32),
            pltpu.VMEM((4, LANES), jnp.int32),
            pltpu.VMEM((TABLE_ROWS, 256), F32),
            pltpu.VMEM((BLOCKS * PANEL, CELLS), BF16),
            pltpu.VMEM((4 * BLOCKS, PANEL * PANEL), BF16),
            pltpu.VMEM((2, 4 * NDEV, LANES), BF16),
            pltpu.VMEM((2, 4 * NDEV, LANES), BF16),
            pltpu.VMEM((6, 4 * NDEV, LANES), jnp.int32),
            pltpu.VMEM((6, 4 * NDEV, LANES), jnp.int32),
            pltpu.VMEM((512, LANES), jnp.int32),
            pltpu.VMEM((512, LANES), jnp.int32),
            pltpu.VMEM((128, 512), F32),
            pltpu.VMEM((128, LANES), F32),
            pltpu.VMEM((128, 256), F32),
            pltpu.VMEM((128, 128), F32),
            pltpu.VMEM((128, 128), F32),
            pltpu.VMEM((128, 128), F32),
            pltpu.VMEM((128, 256), F32),
            pltpu.VMEM((4, 256, 256), BF16),
            pltpu.VMEM((2, 256, 512), BF16),
            pltpu.VMEM((32, 256, 256), BF16),
            pltpu.VMEM((512, LANES), F32),
            pltpu.VMEM((512, LANES), F32),
            pltpu.VMEM((128, LANES), F32),
            pltpu.VMEM((144, LANES), F32),
            pltpu.VMEM((2, REACH, LANES), F32),
            pltpu.VMEM((2, REACH, LANES), F32),
            pltpu.SemaphoreType.DMA((8,)),
            pltpu.SemaphoreType.DMA((8,)),
            pltpu.SemaphoreType.DMA((32,)),
            pltpu.SemaphoreType.DMA,
            pltpu.SemaphoreType.DMA((8,)),
            pltpu.SemaphoreType.DMA,
            pltpu.SemaphoreType.DMA((4,)),
            pltpu.SemaphoreType.DMA((4,)),
        ],
        compiler_params=pltpu.CompilerParams(collective_id=0, has_side_effects=True),
        name="panel_solver",
    )(
        charges.reshape(64, LANES), target.reshape(64, LANES),
        stencil.reshape(BLOCKS * PANEL, CELLS), near_matrix, green.T,
        block_dest.reshape(1, BLOCKS), block_tile.reshape(1, BLOCKS), near_offset.T, table,
    )
    return (out[:64].reshape(-1), out[64:].reshape(-1))


def solution(mesh):
    table = jnp.asarray(make_tables())
    return jax.shard_map(
        functools.partial(local, table),
        mesh=mesh,
        in_specs=(
            P(("panel", "slab")),
            P(("panel", "slab")),
            P(("panel", "slab"), None, None),
            P(("panel", "slab"), None, None),
            P(None, ("panel", "slab")),
            P(("panel", "slab"), None),
            P(("panel", "slab")),
            P(("panel", "slab"), None),
        ),
        out_specs=(P(("panel", "slab")), P(("panel", "slab"))),
        check_vma=False,
    )
```

```python
import functools
import math

import jax
import jax.numpy as jnp
import numpy as np
from jax import lax
from jax.experimental import pallas as pl
from jax.experimental.pallas import tpu as pltpu
from jax.sharding import PartitionSpec as P

GRID = 4096
TILE = 16
REACH = 8
NDEV = 128
SLABS = 4
BLOCKS = 128
PANEL = 64
CELLS = 256
LANES = 128
GREEN_UNIT = 8191.0
MESH = pl.DeviceIdType.MESH
F32 = jnp.float32
BF16 = jnp.bfloat16
TABLES = (("w1", 256), ("m0", 256), ("m0i", 256), ("w2", 128), ("a1", 128), ("w3", 512), ("w5", 128), ("t2", 128),
          ("c0", 128), ("c1", 128), ("s0", 128), ("s1", 128))
START = {name: sum(n for _, n in TABLES[:i]) for i, (name, _) in enumerate(TABLES)}
TABLE_ROWS = sum(n for _, n in TABLES)


def make_tables():
    def angle(rows, cols, modulus):
        return 2.0 * math.pi / modulus * ((np.outer(rows, cols)) % modulus)

    out = {}
    th = angle(np.arange(128), np.arange(256), 256)
    w1 = np.concatenate([np.cos(th), -np.sin(th)], 0)
    w1[128] = (-1.0) ** np.arange(256)
    out["w1"] = w1
    th = angle(np.arange(16), np.arange(16), 16)
    c, s = np.kron(np.eye(8), np.cos(th)), np.kron(np.eye(8), np.sin(th))
    out["w2"] = np.concatenate([c, s], 1)
    m0 = np.zeros((2, 16, 2, 16))
    idx = np.arange(16)
    m0[0, :, 0, 0] = 1.0
    m0[0, :, 1, 0] = (-1.0) ** idx
    for k in range(1, 8):
        t = 2 * math.pi * ((idx * k) % 16) / 16
        m0[0, :, 0, k], m0[0, :, 1, k] = np.cos(t), -np.sin(t)
    for n in range(8):
        t = 2 * math.pi * ((idx * (1 + 2 * n)) % 32) / 32
        m0[1, :, 0, 8 + n], m0[1, :, 1, 8 + n] = np.cos(t), -np.sin(t)
    big = np.zeros((2, 8, 16, 2, 8, 16))
    for a in range(8):
        big[:, a, :, :, a, :] = m0
    out["m0"] = big.reshape(256, 256)
    inv = m0.copy()
    inv[:, :, :, 0] *= 0.5
    big = np.zeros((2, 8, 16, 2, 8, 16))
    for a in range(8):
        big[:, a, :, :, a, :] = inv
    out["m0i"] = big.reshape(256, 256).T
    th = angle(np.arange(128), np.arange(128), 128)
    out["a1"] = np.concatenate([np.cos(th), np.sin(th)], 1)
    parts = []
    for m in range(4):
        th = angle(np.arange(8), m + 4 * np.arange(8), 32)
        parts.append(
            np.concatenate([np.kron(np.cos(th), np.eye(16)), np.kron(np.sin(th), np.eye(16))], 1)
        )
    out["w3"] = np.concatenate(parts, 0)
    w5 = np.zeros((2, 8, 16, 8, 16))
    for m in range(4):
        for j in range(4):
            th = angle(m + 4 * np.arange(8), 8 * j + np.arange(8), 32)
            w5[0, :, m, :, j], w5[1, :, m, :, j] = np.cos(th), np.sin(th)
    out["w5"] = np.concatenate([w5[0].reshape(128, 128), w5[1].reshape(128, 128)], 1)
    th = np.tile(angle(np.arange(128), np.arange(16), GRID), (1, 8))
    th[0] = 0.0
    out["t2"] = np.concatenate([np.cos(th), np.sin(th)], 1)
    th = np.repeat(angle(np.arange(128), np.arange(32), GRID), 16, axis=1)
    out["c0"], out["c1"] = np.cos(th[:, :256]), np.cos(th[:, 256:])
    out["s0"], out["s1"] = np.sin(th[:, :256]), np.sin(th[:, 256:])
    return np.concatenate([out[name] for name, _ in TABLES], 0).astype(np.float32)


def dot(a, b):
    return lax.dot_general(a, b, (((1,), (0,)), ((), ())), preferred_element_type=F32)


def dot_nt(a, b):
    return lax.dot_general(a, b, (((1,), (1,)), ((), ())), preferred_element_type=F32)


def split(x):
    hi = x.astype(BF16)
    return hi, (x - hi.astype(F32)).astype(BF16)


def dot3(a, b):
    n = a[0].shape[0]
    both = dot(jnp.concatenate(a, 0), b[0])
    return both[:n] + (both[n:] + dot(a[0], b[1]))


def iota(shape, dim):
    return lax.broadcasted_iota(jnp.int32, shape, dim)


def cat(parts, axis):
    return jnp.concatenate(parts, axis=axis)


COMBOS = sorted(
    ((dz, dx) for dz in range(4) for dx in range(4)),
    key=lambda c: -(min(c[0], 4 - c[0]) + min(c[1], 4 - c[1])),
)
Z_DIGITS = sum(c[0] << (2 * i) for i, c in enumerate(COMBOS))
X_DIGITS = sum(c[1] << (2 * i) for i, c in enumerate(COMBOS))


def encode(re, im):
    top = jnp.abs(re[0])
    for x in list(re[1:]) + list(im):
        top = jnp.maximum(top, jnp.abs(x))
    top = jnp.maximum(top, 2.0 ** -100)
    power = jnp.floor(jnp.log2(top)) + 1.0
    scale = jnp.exp2(14.0 - power)
    code = power.astype(jnp.int32) + 128

    def mantissa(x):
        return jnp.minimum(x * scale + 16384.5, 32767.5).astype(jnp.int32)

    return [
        (((code >> (2 * j)) & 3) << 30) | (mantissa(re[j]) << 15) | mantissa(im[j])
        for j in range(4)
    ]


def decode(words):
    code = words[0] >> 30 & 3
    for j in range(1, 4):
        code = code | ((words[j] >> 30 & 3) << (2 * j))
    scale = jnp.exp2(code.astype(F32) - 142.0)
    re = [((w >> 15 & 32767).astype(F32) - 16384.0) * scale for w in words]
    im = [((w & 32767).astype(F32) - 16384.0) * scale for w in words]
    return re, im


def encode_pairs(values):
    flat = [x for pair in values for x in pair]
    top = jnp.abs(flat[0])
    for x in flat[1:]:
        top = jnp.maximum(top, jnp.abs(x))
    power = jnp.floor(jnp.log2(jnp.maximum(top, 2.0 ** -100))) + 1.0
    scale = jnp.exp2(13.0 - power)
    code = power.astype(jnp.int32) + 128

    def mantissa(x):
        return jnp.minimum(x * scale + 8192.5, 16383.5).astype(jnp.int32)

    return [
        (((code >> (4 * k)) & 15) << 28) | (mantissa(a) << 14) | mantissa(b)
        for k, (a, b) in enumerate(values)
    ]


def decode_pairs(words):
    code = (words[0] >> 28 & 15) | ((words[1] >> 28 & 15) << 4)
    scale = jnp.exp2(code.astype(F32) - 141.0)
    return [
        [((w >> at & 16383).astype(F32) - 8192.0) * scale for at in (14, 0)] for w in words
    ]


def kernel(
    q_hbm, target_hbm, stencil_hbm, near_hbm, green_hbm, dest_hbm, tile_hbm, offset_hbm, table_hbm,
    out_ref,
    q_ref, target_ref, green_ref, dest_ref, tile_ref, offset_ref, table,
    stencil, turned, near_mat, sback, rback, swords, rwords, gsend, grecv, ga, gb5, t5, val, charge, goal, tv,
    wf, wi, mats, xs, order, acc, near, ext, halo, rim,
    send_sem, recv_sem, gsend_sem, grecv_sem, load_sem, near_sem, halo_sem, rim_sem,
):
    panel = lax.axis_index("panel")
    slab = lax.axis_index("slab")
    me = panel * SLABS + slab
    pz, px, pc = panel // 8, (panel // 2) % 4, panel % 2

    def rows_at(name):
        n = dict(TABLES)[name]
        return table[START[name]:START[name] + n, :]

    def half_at(name, half):
        n = dict(TABLES)[name]
        return table[START[name]:START[name] + n, half * LANES:(half + 1) * LANES]

    def others(visit):
        def body(g, carry):
            z = (pz + ((Z_DIGITS >> (2 * g)) & 3)) % 4
            x = (px + ((X_DIGITS >> (2 * g)) & 3)) % 4
            for dy in (2, 1, 3, 0):
                for dc in (1, 0):
                    def go(z=z, x=x, dy=dy, dc=dc):
                        visit(z * 8 + x * 2 + (pc + dc) % 2, (slab + dy) % 4)

                    if dy == 0 and dc == 0:
                        pl.when(g != 15)(go)
                    else:
                        go()
            return carry

        lax.fori_loop(0, 16, body, 0)

    barrier = pltpu.get_barrier_semaphore()
    others(
        lambda p, y: pl.semaphore_signal(barrier, inc=1, device_id=(p, y), device_id_type=MESH)
    )

    loads = {}
    for i, (name, src, dst) in enumerate((
        ("q", q_hbm, q_ref), ("dest", dest_hbm, dest_ref), ("tile", tile_hbm, tile_ref),
        ("stencil", stencil_hbm, stencil), ("table", table_hbm, table),
        ("green", green_hbm, green_ref), ("offset", offset_hbm, offset_ref),
        ("target", target_hbm, target_ref),
    )):
        loads[name] = pltpu.make_async_copy(src, dst, load_sem.at[i])
        loads[name].start()

    def near_load(b, carry):
        pltpu.make_async_copy(
            near_hbm.at[b], near_mat.at[pl.ds(pl.multiple_of(b * 4, 4), 4)], near_sem
        ).start()
        return carry

    rows128, lanes128 = iota((128, 128), 0), iota((128, 128), 1)

    def unfold(ref, out):
        x = ref[...].astype(F32)
        y = pltpu.roll(x, 64, 1)
        low = iota((64, 128), 1) < 64
        out[pl.ds(0, 64, stride=2), :] = jnp.where(low, x, y)
        out[pl.ds(1, 64, stride=2), :] = jnp.where(low, y, x)

    def fold(row, value):
        goal[...] = value
        low = iota((64, 128), 1) < 64
        out_ref[row:row + 64, :] = jnp.where(
            low, goal[pl.ds(0, 64, stride=2), :], goal[pl.ds(1, 64, stride=2), :]
        )

    loads["q"].wait()
    unfold(q_ref, charge)
    val[...] = charge[...]

    def pair(slot, value):
        hi, lo = split(value)
        mats[2 * slot] = hi
        mats[2 * slot + 1] = lo

    def mat(slot):
        return mats[2 * slot], mats[2 * slot + 1]

    every16 = lanes128 % 16 == 0

    def squeeze(tiles):
        total = jnp.where(every16, tiles[0], 0.0)
        for j in range(1, 4):
            total = total + pltpu.roll(jnp.where(every16, tiles[j], 0.0), j, 1)
        return total

    def split_tables():
        def circle(name):
            return half_at(name, 0), half_at(name, 1)

        pair(0, rows_at("w1"))
        c, s = circle("w2")
        pair(1, cat([cat([c, -s], 1), cat([s, c], 1)], 0))
        pair(2, cat([cat([c, s], 1), cat([-s, c], 1)], 0))
        pair(3, rows_at("m0"))
        pair(4, rows_at("m0i"))
        c, s = circle("a1")
        pair(5, cat([cat([c, s], 1), cat([-s, c], 1)], 0))
        pair(6, cat([cat([c, -s], 1), cat([s, c], 1)], 0))
        for m in range(4):
            base = START["w3"] + 128 * m
            c, s = table[base:base + 128, :LANES], table[base:base + 128, LANES:]
            pair(7 + m, cat([cat([c, -s], 1), cat([s, c], 1)], 0))
            c, s = c.T, s.T
            pair(11 + m, cat([cat([c, s], 1), cat([-s, c], 1)], 0))
        c, s = circle("w5")
        pair(15, cat([cat([c, s], 1), cat([-s, c], 1)], 0))
        t5[:, :LANES] = squeeze([half_at("c%d" % (j // 2), j % 2) for j in range(4)])
        t5[:, LANES:] = squeeze([half_at("s%d" % (j // 2), j % 2) for j in range(4)])

    loads["dest"].wait()
    loads["tile"].wait()
    dest_row = dest_ref[...]
    tile_row = tile_ref[...]

    def column(row):
        return jnp.sum(jnp.where(rows128 == lanes128, row, 0), axis=1, keepdims=True)

    dest_col = column(dest_row)
    same = dest_col == dest_row
    rank_row = jnp.sum(jnp.where(same & (rows128 < lanes128), 1, 0), axis=0, keepdims=True)
    rank_col = jnp.sum(jnp.where(same & (lanes128 < rows128), 1, 0), axis=1, keepdims=True)
    one, zero = F32(1.0), F32(0.0)
    out_pick = cat(
        [jnp.where((dest_row == rows128) & (rank_row == k), one, zero) for k in range(2)], 0
    )
    wanted = iota((128, 512), 1) - 4 * dest_col - 2 * rank_col
    in_pick = [jnp.where(wanted == h, one, zero).astype(BF16) for h in range(2)]
    ids = jnp.sum(out_pick * (tile_row + 1).astype(F32), axis=1, keepdims=True)
    id_rows = jnp.where(lanes128 == 0, ids[:128], jnp.where(lanes128 == 1, ids[128:], 0.0))
    out_pick = out_pick.astype(BF16)

    def exchange(step, src, dst, stride, count):
        mine = pl.ds(pl.multiple_of(me * stride, stride), count)

        def send(p, y):
            theirs = pl.ds(pl.multiple_of((p * SLABS + y) * stride, stride), count)
            pltpu.make_async_remote_copy(
                src_ref=src.at[theirs],
                dst_ref=dst.at[mine],
                send_sem=send_sem.at[step],
                recv_sem=recv_sem.at[step],
                device_id=(p, y),
                device_id_type=MESH,
            ).start()

        others(send)
        pltpu.make_async_copy(src.at[mine], dst.at[mine], recv_sem.at[step]).start()

    def arrived(step, src, dst, count):
        part = pl.ds(0, NDEV * count)
        pltpu.make_async_copy(src.at[part], dst.at[part], recv_sem.at[step]).wait()

    def sent(step, src, dst, count):
        part = pl.ds(0, (NDEV - 1) * count)
        pltpu.make_async_copy(src.at[part], dst.at[part], send_sem.at[step]).wait()

    def put_row(slot, row, value):
        swords[slot, pl.ds(row, NDEV, stride=4), :] = value

    def get_row(slot, row):
        return rwords[slot, pl.ds(row, NDEV, stride=4), :]

    def put_words(slot, re, im):
        for j, w in enumerate(encode(re, im)):
            put_row(slot, j, w)

    def get_words(slot):
        return decode([get_row(slot, j) for j in range(4)])

    def next_to(shift):
        other = (me + shift + NDEV) % NDEV
        return (other // SLABS, other % SLABS)

    def edge_copies(src, rows_prev, rows_next, dst, sem):
        for way, (shift, rows) in enumerate(((-1, rows_prev), (1, rows_next))):
            yield pltpu.make_async_remote_copy(
                src_ref=src.at[pl.ds(rows, REACH)],
                dst_ref=dst.at[1 - way],
                send_sem=sem.at[way],
                recv_sem=sem.at[3 - way],
                device_id=next_to(shift),
                device_id_type=MESH,
            )

    halo_copies = list(edge_copies(charge, 0, BLOCKS - REACH, halo, halo_sem))
    rim_copies = list(edge_copies(ext, BLOCKS, BLOCKS + REACH, rim, rim_sem))

    def place(index):
        return jnp.where(index < 128, index, jnp.where(index < 136, index - 136, index - 8))

    def near_forward():
        loads["offset"].wait()
        for copy in halo_copies:
            copy.wait_recv()
        before = jnp.where(me == 0, 0.0, halo[0])
        after = jnp.where(me == NDEV - 1, 0.0, halo[1])
        source = cat([charge[...], before, after], 0).astype(BF16)
        spot = place(iota((128, 144), 1)) - iota((128, 144), 0)
        for k in range(4):
            pick = jnp.where(spot == column(offset_ref[k:k + 1, :]), one, zero).astype(BF16)
            xs[pl.ds(k, 128, stride=4), :] = dot(pick, source)
        pltpu.make_async_copy(near_mat, near_mat, near_sem).wait()
        acc[...] = jnp.zeros((512, 128), F32)

    def near_products(begin, end):
        def body(c, carry):
            col = pl.ds(pl.multiple_of(c * 256, 256), 256)
            gather = jnp.where(
                iota((256, 128), 1) % 64 == c * 4 + iota((256, 128), 0) // 64, one, zero
            ).astype(BF16)
            for r in range(4):
                row = pl.ds(128 * r, 128)
                x = xs[row, :]
                hi, lo = split(near_mat[row, col].astype(F32) * cat([x, x], 1))
                acc[row, :] = acc[row, :] + (dot(hi, gather) + dot(lo, gather))
            return carry

        lax.fori_loop(begin, end, body, 0)

    def near_adjoint():
        for k in range(4):
            xs[pl.ds(k, 128, stride=4), :] = val[...]
        acc[...] = jnp.zeros((512, 128), F32)

        def body(c, carry):
            col = pl.ds(pl.multiple_of(c * 256, 256), 256)
            spread = jnp.where(
                iota((128, 256), 0) == c * 4 + iota((128, 256), 1) // 64, one, zero
            ).astype(BF16)
            for r in range(4):
                row = pl.ds(128 * r, 128)
                p = near_mat[row, col].astype(F32) * dot(xs[row, :].astype(BF16), spread)
                acc[row, :] = acc[row, :] + (p[:, :128] + p[:, 128:])
            return carry

        lax.fori_loop(0, 16, body, 0)

    def near_scatter():
        acc[...] = acc[...] + pltpu.roll(acc[...], 64, 1)
        total = jnp.zeros((144, 128), F32)
        spot = place(iota((144, 128), 0)) - iota((144, 128), 1)
        for k in range(4):
            pick = jnp.where(spot == offset_ref[k:k + 1, :], one, zero).astype(BF16)
            hi, lo = split(acc[pl.ds(k, 128, stride=4), :])
            total = total + (dot(pick, hi) + dot(pick, lo))
        ext[...] = total
        for copy in rim_copies:
            copy.start()

    def back_table():
        idm = get_row(4, 2)
        for k in range(2):
            xs[pl.ds(k, 128, stride=2), :] = jnp.broadcast_to(
                idm[:, k:k + 1].astype(F32), (128, 128)
            )
        ordered = xs[:256, :1].astype(jnp.int32)
        for tr in range(2):
            pick = jnp.where(
                ordered == iota((256, 256), 1) + (tr * 256 + 1), one, zero
            ).astype(BF16)
            for t in range(2):
                wi[t, :, tr * 256:(tr + 1) * 256] = dot_nt(pick, mats[t]).astype(BF16)

    def turn_stencil():
        eye = jnp.where(iota((256, 256), 0) == iota((256, 256), 1), one, zero).astype(BF16)

        def body(g, carry):
            at = pl.multiple_of(g * 512, 512)
            turned[:, pl.ds(at, 512)] = dot_nt(eye, stencil[pl.ds(at, 512), :]).astype(BF16)
            return carry

        lax.fori_loop(0, 16, body, 0)

    def pack(kk, carry):
        def code(at):
            x = green_ref[:, pl.ds(pl.multiple_of(at * LANES, LANES), LANES)]
            return (x * GREEN_UNIT + 0.5).astype(jnp.int32)

        gsend[pl.ds(kk, 32, stride=16), :] = (code(kk + 16) << 16) | code(kk)
        return carry

    def green_copies():
        k2 = me // 8

        def body(j, carry):
            k1 = (me % 8) * 32 + j
            low = jnp.where(k1 < 128, 1, 0)
            is_mid = jnp.where(k1 == 128, 1, 0)
            is_zero = jnp.where(k1 == 0, 1, 0)
            high = 1 - low - is_mid
            target_dev = low * k1 + high * (256 - k1)
            upper = k2 // 8
            beyond = jnp.where(k2 > 8, 1, 0)
            slot_zero = (1 - upper) * k2 + upper * (1 - beyond) * 16 + beyond * (32 - k2)
            slot_mid = (1 - upper) * (8 + k2) + upper * (39 - k2)
            slot = (low - is_zero) * k2 + is_zero * slot_zero + is_mid * slot_mid + high * (31 - k2)
            src = gsend.at[pl.ds(pl.multiple_of(j * 16, 16), 16)]
            dst = grecv.at[pl.ds(pl.multiple_of(slot * 16, 16), 16)]

            @pl.when(target_dev != me)
            def _():
                pltpu.make_async_remote_copy(
                    src_ref=src, dst_ref=dst, send_sem=gsend_sem.at[j], recv_sem=grecv_sem,
                    device_id=(target_dev // SLABS, target_dev % SLABS), device_id_type=MESH,
                ).start()

            @pl.when(target_dev == me)
            def _():
                pltpu.make_async_copy(src, dst, grecv_sem).start()

            return carry

        lax.fori_loop(0, 32, body, 0)

    def green_sent():
        def body(j, carry):
            k1 = (me % 8) * 32 + j
            low = jnp.where(k1 < 128, 1, 0)
            high = jnp.where(k1 > 128, 1, 0)
            target_dev = low * k1 + high * (256 - k1)

            @pl.when(target_dev != me)
            def _():
                part = pl.ds(pl.multiple_of(j * 16, 16), 16)
                pltpu.make_async_copy(gsend.at[part], grecv.at[part], gsend_sem.at[j]).wait()

            return carry

        lax.fori_loop(0, 32, body, 0)

    def green_ready():
        pltpu.make_async_copy(gsend, grecv, grecv_sem).wait()
        scale = 2.0 ** -24 / GREEN_UNIT
        flip = jnp.where((rows128 + lanes128 == 128) & (rows128 > 0), one, zero).astype(BF16)
        first = jnp.where((rows128 == 0) & (lanes128 == 0), one, zero).astype(BF16)
        eye = jnp.where(rows128 == lanes128, one, zero).astype(BF16)
        turn = cat([flip, first], 1)
        special = every16 & (me == 0)

        def rows_of(base, kappa):
            rows = []
            for n in range(8):
                k = kappa(n)
                words = grecv[pl.ds(base * 16 + k % 16, 16, stride=16), :]
                rows.append(((words >> 16 if k >= 16 else words) & 65535).astype(F32))
            return cat(rows, 0)

        nyquist = []

        for m in range(4):
            def plain(base):
                hi, lo = split(rows_of(base, lambda n: m + 4 * n))
                return dot_nt(eye, hi) + dot_nt(eye, lo)

            def turned(base):
                one_ = rows_of(base, lambda n: 31 - m - 4 * n)
                two_ = rows_of(base, lambda n: (32 - m - 4 * n) % 32)
                hi, lo = split(cat([one_, two_], 1))
                return dot_nt(turn, hi) + dot_nt(turn, lo)

            d, dr, o, orr = plain(0), turned(0), plain(16), turned(16)
            ga[:, m * LANES:(m + 1) * LANES] = (d + jnp.where(special, dr, orr)) * scale
            nyquist.append((o + orr) * scale)
        gb5[...] = squeeze(nyquist)

    lane64 = iota((128, 128), 1) // 64
    row16 = iota((128, 128), 0) % 16

    def project():
        v = val[...]
        spread = cat(
            [jnp.where(lane64 + 2 * i == row16, v, 0.0).astype(BF16) for i in range(8)], 1
        )
        for g in range(8):
            part = stencil[g * 1024:(g + 1) * 1024, :]
            tv[g * 16:(g + 1) * 16, :] = dot(spread[g * 16:(g + 1) * 16, :], part)
        hi, lo = split(tv[...])
        return dot(out_pick, hi) + dot(out_pick, lo)

    def interpolate(own_tiles):
        rows = []
        l64, r16 = iota((16, 128), 1) // 64, iota((16, 128), 0)
        for g in range(8):
            r = dot(own_tiles[g * 16:(g + 1) * 16, :], turned[:, g * 1024:(g + 1) * 1024])
            acc = jnp.zeros((16, 128), F32)
            for i in range(8):
                acc = acc + jnp.where(l64 + 2 * i == r16, r[:, i * LANES:(i + 1) * LANES], 0.0)
            rows.append(acc)
        far = cat(rows, 0)
        return far + pltpu.roll(far, 64, 1)

    def cmul(re, im, c, s):
        return re * c + im * s, im * c - re * s

    def cmul_conj(re, im, c, s):
        return re * c - im * s, im * c + re * s

    def lane_tile(x, j):
        return x[:, j * LANES:(j + 1) * LANES]

    head = iota((8, 128), 0) == 0

    def special_rows(parts, slot, outs):
        small = dot3(split(cat([p[:8] for p in parts], 0)), mat(slot))
        fixed = []
        for j in range(4):
            out = outs[j]
            h2 = iota((8, 256), 0) == 0
            fixed.append(cat([jnp.where(h2, small[8 * j:8 * j + 8], out[:8]), out[8:]], 0))
        return fixed

    def evaluate(which):
        step0 = which * 4
        first, last = which == 0, which == 1
        fwd, inv_ = which * 2, which * 2 + 1
        out = project()
        coded = encode_pairs(
            [[lane_tile(out[128 * k:128 * k + 128], h) for h in range(2)] for k in range(2)]
        )
        for k in range(2):
            put_row(4 + which, k, coded[k])

        @pl.when(first)
        def _():
            put_row(4, 2, id_rows.astype(jnp.int32))
            pl.semaphore_wait(barrier, NDEV - 1)
            exchange(0, swords.at[4], rwords.at[4], 4, 3)
            for copy in halo_copies:
                copy.start()
            loads["green"].wait()
            lax.fori_loop(0, 16, pack, 0)
            green_copies()
            lax.fori_loop(0, BLOCKS, near_load, 0)
            loads["table"].wait()
            split_tables()
            loads["target"].wait()
            unfold(target_ref, goal)
            arrived(0, swords.at[4], rwords.at[4], 3)
            idm = get_row(4, 2)
            tc = iota((128, 256), 1)
            for tr in range(2):
                pick = cat(
                    [
                        jnp.where(idm[:, k:k + 1] == tc + (tr * 256 + 1), one, zero)
                        for k in range(2)
                    ],
                    0,
                ).astype(BF16)
                for t in range(2):
                    wf[2 * tr + t] = dot_nt(mats[t], pick).astype(BF16)

        @pl.when(last)
        def _():
            exchange(4, swords.at[5], rwords.at[5], 4, 2)
            near_adjoint()
            arrived(4, swords.at[5], rwords.at[5], 2)

        values = decode_pairs([get_row(4 + which, k) for k in range(2)])
        tiles = split(cat([cat(v, 1) for v in values], 0))
        c2, s2 = half_at("t2", 0), half_at("t2", 1)
        c1 = cat([rows_at("c0"), rows_at("c1")], 1)
        s1 = cat([rows_at("s0"), rows_at("s1")], 1)
        parts = []
        for tr in range(2):
            y = dot3((wf[2 * tr], wf[2 * tr + 1]), tiles)
            for h in range(2):
                re, im = cmul(lane_tile(y[:128], h), lane_tile(y[128:], h), c2, s2)
                parts.append(cat([re, im], 1))
        prod = dot3(split(cat(parts, 0)), mat(1))
        outs = special_rows(parts, 3, [prod[128 * j:128 * j + 128] for j in range(4)])
        put_words(fwd, [o[:, :LANES] for o in outs], [o[:, LANES:] for o in outs])
        exchange(step0 + 1, swords.at[fwd], rwords.at[fwd], 4, 4)

        @pl.when(first)
        def _():
            green_ready()
            back_table()
            turn_stencil()

        @pl.when(last)
        def _():
            near_scatter()

        arrived(step0 + 1, swords.at[fwd], rwords.at[fwd], 4)
        re, im = get_words(fwd)
        y = dot3(mat(5), split(cat([cat(re, 1), cat(im, 1)], 0)))
        re, im = cmul(y[:128], y[128:], c1, s1)
        r = [lane_tile(re, j) for j in range(4)]
        i = [lane_tile(im, j) for j in range(4)]
        er, ei, dr, di = r[0] + r[2], i[0] + i[2], r[0] - r[2], i[0] - i[2]
        fr, fi, hr, hi_ = r[1] + r[3], i[1] + i[3], r[1] - r[3], i[1] - i[3]
        vs = [(er + fr, ei + fi), (dr + hi_, di - hr), (er - fr, ei - fi), (dr - hi_, di + hr)]
        spectrum = [dot3(split(cat(list(vs[m]), 1)), mat(7 + m)) for m in range(4)]
        vs = []
        for m in range(4):
            gm = ga[:, m * LANES:(m + 1) * LANES]
            p = dot3(split(spectrum[m] * cat([gm, gm], 1)), mat(11 + m))
            vs.append((p[:, :LANES], p[:, LANES:]))
        r = [v[0] for v in vs]
        i = [v[1] for v in vs]
        er, ei, dr, di = r[0] + r[2], i[0] + i[2], r[0] - r[2], i[0] - i[2]
        fr, fi, hr, hi_ = r[1] + r[3], i[1] + i[3], r[1] - r[3], i[1] - i[3]
        zs = [(er + fr, ei + fi), (dr - hi_, di + hr), (er - fr, ei - fi), (dr + hi_, di - hr)]
        re, im = cmul_conj(cat([z[0] for z in zs], 1), cat([z[1] for z in zs], 1), c1, s1)
        y = dot3(mat(6), split(cat([re, im], 0)))
        g5 = gb5[...]
        p = dot3(
            split(cat([squeeze([f[:, :LANES] for f in spectrum]) * g5,
                       squeeze([f[:, LANES:] for f in spectrum]) * g5], 1)),
            mat(15),
        )
        re, im = cmul_conj(p[:, :LANES], p[:, LANES:], t5[:, :LANES], t5[:, LANES:])
        y5 = dot3((mats[12, 128:, :], mats[13, 128:, :]), split(cat([re, im], 0)))
        here = every16 & (me == 0)
        yr = [lane_tile(y[:128], j) for j in range(4)]
        yi = [
            jnp.where(here, pltpu.roll(y5, LANES - j, 1) if j else y5, lane_tile(y[128:], j))
            for j in range(4)
        ]
        put_words(inv_, yr, yi)
        exchange(step0 + 2, swords.at[inv_], rwords.at[inv_], 4, 4)

        @pl.when(first)
        def _():
            near_forward()
            near_products(0, 9)

        arrived(step0 + 2, swords.at[inv_], rwords.at[inv_], 4)
        re, im = get_words(inv_)
        parts = [cat([re[j], im[j]], 1) for j in range(4)]
        prod = dot3(split(cat(parts, 0)), mat(2))
        outs = special_rows(parts, 4, [prod[128 * j:128 * j + 128] for j in range(4)])
        zs = [cmul_conj(o[:, :LANES], o[:, LANES:], c2, s2) for o in outs]
        y = cat(
            [
                cat([cat([zs[2 * tr][0], zs[2 * tr + 1][0]], 1), cat([zs[2 * tr][1], zs[2 * tr + 1][1]], 1)], 0)
                for tr in range(2)
            ],
            0,
        )
        back = dot3((wi[0], wi[1]), split(y))
        for h in range(2):
            order[pl.ds(h, 256, stride=2), :] = lane_tile(back, h)
        sback[which] = order[...].astype(BF16)
        exchange(step0 + 3, sback.at[which], rback.at[which], 4, 4)

        @pl.when(first)
        def _():
            near_products(9, 16)
            near[...] = sum(acc[pl.ds(k, 128, stride=4), :] for k in range(4))

        arrived(step0 + 3, sback.at[which], rback.at[which], 4)
        tiles = rback[which]
        far = interpolate(cat([dot(in_pick[h], tiles) for h in range(2)], 1).astype(BF16))

        @pl.when(first)
        def _():
            pot = far + near[...]
            val[...] = (pot - goal[...]).astype(BF16).astype(F32)
            fold(0, pot)

        @pl.when(last)
        def _():
            for copy in rim_copies:
                copy.wait_recv()
            before = jnp.where(me == 0, 0.0, rim[0])
            after = jnp.where(me == NDEV - 1, 0.0, rim[1])
            grad = far + ext[:BLOCKS, :]
            grad = cat(
                [grad[:REACH] + before, grad[REACH:BLOCKS - REACH], grad[BLOCKS - REACH:] + after], 0
            )
            fold(64, grad)

    loads["stencil"].wait()

    def both_passes(which, carry):
        evaluate(which)
        return carry

    lax.fori_loop(0, 2, both_passes, 0)
    for p in range(2):
        sent(4 * p, swords.at[4 + p], rwords.at[4 + p], 3 - p)
        sent(4 * p + 1, swords.at[2 * p], rwords.at[2 * p], 4)
        sent(4 * p + 2, swords.at[2 * p + 1], rwords.at[2 * p + 1], 4)
        sent(4 * p + 3, sback.at[p], rback.at[p], 4)
    green_sent()
    for copy in halo_copies + rim_copies:
        copy.wait_send()


def local(table, charges, target, stencil, near_matrix, green, block_dest, block_tile, near_offset):
    out = pl.pallas_call(
        kernel,
        out_shape=jax.ShapeDtypeStruct((128, LANES), F32),
        in_specs=[pl.BlockSpec(memory_space=pl.ANY)] * 9,
        out_specs=pl.BlockSpec(memory_space=pltpu.VMEM),
        scratch_shapes=[
            pltpu.VMEM((64, LANES), BF16),
            pltpu.VMEM((64, LANES), F32),
            pltpu.VMEM((32, GRID), F32),
            pltpu.VMEM((1, LANES), jnp.int32),
            pltpu.VMEM((1, LANES), jnp.int32),
            pltpu.VMEM((4, LANES), jnp.int32),
            pltpu.VMEM((TABLE_ROWS, 256), F32),
            pltpu.VMEM((BLOCKS * PANEL, CELLS), BF16),
            pltpu.VMEM((CELLS, BLOCKS * PANEL), BF16),
            pltpu.VMEM((4 * BLOCKS, PANEL * PANEL), BF16),
            pltpu.VMEM((2, 4 * NDEV, LANES), BF16),
            pltpu.VMEM((2, 4 * NDEV, LANES), BF16),
            pltpu.VMEM((6, 4 * NDEV, LANES), jnp.int32),
            pltpu.VMEM((6, 4 * NDEV, LANES), jnp.int32),
            pltpu.VMEM((512, LANES), jnp.int32),
            pltpu.VMEM((512, LANES), jnp.int32),
            pltpu.VMEM((128, 512), F32),
            pltpu.VMEM((128, LANES), F32),
            pltpu.VMEM((128, 256), F32),
            pltpu.VMEM((128, 128), F32),
            pltpu.VMEM((128, 128), F32),
            pltpu.VMEM((128, 128), F32),
            pltpu.VMEM((128, 256), F32),
            pltpu.VMEM((4, 256, 256), BF16),
            pltpu.VMEM((2, 256, 512), BF16),
            pltpu.VMEM((32, 256, 256), BF16),
            pltpu.VMEM((512, LANES), F32),
            pltpu.VMEM((512, LANES), F32),
            pltpu.VMEM((512, LANES), F32),
            pltpu.VMEM((128, LANES), F32),
            pltpu.VMEM((144, LANES), F32),
            pltpu.VMEM((2, REACH, LANES), F32),
            pltpu.VMEM((2, REACH, LANES), F32),
            pltpu.SemaphoreType.DMA((8,)),
            pltpu.SemaphoreType.DMA((8,)),
            pltpu.SemaphoreType.DMA((32,)),
            pltpu.SemaphoreType.DMA,
            pltpu.SemaphoreType.DMA((8,)),
            pltpu.SemaphoreType.DMA,
            pltpu.SemaphoreType.DMA((4,)),
            pltpu.SemaphoreType.DMA((4,)),
        ],
        compiler_params=pltpu.CompilerParams(collective_id=0, has_side_effects=True),
        name="panel_solver",
    )(
        charges.reshape(64, LANES), target.reshape(64, LANES),
        stencil.reshape(BLOCKS * PANEL, CELLS), near_matrix, green.T,
        block_dest.reshape(1, BLOCKS), block_tile.reshape(1, BLOCKS), near_offset.T, table,
    )
    return (out[:64].reshape(-1), out[64:].reshape(-1))


def solution(mesh):
    table = jnp.asarray(make_tables())
    return jax.shard_map(
        functools.partial(local, table),
        mesh=mesh,
        in_specs=(
            P(("panel", "slab")),
            P(("panel", "slab")),
            P(("panel", "slab"), None, None),
            P(("panel", "slab"), None, None),
            P(None, ("panel", "slab")),
            P(("panel", "slab"), None),
            P(("panel", "slab")),
            P(("panel", "slab"), None),
        ),
        out_specs=(P(("panel", "slab")), P(("panel", "slab"))),
        check_vma=False,
    )
```

```python
import functools
import math

import jax
import jax.numpy as jnp
import numpy as np
from jax import lax
from jax.experimental import pallas as pl
from jax.experimental.pallas import tpu as pltpu
from jax.sharding import PartitionSpec as P

GRID = 4096
TILE = 16
REACH = 8
NDEV = 128
SLABS = 4
BLOCKS = 128
PANEL = 64
CELLS = 256
LANES = 128
GREEN_UNIT = 8191.0
MESH = pl.DeviceIdType.MESH
F32 = jnp.float32
BF16 = jnp.bfloat16
TABLES = (("w1", 256), ("m0", 256), ("m0i", 256), ("w2", 128), ("a1", 128), ("w3", 512), ("w5", 128), ("t2", 128),
          ("c0", 128), ("c1", 128), ("s0", 128), ("s1", 128))
START = {name: sum(n for _, n in TABLES[:i]) for i, (name, _) in enumerate(TABLES)}
TABLE_ROWS = sum(n for _, n in TABLES)


def make_tables():
    def angle(rows, cols, modulus):
        return 2.0 * math.pi / modulus * ((np.outer(rows, cols)) % modulus)

    out = {}
    th = angle(np.arange(128), np.arange(256), 256)
    w1 = np.concatenate([np.cos(th), -np.sin(th)], 0)
    w1[128] = (-1.0) ** np.arange(256)
    out["w1"] = w1
    th = angle(np.arange(16), np.arange(16), 16)
    c, s = np.kron(np.eye(8), np.cos(th)), np.kron(np.eye(8), np.sin(th))
    out["w2"] = np.concatenate([c, s], 1)
    m0 = np.zeros((2, 16, 2, 16))
    idx = np.arange(16)
    m0[0, :, 0, 0] = 1.0
    m0[0, :, 1, 0] = (-1.0) ** idx
    for k in range(1, 8):
        t = 2 * math.pi * ((idx * k) % 16) / 16
        m0[0, :, 0, k], m0[0, :, 1, k] = np.cos(t), -np.sin(t)
    for n in range(8):
        t = 2 * math.pi * ((idx * (1 + 2 * n)) % 32) / 32
        m0[1, :, 0, 8 + n], m0[1, :, 1, 8 + n] = np.cos(t), -np.sin(t)
    big = np.zeros((2, 8, 16, 2, 8, 16))
    for a in range(8):
        big[:, a, :, :, a, :] = m0
    out["m0"] = big.reshape(256, 256)
    inv = m0.copy()
    inv[:, :, :, 0] *= 0.5
    big = np.zeros((2, 8, 16, 2, 8, 16))
    for a in range(8):
        big[:, a, :, :, a, :] = inv
    out["m0i"] = big.reshape(256, 256).T
    th = angle(np.arange(128), np.arange(128), 128)
    out["a1"] = np.concatenate([np.cos(th), np.sin(th)], 1)
    parts = []
    for m in range(4):
        th = angle(np.arange(8), m + 4 * np.arange(8), 32)
        parts.append(
            np.concatenate([np.kron(np.cos(th), np.eye(16)), np.kron(np.sin(th), np.eye(16))], 1)
        )
    out["w3"] = np.concatenate(parts, 0)
    w5 = np.zeros((2, 8, 16, 8, 16))
    for m in range(4):
        for j in range(4):
            th = angle(m + 4 * np.arange(8), 8 * j + np.arange(8), 32)
            w5[0, :, m, :, j], w5[1, :, m, :, j] = np.cos(th), np.sin(th)
    out["w5"] = np.concatenate([w5[0].reshape(128, 128), w5[1].reshape(128, 128)], 1)
    th = np.tile(angle(np.arange(128), np.arange(16), GRID), (1, 8))
    th[0] = 0.0
    out["t2"] = np.concatenate([np.cos(th), np.sin(th)], 1)
    th = np.repeat(angle(np.arange(128), np.arange(32), GRID), 16, axis=1)
    out["c0"], out["c1"] = np.cos(th[:, :256]), np.cos(th[:, 256:])
    out["s0"], out["s1"] = np.sin(th[:, :256]), np.sin(th[:, 256:])
    return np.concatenate([out[name] for name, _ in TABLES], 0).astype(np.float32)


def dot(a, b):
    return lax.dot_general(a, b, (((1,), (0,)), ((), ())), preferred_element_type=F32)


def dot_nt(a, b):
    return lax.dot_general(a, b, (((1,), (1,)), ((), ())), preferred_element_type=F32)


def split(x):
    hi = x.astype(BF16)
    return hi, (x - hi.astype(F32)).astype(BF16)


def dot3(a, b):
    n = a[0].shape[0]
    both = dot(jnp.concatenate(a, 0), b[0])
    return both[:n] + (both[n:] + dot(a[0], b[1]))


def iota(shape, dim):
    return lax.broadcasted_iota(jnp.int32, shape, dim)


def cat(parts, axis):
    return jnp.concatenate(parts, axis=axis)


COMBOS = sorted(
    ((dz, dx) for dz in range(4) for dx in range(4)),
    key=lambda c: -(min(c[0], 4 - c[0]) + min(c[1], 4 - c[1])),
)
Z_DIGITS = sum(c[0] << (2 * i) for i, c in enumerate(COMBOS))
X_DIGITS = sum(c[1] << (2 * i) for i, c in enumerate(COMBOS))


def encode(re, im):
    top = jnp.abs(re[0])
    for x in list(re[1:]) + list(im):
        top = jnp.maximum(top, jnp.abs(x))
    top = jnp.maximum(top, 2.0 ** -100)
    power = jnp.floor(jnp.log2(top)) + 1.0
    scale = jnp.exp2(14.0 - power)
    code = power.astype(jnp.int32) + 128

    def mantissa(x):
        return jnp.minimum(x * scale + 16384.5, 32767.5).astype(jnp.int32)

    return [
        (((code >> (2 * j)) & 3) << 30) | (mantissa(re[j]) << 15) | mantissa(im[j])
        for j in range(4)
    ]


def decode(words):
    code = words[0] >> 30 & 3
    for j in range(1, 4):
        code = code | ((words[j] >> 30 & 3) << (2 * j))
    scale = jnp.exp2(code.astype(F32) - 142.0)
    re = [((w >> 15 & 32767).astype(F32) - 16384.0) * scale for w in words]
    im = [((w & 32767).astype(F32) - 16384.0) * scale for w in words]
    return re, im


def encode_pairs(values):
    flat = [x for pair in values for x in pair]
    top = jnp.abs(flat[0])
    for x in flat[1:]:
        top = jnp.maximum(top, jnp.abs(x))
    power = jnp.floor(jnp.log2(jnp.maximum(top, 2.0 ** -100))) + 1.0
    scale = jnp.exp2(13.0 - power)
    code = power.astype(jnp.int32) + 128

    def mantissa(x):
        return jnp.minimum(x * scale + 8192.5, 16383.5).astype(jnp.int32)

    return [
        (((code >> (4 * k)) & 15) << 28) | (mantissa(a) << 14) | mantissa(b)
        for k, (a, b) in enumerate(values)
    ]


def decode_pairs(words):
    code = (words[0] >> 28 & 15) | ((words[1] >> 28 & 15) << 4)
    scale = jnp.exp2(code.astype(F32) - 141.0)
    return [
        [((w >> at & 16383).astype(F32) - 8192.0) * scale for at in (14, 0)] for w in words
    ]


def kernel(
    q_hbm, target_hbm, stencil_hbm, near_hbm, green_hbm, dest_hbm, tile_hbm, offset_hbm, table_hbm,
    out_ref,
    q_ref, target_ref, green_ref, dest_ref, tile_ref, offset_ref, table,
    stencil, turned, near_mat, sback, rback, swords, rwords, gsend, grecv, ga, gb5, t5, val, charge, goal, tv,
    wf, wi, mats, xs, order, acc, near, ext, halo, rim,
    send_sem, recv_sem, gsend_sem, grecv_sem, load_sem, near_sem, halo_sem, rim_sem,
):
    panel = lax.axis_index("panel")
    slab = lax.axis_index("slab")
    me = panel * SLABS + slab
    pz, px, pc = panel // 8, (panel // 2) % 4, panel % 2

    def rows_at(name):
        n = dict(TABLES)[name]
        return table[START[name]:START[name] + n, :]

    def half_at(name, half):
        n = dict(TABLES)[name]
        return table[START[name]:START[name] + n, half * LANES:(half + 1) * LANES]

    loads = {
        name: pltpu.make_async_copy(src, dst, load_sem.at[i])
        for i, (name, src, dst) in enumerate((
            ("q", q_hbm, q_ref), ("dest", dest_hbm, dest_ref), ("tile", tile_hbm, tile_ref),
            ("stencil", stencil_hbm, stencil), ("table", table_hbm, table),
            ("green", green_hbm, green_ref), ("offset", offset_hbm, offset_ref),
            ("target", target_hbm, target_ref),
        ))
    }
    for name in ("q", "dest", "tile", "stencil"):
        loads[name].start()

    def others(visit):
        def body(g, carry):
            z = (pz + ((Z_DIGITS >> (2 * g)) & 3)) % 4
            x = (px + ((X_DIGITS >> (2 * g)) & 3)) % 4
            for dy in (2, 1, 3, 0):
                for dc in (1, 0):
                    def go(z=z, x=x, dy=dy, dc=dc):
                        visit(z * 8 + x * 2 + (pc + dc) % 2, (slab + dy) % 4)

                    if dy == 0 and dc == 0:
                        pl.when(g != 15)(go)
                    else:
                        go()
            return carry

        lax.fori_loop(0, 16, body, 0)

    barrier = pltpu.get_barrier_semaphore()
    others(
        lambda p, y: pl.semaphore_signal(barrier, inc=1, device_id=(p, y), device_id_type=MESH)
    )

    for name in ("table", "green", "offset", "target"):
        loads[name].start()

    def near_load(b, carry):
        pltpu.make_async_copy(
            near_hbm.at[b], near_mat.at[pl.ds(pl.multiple_of(b * 4, 4), 4)], near_sem
        ).start()
        return carry

    rows128, lanes128 = iota((128, 128), 0), iota((128, 128), 1)

    def unfold(ref, out):
        x = ref[...].astype(F32)
        y = pltpu.roll(x, 64, 1)
        low = iota((64, 128), 1) < 64
        out[pl.ds(0, 64, stride=2), :] = jnp.where(low, x, y)
        out[pl.ds(1, 64, stride=2), :] = jnp.where(low, y, x)

    def fold(row, value):
        goal[...] = value
        low = iota((64, 128), 1) < 64
        out_ref[row:row + 64, :] = jnp.where(
            low, goal[pl.ds(0, 64, stride=2), :], goal[pl.ds(1, 64, stride=2), :]
        )

    loads["q"].wait()
    unfold(q_ref, charge)
    val[...] = charge[...]

    def pair(slot, value):
        hi, lo = split(value)
        mats[2 * slot] = hi
        mats[2 * slot + 1] = lo

    def mat(slot):
        return mats[2 * slot], mats[2 * slot + 1]

    every16 = lanes128 % 16 == 0

    def squeeze(tiles):
        total = jnp.where(every16, tiles[0], 0.0)
        for j in range(1, 4):
            total = total + pltpu.roll(jnp.where(every16, tiles[j], 0.0), j, 1)
        return total

    def split_tables():
        def circle(name):
            return half_at(name, 0), half_at(name, 1)

        pair(0, rows_at("w1"))
        c, s = circle("w2")
        pair(1, cat([cat([c, -s], 1), cat([s, c], 1)], 0))
        pair(2, cat([cat([c, s], 1), cat([-s, c], 1)], 0))
        pair(3, rows_at("m0"))
        pair(4, rows_at("m0i"))
        c, s = circle("a1")
        pair(5, cat([cat([c, s], 1), cat([-s, c], 1)], 0))
        pair(6, cat([cat([c, -s], 1), cat([s, c], 1)], 0))
        for m in range(4):
            base = START["w3"] + 128 * m
            c, s = table[base:base + 128, :LANES], table[base:base + 128, LANES:]
            pair(7 + m, cat([cat([c, -s], 1), cat([s, c], 1)], 0))
            c, s = c.T, s.T
            pair(11 + m, cat([cat([c, s], 1), cat([-s, c], 1)], 0))
        c, s = circle("w5")
        pair(15, cat([cat([c, s], 1), cat([-s, c], 1)], 0))
        t5[:, :LANES] = squeeze([half_at("c%d" % (j // 2), j % 2) for j in range(4)])
        t5[:, LANES:] = squeeze([half_at("s%d" % (j // 2), j % 2) for j in range(4)])

    loads["dest"].wait()
    loads["tile"].wait()
    dest_row = dest_ref[...]
    tile_row = tile_ref[...]

    def column(row):
        return jnp.sum(jnp.where(rows128 == lanes128, row, 0), axis=1, keepdims=True)

    dest_col = column(dest_row)
    same = dest_col == dest_row
    rank_row = jnp.sum(jnp.where(same & (rows128 < lanes128), 1, 0), axis=0, keepdims=True)
    rank_col = jnp.sum(jnp.where(same & (lanes128 < rows128), 1, 0), axis=1, keepdims=True)
    one, zero = F32(1.0), F32(0.0)
    out_pick = cat(
        [jnp.where((dest_row == rows128) & (rank_row == k), one, zero) for k in range(2)], 0
    )
    wanted = iota((128, 512), 1) - 4 * dest_col - 2 * rank_col
    in_pick = [jnp.where(wanted == h, one, zero).astype(BF16) for h in range(2)]
    ids = jnp.sum(out_pick * (tile_row + 1).astype(F32), axis=1, keepdims=True)
    id_rows = jnp.where(lanes128 == 0, ids[:128], jnp.where(lanes128 == 1, ids[128:], 0.0))
    out_pick = out_pick.astype(BF16)

    def exchange(step, src, dst, stride, count):
        mine = pl.ds(pl.multiple_of(me * stride, stride), count)

        def send(p, y):
            theirs = pl.ds(pl.multiple_of((p * SLABS + y) * stride, stride), count)
            pltpu.make_async_remote_copy(
                src_ref=src.at[theirs],
                dst_ref=dst.at[mine],
                send_sem=send_sem.at[step],
                recv_sem=recv_sem.at[step],
                device_id=(p, y),
                device_id_type=MESH,
            ).start()

        others(send)
        pltpu.make_async_copy(src.at[mine], dst.at[mine], recv_sem.at[step]).start()

    def arrived(step, src, dst, count):
        part = pl.ds(0, NDEV * count)
        pltpu.make_async_copy(src.at[part], dst.at[part], recv_sem.at[step]).wait()

    def sent(step, src, dst, count):
        part = pl.ds(0, (NDEV - 1) * count)
        pltpu.make_async_copy(src.at[part], dst.at[part], send_sem.at[step]).wait()

    def pass_sent(p):
        sent(4 * p, swords.at[4 + p], rwords.at[4 + p], 3 - p)
        sent(4 * p + 1, swords.at[2 * p], rwords.at[2 * p], 4)
        sent(4 * p + 2, swords.at[2 * p + 1], rwords.at[2 * p + 1], 4)
        sent(4 * p + 3, sback.at[p], rback.at[p], 4)

    def put_row(slot, row, value):
        swords[slot, pl.ds(row, NDEV, stride=4), :] = value

    def get_row(slot, row):
        return rwords[slot, pl.ds(row, NDEV, stride=4), :]

    def put_words(slot, re, im):
        for j, w in enumerate(encode(re, im)):
            put_row(slot, j, w)

    def get_words(slot):
        return decode([get_row(slot, j) for j in range(4)])

    def next_to(shift):
        other = (me + shift + NDEV) % NDEV
        return (other // SLABS, other % SLABS)

    def edge_copies(src, rows_prev, rows_next, dst, sem):
        for way, (shift, rows) in enumerate(((-1, rows_prev), (1, rows_next))):
            yield pltpu.make_async_remote_copy(
                src_ref=src.at[pl.ds(rows, REACH)],
                dst_ref=dst.at[1 - way],
                send_sem=sem.at[way],
                recv_sem=sem.at[3 - way],
                device_id=next_to(shift),
                device_id_type=MESH,
            )

    halo_copies = list(edge_copies(charge, 0, BLOCKS - REACH, halo, halo_sem))
    rim_copies = list(edge_copies(ext, BLOCKS, BLOCKS + REACH, rim, rim_sem))

    def place(index):
        return jnp.where(index < 128, index, jnp.where(index < 136, index - 136, index - 8))

    def near_forward():
        loads["offset"].wait()
        for copy in halo_copies:
            copy.wait_recv()
        before = jnp.where(me == 0, 0.0, halo[0])
        after = jnp.where(me == NDEV - 1, 0.0, halo[1])
        source = cat([charge[...], before, after], 0).astype(BF16)
        spot = place(iota((128, 144), 1)) - iota((128, 144), 0)
        for k in range(4):
            pick = jnp.where(spot == column(offset_ref[k:k + 1, :]), one, zero).astype(BF16)
            xs[pl.ds(k, 128, stride=4), :] = dot(pick, source)
        pltpu.make_async_copy(near_mat, near_mat, near_sem).wait()
        acc[...] = jnp.zeros((512, 128), F32)

    def near_products(begin, end):
        def body(c, carry):
            col = pl.ds(pl.multiple_of(c * 256, 256), 256)
            gather = jnp.where(
                iota((256, 128), 1) % 64 == c * 4 + iota((256, 128), 0) // 64, one, zero
            ).astype(BF16)
            for r in range(4):
                row = pl.ds(128 * r, 128)
                x = xs[row, :]
                hi, lo = split(near_mat[row, col].astype(F32) * cat([x, x], 1))
                acc[row, :] = acc[row, :] + (dot(hi, gather) + dot(lo, gather))
            return carry

        lax.fori_loop(begin, end, body, 0)

    def near_adjoint():
        for k in range(4):
            xs[pl.ds(k, 128, stride=4), :] = val[...]
        acc[...] = jnp.zeros((512, 128), F32)

        def body(c, carry):
            col = pl.ds(pl.multiple_of(c * 256, 256), 256)
            spread = jnp.where(
                iota((128, 256), 0) == c * 4 + iota((128, 256), 1) // 64, one, zero
            ).astype(BF16)
            for r in range(4):
                row = pl.ds(128 * r, 128)
                p = near_mat[row, col].astype(F32) * dot(xs[row, :].astype(BF16), spread)
                acc[row, :] = acc[row, :] + (p[:, :128] + p[:, 128:])
            return carry

        lax.fori_loop(0, 16, body, 0)

    def near_scatter():
        acc[...] = acc[...] + pltpu.roll(acc[...], 64, 1)
        total = jnp.zeros((144, 128), F32)
        spot = place(iota((144, 128), 0)) - iota((144, 128), 1)
        for k in range(4):
            pick = jnp.where(spot == offset_ref[k:k + 1, :], one, zero).astype(BF16)
            hi, lo = split(acc[pl.ds(k, 128, stride=4), :])
            total = total + (dot(pick, hi) + dot(pick, lo))
        ext[...] = total
        for copy in rim_copies:
            copy.start()

    def back_table():
        idm = get_row(4, 2)
        for k in range(2):
            xs[pl.ds(k, 128, stride=2), :] = jnp.broadcast_to(
                idm[:, k:k + 1].astype(F32), (128, 128)
            )
        ordered = xs[:256, :1].astype(jnp.int32)
        for tr in range(2):
            pick = jnp.where(
                ordered == iota((256, 256), 1) + (tr * 256 + 1), one, zero
            ).astype(BF16)
            for t in range(2):
                wi[t, :, tr * 256:(tr + 1) * 256] = dot_nt(pick, mats[t]).astype(BF16)

    def turn_stencil():
        eye = jnp.where(iota((256, 256), 0) == iota((256, 256), 1), one, zero).astype(BF16)

        def body(g, carry):
            at = pl.multiple_of(g * 512, 512)
            turned[:, pl.ds(at, 512)] = dot_nt(eye, stencil[pl.ds(at, 512), :]).astype(BF16)
            return carry

        lax.fori_loop(0, 16, body, 0)

    def pack(kk, carry):
        def code(at):
            x = green_ref[:, pl.ds(pl.multiple_of(at * LANES, LANES), LANES)]
            return (x * GREEN_UNIT + 0.5).astype(jnp.int32)

        gsend[pl.ds(kk, 32, stride=16), :] = (code(kk + 16) << 16) | code(kk)
        return carry

    def green_copies():
        k2 = me // 8

        def body(j, carry):
            k1 = (me % 8) * 32 + j
            low = jnp.where(k1 < 128, 1, 0)
            is_mid = jnp.where(k1 == 128, 1, 0)
            is_zero = jnp.where(k1 == 0, 1, 0)
            high = 1 - low - is_mid
            target_dev = low * k1 + high * (256 - k1)
            upper = k2 // 8
            beyond = jnp.where(k2 > 8, 1, 0)
            slot_zero = (1 - upper) * k2 + upper * (1 - beyond) * 16 + beyond * (32 - k2)
            slot_mid = (1 - upper) * (8 + k2) + upper * (39 - k2)
            slot = (low - is_zero) * k2 + is_zero * slot_zero + is_mid * slot_mid + high * (31 - k2)
            src = gsend.at[pl.ds(pl.multiple_of(j * 16, 16), 16)]
            dst = grecv.at[pl.ds(pl.multiple_of(slot * 16, 16), 16)]

            @pl.when(target_dev != me)
            def _():
                pltpu.make_async_remote_copy(
                    src_ref=src, dst_ref=dst, send_sem=gsend_sem.at[j], recv_sem=grecv_sem,
                    device_id=(target_dev // SLABS, target_dev % SLABS), device_id_type=MESH,
                ).start()

            @pl.when(target_dev == me)
            def _():
                pltpu.make_async_copy(src, dst, grecv_sem).start()

            return carry

        lax.fori_loop(0, 32, body, 0)

    def green_sent():
        def body(j, carry):
            k1 = (me % 8) * 32 + j
            low = jnp.where(k1 < 128, 1, 0)
            high = jnp.where(k1 > 128, 1, 0)
            target_dev = low * k1 + high * (256 - k1)

            @pl.when(target_dev != me)
            def _():
                part = pl.ds(pl.multiple_of(j * 16, 16), 16)
                pltpu.make_async_copy(gsend.at[part], grecv.at[part], gsend_sem.at[j]).wait()

            return carry

        lax.fori_loop(0, 32, body, 0)

    def green_ready():
        pltpu.make_async_copy(gsend, grecv, grecv_sem).wait()
        scale = 2.0 ** -24 / GREEN_UNIT
        flip = jnp.where((rows128 + lanes128 == 128) & (rows128 > 0), one, zero).astype(BF16)
        first = jnp.where((rows128 == 0) & (lanes128 == 0), one, zero).astype(BF16)
        eye = jnp.where(rows128 == lanes128, one, zero).astype(BF16)
        turn = cat([flip, first], 1)
        special = every16 & (me == 0)

        def rows_of(base, kappa):
            rows = []
            for n in range(8):
                k = kappa(n)
                words = grecv[pl.ds(base * 16 + k % 16, 16, stride=16), :]
                rows.append(((words >> 16 if k >= 16 else words) & 65535).astype(F32))
            return cat(rows, 0)

        nyquist = []

        for m in range(4):
            def plain(base):
                hi, lo = split(rows_of(base, lambda n: m + 4 * n))
                return dot_nt(eye, hi) + dot_nt(eye, lo)

            def turned(base):
                one_ = rows_of(base, lambda n: 31 - m - 4 * n)
                two_ = rows_of(base, lambda n: (32 - m - 4 * n) % 32)
                hi, lo = split(cat([one_, two_], 1))
                return dot_nt(turn, hi) + dot_nt(turn, lo)

            d, dr, o, orr = plain(0), turned(0), plain(16), turned(16)
            ga[:, m * LANES:(m + 1) * LANES] = (d + jnp.where(special, dr, orr)) * scale
            nyquist.append((o + orr) * scale)
        gb5[...] = squeeze(nyquist)

    lane64 = iota((128, 128), 1) // 64
    row16 = iota((128, 128), 0) % 16

    def project():
        v = val[...]
        spread = cat(
            [jnp.where(lane64 + 2 * i == row16, v, 0.0).astype(BF16) for i in range(8)], 1
        )
        for g in range(8):
            part = stencil[g * 1024:(g + 1) * 1024, :]
            tv[g * 16:(g + 1) * 16, :] = dot(spread[g * 16:(g + 1) * 16, :], part)
        hi, lo = split(tv[...])
        return dot(out_pick, hi) + dot(out_pick, lo)

    def interpolate(own_tiles):
        rows = []
        l64, r16 = iota((16, 128), 1) // 64, iota((16, 128), 0)
        for g in range(8):
            r = dot(own_tiles[g * 16:(g + 1) * 16, :], turned[:, g * 1024:(g + 1) * 1024])
            acc = jnp.zeros((16, 128), F32)
            for i in range(8):
                acc = acc + jnp.where(l64 + 2 * i == r16, r[:, i * LANES:(i + 1) * LANES], 0.0)
            rows.append(acc)
        far = cat(rows, 0)
        return far + pltpu.roll(far, 64, 1)

    def cmul(re, im, c, s):
        return re * c + im * s, im * c - re * s

    def cmul_conj(re, im, c, s):
        return re * c - im * s, im * c + re * s

    def lane_tile(x, j):
        return x[:, j * LANES:(j + 1) * LANES]

    head = iota((8, 128), 0) == 0

    def special_rows(parts, slot, outs):
        small = dot3(split(cat([p[:8] for p in parts], 0)), mat(slot))
        fixed = []
        for j in range(4):
            out = outs[j]
            h2 = iota((8, 256), 0) == 0
            fixed.append(cat([jnp.where(h2, small[8 * j:8 * j + 8], out[:8]), out[8:]], 0))
        return fixed

    def evaluate(which):
        step0 = which * 4
        first, last = which == 0, which == 1
        fwd, inv_ = which * 2, which * 2 + 1
        out = project()
        coded = encode_pairs(
            [[lane_tile(out[128 * k:128 * k + 128], h) for h in range(2)] for k in range(2)]
        )
        for k in range(2):
            put_row(4 + which, k, coded[k])

        @pl.when(first)
        def _():
            put_row(4, 2, id_rows.astype(jnp.int32))
            pl.semaphore_wait(barrier, NDEV - 1)
            exchange(0, swords.at[4], rwords.at[4], 4, 3)
            for copy in halo_copies:
                copy.start()
            loads["green"].wait()
            lax.fori_loop(0, 16, pack, 0)
            green_copies()
            lax.fori_loop(0, BLOCKS, near_load, 0)
            loads["table"].wait()
            split_tables()
            loads["target"].wait()
            unfold(target_ref, goal)
            arrived(0, swords.at[4], rwords.at[4], 3)
            idm = get_row(4, 2)
            tc = iota((128, 256), 1)
            for tr in range(2):
                pick = cat(
                    [
                        jnp.where(idm[:, k:k + 1] == tc + (tr * 256 + 1), one, zero)
                        for k in range(2)
                    ],
                    0,
                ).astype(BF16)
                for t in range(2):
                    wf[2 * tr + t] = dot_nt(mats[t], pick).astype(BF16)

        @pl.when(last)
        def _():
            exchange(4, swords.at[5], rwords.at[5], 4, 2)
            near_adjoint()
            arrived(4, swords.at[5], rwords.at[5], 2)

        values = decode_pairs([get_row(4 + which, k) for k in range(2)])
        tiles = split(cat([cat(v, 1) for v in values], 0))
        c2, s2 = half_at("t2", 0), half_at("t2", 1)
        c1 = cat([rows_at("c0"), rows_at("c1")], 1)
        s1 = cat([rows_at("s0"), rows_at("s1")], 1)
        parts = []
        for tr in range(2):
            y = dot3((wf[2 * tr], wf[2 * tr + 1]), tiles)
            for h in range(2):
                re, im = cmul(lane_tile(y[:128], h), lane_tile(y[128:], h), c2, s2)
                parts.append(cat([re, im], 1))
        prod = dot3(split(cat(parts, 0)), mat(1))
        outs = special_rows(parts, 3, [prod[128 * j:128 * j + 128] for j in range(4)])
        put_words(fwd, [o[:, :LANES] for o in outs], [o[:, LANES:] for o in outs])
        exchange(step0 + 1, swords.at[fwd], rwords.at[fwd], 4, 4)

        @pl.when(first)
        def _():
            green_ready()
            back_table()
            turn_stencil()

        @pl.when(last)
        def _():
            near_scatter()
            green_sent()
            pass_sent(0)
            for copy in halo_copies:
                copy.wait_send()

        arrived(step0 + 1, swords.at[fwd], rwords.at[fwd], 4)
        re, im = get_words(fwd)
        y = dot3(mat(5), split(cat([cat(re, 1), cat(im, 1)], 0)))
        re, im = cmul(y[:128], y[128:], c1, s1)
        r = [lane_tile(re, j) for j in range(4)]
        i = [lane_tile(im, j) for j in range(4)]
        er, ei, dr, di = r[0] + r[2], i[0] + i[2], r[0] - r[2], i[0] - i[2]
        fr, fi, hr, hi_ = r[1] + r[3], i[1] + i[3], r[1] - r[3], i[1] - i[3]
        vs = [(er + fr, ei + fi), (dr + hi_, di - hr), (er - fr, ei - fi), (dr - hi_, di + hr)]
        spectrum = [dot3(split(cat(list(vs[m]), 1)), mat(7 + m)) for m in range(4)]
        vs = []
        for m in range(4):
            gm = ga[:, m * LANES:(m + 1) * LANES]
            p = dot3(split(spectrum[m] * cat([gm, gm], 1)), mat(11 + m))
            vs.append((p[:, :LANES], p[:, LANES:]))
        r = [v[0] for v in vs]
        i = [v[1] for v in vs]
        er, ei, dr, di = r[0] + r[2], i[0] + i[2], r[0] - r[2], i[0] - i[2]
        fr, fi, hr, hi_ = r[1] + r[3], i[1] + i[3], r[1] - r[3], i[1] - i[3]
        zs = [(er + fr, ei + fi), (dr - hi_, di + hr), (er - fr, ei - fi), (dr + hi_, di - hr)]
        re, im = cmul_conj(cat([z[0] for z in zs], 1), cat([z[1] for z in zs], 1), c1, s1)
        y = dot3(mat(6), split(cat([re, im], 0)))
        g5 = gb5[...]
        p = dot3(
            split(cat([squeeze([f[:, :LANES] for f in spectrum]) * g5,
                       squeeze([f[:, LANES:] for f in spectrum]) * g5], 1)),
            mat(15),
        )
        re, im = cmul_conj(p[:, :LANES], p[:, LANES:], t5[:, :LANES], t5[:, LANES:])
        y5 = dot3((mats[12, 128:, :], mats[13, 128:, :]), split(cat([re, im], 0)))
        here = every16 & (me == 0)
        yr = [lane_tile(y[:128], j) for j in range(4)]
        yi = [
            jnp.where(here, pltpu.roll(y5, LANES - j, 1) if j else y5, lane_tile(y[128:], j))
            for j in range(4)
        ]
        put_words(inv_, yr, yi)
        exchange(step0 + 2, swords.at[inv_], rwords.at[inv_], 4, 4)

        @pl.when(first)
        def _():
            near_forward()
            near_products(0, 9)

        arrived(step0 + 2, swords.at[inv_], rwords.at[inv_], 4)
        re, im = get_words(inv_)
        parts = [cat([re[j], im[j]], 1) for j in range(4)]
        prod = dot3(split(cat(parts, 0)), mat(2))
        outs = special_rows(parts, 4, [prod[128 * j:128 * j + 128] for j in range(4)])
        zs = [cmul_conj(o[:, :LANES], o[:, LANES:], c2, s2) for o in outs]
        y = cat(
            [
                cat([cat([zs[2 * tr][0], zs[2 * tr + 1][0]], 1), cat([zs[2 * tr][1], zs[2 * tr + 1][1]], 1)], 0)
                for tr in range(2)
            ],
            0,
        )
        back = dot3((wi[0], wi[1]), split(y))
        for h in range(2):
            order[pl.ds(h, 256, stride=2), :] = lane_tile(back, h)
        sback[which] = order[...].astype(BF16)
        exchange(step0 + 3, sback.at[which], rback.at[which], 4, 4)

        @pl.when(first)
        def _():
            near_products(9, 16)
            near[...] = sum(acc[pl.ds(k, 128, stride=4), :] for k in range(4))

        arrived(step0 + 3, sback.at[which], rback.at[which], 4)
        tiles = rback[which]
        far = interpolate(cat([dot(in_pick[h], tiles) for h in range(2)], 1).astype(BF16))

        @pl.when(first)
        def _():
            pot = far + near[...]
            val[...] = (pot - goal[...]).astype(BF16).astype(F32)
            fold(0, pot)

        @pl.when(last)
        def _():
            for copy in rim_copies:
                copy.wait_recv()
            before = jnp.where(me == 0, 0.0, rim[0])
            after = jnp.where(me == NDEV - 1, 0.0, rim[1])
            grad = far + ext[:BLOCKS, :]
            grad = cat(
                [grad[:REACH] + before, grad[REACH:BLOCKS - REACH], grad[BLOCKS - REACH:] + after], 0
            )
            fold(64, grad)

    loads["stencil"].wait()

    def both_passes(which, carry):
        evaluate(which)
        return carry

    lax.fori_loop(0, 2, both_passes, 0)
    pass_sent(1)
    for copy in rim_copies:
        copy.wait_send()


def local(table, charges, target, stencil, near_matrix, green, block_dest, block_tile, near_offset):
    out = pl.pallas_call(
        kernel,
        out_shape=jax.ShapeDtypeStruct((128, LANES), F32),
        in_specs=[pl.BlockSpec(memory_space=pl.ANY)] * 9,
        out_specs=pl.BlockSpec(memory_space=pltpu.VMEM),
        scratch_shapes=[
            pltpu.VMEM((64, LANES), BF16),
            pltpu.VMEM((64, LANES), F32),
            pltpu.VMEM((32, GRID), F32),
            pltpu.VMEM((1, LANES), jnp.int32),
            pltpu.VMEM((1, LANES), jnp.int32),
            pltpu.VMEM((4, LANES), jnp.int32),
            pltpu.VMEM((TABLE_ROWS, 256), F32),
            pltpu.VMEM((BLOCKS * PANEL, CELLS), BF16),
            pltpu.VMEM((CELLS, BLOCKS * PANEL), BF16),
            pltpu.VMEM((4 * BLOCKS, PANEL * PANEL), BF16),
            pltpu.VMEM((2, 4 * NDEV, LANES), BF16),
            pltpu.VMEM((2, 4 * NDEV, LANES), BF16),
            pltpu.VMEM((6, 4 * NDEV, LANES), jnp.int32),
            pltpu.VMEM((6, 4 * NDEV, LANES), jnp.int32),
            pltpu.VMEM((512, LANES), jnp.int32),
            pltpu.VMEM((512, LANES), jnp.int32),
            pltpu.VMEM((128, 512), F32),
            pltpu.VMEM((128, LANES), F32),
            pltpu.VMEM((128, 256), F32),
            pltpu.VMEM((128, 128), F32),
            pltpu.VMEM((128, 128), F32),
            pltpu.VMEM((128, 128), F32),
            pltpu.VMEM((128, 256), F32),
            pltpu.VMEM((4, 256, 256), BF16),
            pltpu.VMEM((2, 256, 512), BF16),
            pltpu.VMEM((32, 256, 256), BF16),
            pltpu.VMEM((512, LANES), F32),
            pltpu.VMEM((512, LANES), F32),
            pltpu.VMEM((512, LANES), F32),
            pltpu.VMEM((128, LANES), F32),
            pltpu.VMEM((144, LANES), F32),
            pltpu.VMEM((2, REACH, LANES), F32),
            pltpu.VMEM((2, REACH, LANES), F32),
            pltpu.SemaphoreType.DMA((8,)),
            pltpu.SemaphoreType.DMA((8,)),
            pltpu.SemaphoreType.DMA((32,)),
            pltpu.SemaphoreType.DMA,
            pltpu.SemaphoreType.DMA((8,)),
            pltpu.SemaphoreType.DMA,
            pltpu.SemaphoreType.DMA((4,)),
            pltpu.SemaphoreType.DMA((4,)),
        ],
        compiler_params=pltpu.CompilerParams(collective_id=0, has_side_effects=True),
        name="panel_solver",
    )(
        charges.reshape(64, LANES), target.reshape(64, LANES),
        stencil.reshape(BLOCKS * PANEL, CELLS), near_matrix, green.T,
        block_dest.reshape(1, BLOCKS), block_tile.reshape(1, BLOCKS), near_offset.T, table,
    )
    return (out[:64].reshape(-1), out[64:].reshape(-1))


def solution(mesh):
    table = jnp.asarray(make_tables())
    return jax.shard_map(
        functools.partial(local, table),
        mesh=mesh,
        in_specs=(
            P(("panel", "slab")),
            P(("panel", "slab")),
            P(("panel", "slab"), None, None),
            P(("panel", "slab"), None, None),
            P(None, ("panel", "slab")),
            P(("panel", "slab"), None),
            P(("panel", "slab")),
            P(("panel", "slab"), None),
        ),
        out_specs=(P(("panel", "slab")), P(("panel", "slab"))),
        check_vma=False,
    )
```

```python
import functools
import math

import jax
import jax.numpy as jnp
import numpy as np
from jax import lax
from jax.experimental import pallas as pl
from jax.experimental.pallas import tpu as pltpu
from jax.sharding import PartitionSpec as P

GRID = 4096
TILE = 16
REACH = 8
NDEV = 128
SLABS = 4
BLOCKS = 128
PANEL = 64
CELLS = 256
LANES = 128
GREEN_UNIT = 8191.0
MESH = pl.DeviceIdType.MESH
F32 = jnp.float32
BF16 = jnp.bfloat16
TABLES = (("w1", 256), ("m0", 256), ("m0i", 256), ("w2", 128), ("a1", 128), ("w3", 512), ("w5", 128), ("t2", 128),
          ("c0", 128), ("c1", 128), ("s0", 128), ("s1", 128))
START = {name: sum(n for _, n in TABLES[:i]) for i, (name, _) in enumerate(TABLES)}
TABLE_ROWS = sum(n for _, n in TABLES)


def make_tables():
    def angle(rows, cols, modulus):
        return 2.0 * math.pi / modulus * ((np.outer(rows, cols)) % modulus)

    out = {}
    th = angle(np.arange(128), np.arange(256), 256)
    w1 = np.concatenate([np.cos(th), -np.sin(th)], 0)
    w1[128] = (-1.0) ** np.arange(256)
    out["w1"] = w1
    th = angle(np.arange(16), np.arange(16), 16)
    c, s = np.kron(np.eye(8), np.cos(th)), np.kron(np.eye(8), np.sin(th))
    out["w2"] = np.concatenate([c, s], 1)
    m0 = np.zeros((2, 16, 2, 16))
    idx = np.arange(16)
    m0[0, :, 0, 0] = 1.0
    m0[0, :, 1, 0] = (-1.0) ** idx
    for k in range(1, 8):
        t = 2 * math.pi * ((idx * k) % 16) / 16
        m0[0, :, 0, k], m0[0, :, 1, k] = np.cos(t), -np.sin(t)
    for n in range(8):
        t = 2 * math.pi * ((idx * (1 + 2 * n)) % 32) / 32
        m0[1, :, 0, 8 + n], m0[1, :, 1, 8 + n] = np.cos(t), -np.sin(t)
    big = np.zeros((2, 8, 16, 2, 8, 16))
    for a in range(8):
        big[:, a, :, :, a, :] = m0
    out["m0"] = big.reshape(256, 256)
    inv = m0.copy()
    inv[:, :, :, 0] *= 0.5
    big = np.zeros((2, 8, 16, 2, 8, 16))
    for a in range(8):
        big[:, a, :, :, a, :] = inv
    out["m0i"] = big.reshape(256, 256).T
    th = angle(np.arange(128), np.arange(128), 128)
    out["a1"] = np.concatenate([np.cos(th), np.sin(th)], 1)
    parts = []
    for m in range(4):
        th = angle(np.arange(8), m + 4 * np.arange(8), 32)
        parts.append(
            np.concatenate([np.kron(np.cos(th), np.eye(16)), np.kron(np.sin(th), np.eye(16))], 1)
        )
    out["w3"] = np.concatenate(parts, 0)
    w5 = np.zeros((2, 8, 16, 8, 16))
    for m in range(4):
        for j in range(4):
            th = angle(m + 4 * np.arange(8), 8 * j + np.arange(8), 32)
            w5[0, :, m, :, j], w5[1, :, m, :, j] = np.cos(th), np.sin(th)
    out["w5"] = np.concatenate([w5[0].reshape(128, 128), w5[1].reshape(128, 128)], 1)
    th = np.tile(angle(np.arange(128), np.arange(16), GRID), (1, 8))
    th[0] = 0.0
    out["t2"] = np.concatenate([np.cos(th), np.sin(th)], 1)
    th = np.repeat(angle(np.arange(128), np.arange(32), GRID), 16, axis=1)
    out["c0"], out["c1"] = np.cos(th[:, :256]), np.cos(th[:, 256:])
    out["s0"], out["s1"] = np.sin(th[:, :256]), np.sin(th[:, 256:])
    return np.concatenate([out[name] for name, _ in TABLES], 0).astype(np.float32)


def dot(a, b):
    return lax.dot_general(a, b, (((1,), (0,)), ((), ())), preferred_element_type=F32)


def dot_nt(a, b):
    return lax.dot_general(a, b, (((1,), (1,)), ((), ())), preferred_element_type=F32)


def split(x):
    hi = x.astype(BF16)
    return hi, (x - hi.astype(F32)).astype(BF16)


def dot3(a, b):
    n = a[0].shape[0]
    both = dot(jnp.concatenate(a, 0), b[0])
    return both[:n] + (both[n:] + dot(a[0], b[1]))


def iota(shape, dim):
    return lax.broadcasted_iota(jnp.int32, shape, dim)


def cat(parts, axis):
    return jnp.concatenate(parts, axis=axis)


COMBOS = sorted(
    ((dz, dx) for dz in range(4) for dx in range(4)),
    key=lambda c: -(min(c[0], 4 - c[0]) + min(c[1], 4 - c[1])),
)
Z_DIGITS = sum(c[0] << (2 * i) for i, c in enumerate(COMBOS))
X_DIGITS = sum(c[1] << (2 * i) for i, c in enumerate(COMBOS))


def encode(re, im):
    top = jnp.abs(re[0])
    for x in list(re[1:]) + list(im):
        top = jnp.maximum(top, jnp.abs(x))
    top = jnp.maximum(top, 2.0 ** -100)
    power = jnp.floor(jnp.log2(top)) + 1.0
    scale = jnp.exp2(14.0 - power)
    code = power.astype(jnp.int32) + 128

    def mantissa(x):
        return jnp.minimum(x * scale + 16384.5, 32767.5).astype(jnp.int32)

    return [
        (((code >> (2 * j)) & 3) << 30) | (mantissa(re[j]) << 15) | mantissa(im[j])
        for j in range(4)
    ]


def decode(words):
    code = words[0] >> 30 & 3
    for j in range(1, 4):
        code = code | ((words[j] >> 30 & 3) << (2 * j))
    scale = jnp.exp2(code.astype(F32) - 142.0)
    re = [((w >> 15 & 32767).astype(F32) - 16384.0) * scale for w in words]
    im = [((w & 32767).astype(F32) - 16384.0) * scale for w in words]
    return re, im


def encode_pairs(values):
    flat = [x for pair in values for x in pair]
    top = jnp.abs(flat[0])
    for x in flat[1:]:
        top = jnp.maximum(top, jnp.abs(x))
    power = jnp.floor(jnp.log2(jnp.maximum(top, 2.0 ** -100))) + 1.0
    scale = jnp.exp2(13.0 - power)
    code = power.astype(jnp.int32) + 128

    def mantissa(x):
        return jnp.minimum(x * scale + 8192.5, 16383.5).astype(jnp.int32)

    return [
        (((code >> (4 * k)) & 15) << 28) | (mantissa(a) << 14) | mantissa(b)
        for k, (a, b) in enumerate(values)
    ]


def decode_pairs(words):
    code = (words[0] >> 28 & 15) | ((words[1] >> 28 & 15) << 4)
    scale = jnp.exp2(code.astype(F32) - 141.0)
    return [
        [((w >> at & 16383).astype(F32) - 8192.0) * scale for at in (14, 0)] for w in words
    ]


def kernel(
    q_hbm, target_hbm, stencil_hbm, near_hbm, green_hbm, dest_hbm, tile_hbm, offset_hbm, table_hbm,
    out_ref,
    q_ref, target_ref, green_ref, dest_ref, tile_ref, offset_ref, table,
    stencil, turned, near_mat, sback, rback, swords, rwords, gsend, grecv, ga, gb5, t5, val, charge, goal, tv,
    wf, wi, mats, xs, order, acc, near, ext, halo, rim,
    send_sem, recv_sem, gsend_sem, grecv_sem, load_sem, near_sem, halo_sem, rim_sem,
):
    panel = lax.axis_index("panel")
    slab = lax.axis_index("slab")
    me = panel * SLABS + slab
    pz, px, pc = panel // 8, (panel // 2) % 4, panel % 2

    def rows_at(name):
        n = dict(TABLES)[name]
        return table[START[name]:START[name] + n, :]

    def half_at(name, half):
        n = dict(TABLES)[name]
        return table[START[name]:START[name] + n, half * LANES:(half + 1) * LANES]

    loads = {
        name: pltpu.make_async_copy(src, dst, load_sem.at[i])
        for i, (name, src, dst) in enumerate((
            ("q", q_hbm, q_ref), ("dest", dest_hbm, dest_ref), ("tile", tile_hbm, tile_ref),
            ("stencil", stencil_hbm, stencil), ("table", table_hbm, table),
            ("green", green_hbm, green_ref), ("offset", offset_hbm, offset_ref),
            ("target", target_hbm, target_ref),
        ))
    }
    for name in ("q", "dest", "tile", "stencil"):
        loads[name].start()

    def others(visit):
        def body(g, carry):
            z = (pz + ((Z_DIGITS >> (2 * g)) & 3)) % 4
            x = (px + ((X_DIGITS >> (2 * g)) & 3)) % 4
            for dy in (2, 1, 3, 0):
                for dc in (1, 0):
                    def go(z=z, x=x, dy=dy, dc=dc):
                        visit(z * 8 + x * 2 + (pc + dc) % 2, (slab + dy) % 4)

                    if dy == 0 and dc == 0:
                        pl.when(g != 15)(go)
                    else:
                        go()
            return carry

        lax.fori_loop(0, 16, body, 0)

    barrier = pltpu.get_barrier_semaphore()
    others(
        lambda p, y: pl.semaphore_signal(barrier, inc=1, device_id=(p, y), device_id_type=MESH)
    )

    for name in ("table", "green", "offset", "target"):
        loads[name].start()

    def near_load(b, carry):
        pltpu.make_async_copy(
            near_hbm.at[b], near_mat.at[pl.ds(pl.multiple_of(b * 4, 4), 4)], near_sem
        ).start()
        return carry

    rows128, lanes128 = iota((128, 128), 0), iota((128, 128), 1)

    def unfold(ref, out):
        x = ref[...].astype(F32)
        y = pltpu.roll(x, 64, 1)
        low = iota((64, 128), 1) < 64
        out[pl.ds(0, 64, stride=2), :] = jnp.where(low, x, y)
        out[pl.ds(1, 64, stride=2), :] = jnp.where(low, y, x)

    def fold(row, value):
        goal[...] = value
        low = iota((64, 128), 1) < 64
        out_ref[row:row + 64, :] = jnp.where(
            low, goal[pl.ds(0, 64, stride=2), :], goal[pl.ds(1, 64, stride=2), :]
        )

    loads["q"].wait()
    unfold(q_ref, charge)
    val[...] = charge[...]

    def pair(slot, value):
        hi, lo = split(value)
        mats[2 * slot] = hi
        mats[2 * slot + 1] = lo

    def mat(slot):
        return mats[2 * slot], mats[2 * slot + 1]

    every16 = lanes128 % 16 == 0

    def squeeze(tiles):
        total = jnp.where(every16, tiles[0], 0.0)
        for j in range(1, 4):
            total = total + pltpu.roll(jnp.where(every16, tiles[j], 0.0), j, 1)
        return total

    def split_tables():
        def circle(name):
            return half_at(name, 0), half_at(name, 1)

        pair(0, rows_at("w1"))
        c, s = circle("w2")
        pair(1, cat([cat([c, -s], 1), cat([s, c], 1)], 0))
        pair(2, cat([cat([c, s], 1), cat([-s, c], 1)], 0))
        pair(3, rows_at("m0"))
        pair(4, rows_at("m0i"))
        c, s = circle("a1")
        pair(5, cat([cat([c, s], 1), cat([-s, c], 1)], 0))
        pair(6, cat([cat([c, -s], 1), cat([s, c], 1)], 0))
        for m in range(4):
            base = START["w3"] + 128 * m
            c, s = table[base:base + 128, :LANES], table[base:base + 128, LANES:]
            pair(7 + m, cat([cat([c, -s], 1), cat([s, c], 1)], 0))
            c, s = c.T, s.T
            pair(11 + m, cat([cat([c, s], 1), cat([-s, c], 1)], 0))
        c, s = circle("w5")
        pair(15, cat([cat([c, s], 1), cat([-s, c], 1)], 0))
        t5[:, :LANES] = squeeze([half_at("c%d" % (j // 2), j % 2) for j in range(4)])
        t5[:, LANES:] = squeeze([half_at("s%d" % (j // 2), j % 2) for j in range(4)])

    loads["dest"].wait()
    loads["tile"].wait()
    dest_row = dest_ref[...]
    tile_row = tile_ref[...]

    def column(row):
        return jnp.sum(jnp.where(rows128 == lanes128, row, 0), axis=1, keepdims=True)

    dest_col = column(dest_row)
    same = dest_col == dest_row
    rank_row = jnp.sum(jnp.where(same & (rows128 < lanes128), 1, 0), axis=0, keepdims=True)
    rank_col = jnp.sum(jnp.where(same & (lanes128 < rows128), 1, 0), axis=1, keepdims=True)
    one, zero = F32(1.0), F32(0.0)
    out_pick = cat(
        [jnp.where((dest_row == rows128) & (rank_row == k), one, zero) for k in range(2)], 0
    )
    wanted = iota((128, 512), 1) - 4 * dest_col - 2 * rank_col
    in_pick = [jnp.where(wanted == h, one, zero).astype(BF16) for h in range(2)]
    ids = jnp.sum(out_pick * (tile_row + 1).astype(F32), axis=1, keepdims=True)
    id_rows = jnp.where(lanes128 == 0, ids[:128], jnp.where(lanes128 == 1, ids[128:], 0.0))
    out_pick = out_pick.astype(BF16)

    def exchange(step, src, dst, stride, count):
        mine = pl.ds(pl.multiple_of(me * stride, stride), count)

        def send(p, y):
            theirs = pl.ds(pl.multiple_of((p * SLABS + y) * stride, stride), count)
            pltpu.make_async_remote_copy(
                src_ref=src.at[theirs],
                dst_ref=dst.at[mine],
                send_sem=send_sem.at[step],
                recv_sem=recv_sem.at[step],
                device_id=(p, y),
                device_id_type=MESH,
            ).start()

        others(send)
        pltpu.make_async_copy(src.at[mine], dst.at[mine], recv_sem.at[step]).start()

    def arrived(step, src, dst, count):
        part = pl.ds(0, NDEV * count)
        pltpu.make_async_copy(src.at[part], dst.at[part], recv_sem.at[step]).wait()

    def sent(step, src, dst, count):
        part = pl.ds(0, (NDEV - 1) * count)
        pltpu.make_async_copy(src.at[part], dst.at[part], send_sem.at[step]).wait()

    def pass_sent(p):
        sent(4 * p, swords.at[4 + p], rwords.at[4 + p], 3 - p)
        sent(4 * p + 1, swords.at[2 * p], rwords.at[2 * p], 4)
        sent(4 * p + 2, swords.at[2 * p + 1], rwords.at[2 * p + 1], 4)
        sent(4 * p + 3, sback.at[p], rback.at[p], 4)

    def put_row(slot, row, value):
        swords[slot, pl.ds(row, NDEV, stride=4), :] = value

    def get_row(slot, row):
        return rwords[slot, pl.ds(row, NDEV, stride=4), :]

    def put_words(slot, re, im):
        for j, w in enumerate(encode(re, im)):
            put_row(slot, j, w)

    def get_words(slot):
        return decode([get_row(slot, j) for j in range(4)])

    def next_to(shift):
        other = (me + shift + NDEV) % NDEV
        return (other // SLABS, other % SLABS)

    def edge_copies(src, rows_prev, rows_next, dst, sem):
        for way, (shift, rows) in enumerate(((-1, rows_prev), (1, rows_next))):
            yield pltpu.make_async_remote_copy(
                src_ref=src.at[pl.ds(rows, REACH)],
                dst_ref=dst.at[1 - way],
                send_sem=sem.at[way],
                recv_sem=sem.at[3 - way],
                device_id=next_to(shift),
                device_id_type=MESH,
            )

    halo_copies = list(edge_copies(charge, 0, BLOCKS - REACH, halo, halo_sem))
    rim_copies = list(edge_copies(ext, BLOCKS, BLOCKS + REACH, rim, rim_sem))

    def place(index):
        return jnp.where(index < 128, index, jnp.where(index < 136, index - 136, index - 8))

    def near_forward():
        loads["offset"].wait()
        for copy in halo_copies:
            copy.wait_recv()
        before = jnp.where(me == 0, 0.0, halo[0])
        after = jnp.where(me == NDEV - 1, 0.0, halo[1])
        source = cat([charge[...], before, after], 0).astype(BF16)
        spot = place(iota((128, 144), 1)) - iota((128, 144), 0)
        for k in range(4):
            pick = jnp.where(spot == column(offset_ref[k:k + 1, :]), one, zero).astype(BF16)
            xs[pl.ds(k, 128, stride=4), :] = dot(pick, source)
        pltpu.make_async_copy(near_mat, near_mat, near_sem).wait()
        acc[...] = jnp.zeros((512, 128), F32)

    def near_products(begin, end):
        def body(c, carry):
            col = pl.ds(pl.multiple_of(c * 256, 256), 256)
            gather = jnp.where(
                iota((256, 128), 1) % 64 == c * 4 + iota((256, 128), 0) // 64, one, zero
            ).astype(BF16)
            for r in range(4):
                row = pl.ds(128 * r, 128)
                x = xs[row, :]
                hi, lo = split(near_mat[row, col].astype(F32) * cat([x, x], 1))
                acc[row, :] = acc[row, :] + (dot(hi, gather) + dot(lo, gather))
            return carry

        lax.fori_loop(begin, end, body, 0)

    def near_adjoint():
        for k in range(4):
            xs[pl.ds(k, 128, stride=4), :] = val[...]
        acc[...] = jnp.zeros((512, 128), F32)

        def body(c, carry):
            col = pl.ds(pl.multiple_of(c * 256, 256), 256)
            spread = jnp.where(
                iota((128, 256), 0) == c * 4 + iota((128, 256), 1) // 64, one, zero
            ).astype(BF16)
            for r in range(4):
                row = pl.ds(128 * r, 128)
                p = near_mat[row, col].astype(F32) * dot(xs[row, :].astype(BF16), spread)
                acc[row, :] = acc[row, :] + (p[:, :128] + p[:, 128:])
            return carry

        lax.fori_loop(0, 16, body, 0)

    def near_scatter():
        acc[...] = acc[...] + pltpu.roll(acc[...], 64, 1)
        total = jnp.zeros((144, 128), F32)
        spot = place(iota((144, 128), 0)) - iota((144, 128), 1)
        for k in range(4):
            pick = jnp.where(spot == offset_ref[k:k + 1, :], one, zero).astype(BF16)
            hi, lo = split(acc[pl.ds(k, 128, stride=4), :])
            total = total + (dot(pick, hi) + dot(pick, lo))
        ext[...] = total
        for copy in rim_copies:
            copy.start()

    def back_table():
        idm = get_row(4, 2)
        for k in range(2):
            xs[pl.ds(k, 128, stride=2), :] = jnp.broadcast_to(
                idm[:, k:k + 1].astype(F32), (128, 128)
            )
        ordered = xs[:256, :1].astype(jnp.int32)
        for tr in range(2):
            pick = jnp.where(
                ordered == iota((256, 256), 1) + (tr * 256 + 1), one, zero
            ).astype(BF16)
            for t in range(2):
                wi[t, :, tr * 256:(tr + 1) * 256] = dot_nt(pick, mats[t]).astype(BF16)

    def turn_stencil():
        eye = jnp.where(iota((256, 256), 0) == iota((256, 256), 1), one, zero).astype(BF16)

        def body(g, carry):
            at = pl.multiple_of(g * 512, 512)
            turned[:, pl.ds(at, 512)] = dot_nt(eye, stencil[pl.ds(at, 512), :]).astype(BF16)
            return carry

        lax.fori_loop(0, 16, body, 0)

    def pack(kk, carry):
        def code(at):
            x = green_ref[:, pl.ds(pl.multiple_of(at * LANES, LANES), LANES)]
            return (x * GREEN_UNIT + 0.5).astype(jnp.int32)

        gsend[pl.ds(kk, 32, stride=16), :] = (code(kk + 16) << 16) | code(kk)
        return carry

    def green_copies():
        k2 = me // 8

        def body(j, carry):
            k1 = (me % 8) * 32 + j
            low = jnp.where(k1 < 128, 1, 0)
            is_mid = jnp.where(k1 == 128, 1, 0)
            is_zero = jnp.where(k1 == 0, 1, 0)
            high = 1 - low - is_mid
            target_dev = low * k1 + high * (256 - k1)
            upper = k2 // 8
            beyond = jnp.where(k2 > 8, 1, 0)
            slot_zero = (1 - upper) * k2 + upper * (1 - beyond) * 16 + beyond * (32 - k2)
            slot_mid = (1 - upper) * (8 + k2) + upper * (39 - k2)
            slot = (low - is_zero) * k2 + is_zero * slot_zero + is_mid * slot_mid + high * (31 - k2)
            src = gsend.at[pl.ds(pl.multiple_of(j * 16, 16), 16)]
            dst = grecv.at[pl.ds(pl.multiple_of(slot * 16, 16), 16)]

            @pl.when(target_dev != me)
            def _():
                pltpu.make_async_remote_copy(
                    src_ref=src, dst_ref=dst, send_sem=gsend_sem.at[j], recv_sem=grecv_sem,
                    device_id=(target_dev // SLABS, target_dev % SLABS), device_id_type=MESH,
                ).start()

            @pl.when(target_dev == me)
            def _():
                pltpu.make_async_copy(src, dst, grecv_sem).start()

            return carry

        lax.fori_loop(0, 32, body, 0)

    def green_sent():
        def body(j, carry):
            k1 = (me % 8) * 32 + j
            low = jnp.where(k1 < 128, 1, 0)
            high = jnp.where(k1 > 128, 1, 0)
            target_dev = low * k1 + high * (256 - k1)

            @pl.when(target_dev != me)
            def _():
                part = pl.ds(pl.multiple_of(j * 16, 16), 16)
                pltpu.make_async_copy(gsend.at[part], grecv.at[part], gsend_sem.at[j]).wait()

            return carry

        lax.fori_loop(0, 32, body, 0)

    def green_ready():
        pltpu.make_async_copy(gsend, grecv, grecv_sem).wait()
        scale = 2.0 ** -24 / GREEN_UNIT
        flip = jnp.where((rows128 + lanes128 == 128) & (rows128 > 0), one, zero).astype(BF16)
        first = jnp.where((rows128 == 0) & (lanes128 == 0), one, zero).astype(BF16)
        eye = jnp.where(rows128 == lanes128, one, zero).astype(BF16)
        turn = cat([flip, first], 1)
        special = every16 & (me == 0)

        def rows_of(base, kappa):
            rows = []
            for n in range(8):
                k = kappa(n)
                words = grecv[pl.ds(base * 16 + k % 16, 16, stride=16), :]
                rows.append(((words >> 16 if k >= 16 else words) & 65535).astype(F32))
            return cat(rows, 0)

        nyquist = []

        for m in range(4):
            def plain(base):
                hi, lo = split(rows_of(base, lambda n: m + 4 * n))
                return dot_nt(eye, hi) + dot_nt(eye, lo)

            def turned(base):
                one_ = rows_of(base, lambda n: 31 - m - 4 * n)
                two_ = rows_of(base, lambda n: (32 - m - 4 * n) % 32)
                hi, lo = split(cat([one_, two_], 1))
                return dot_nt(turn, hi) + dot_nt(turn, lo)

            d, dr, o, orr = plain(0), turned(0), plain(16), turned(16)
            ga[:, m * LANES:(m + 1) * LANES] = (d + jnp.where(special, dr, orr)) * scale
            nyquist.append((o + orr) * scale)
        gb5[...] = squeeze(nyquist)

    lane64 = iota((128, 128), 1) // 64
    row16 = iota((128, 128), 0) % 16

    def project():
        v = val[...]
        spread = cat(
            [jnp.where(lane64 + 2 * i == row16, v, 0.0).astype(BF16) for i in range(8)], 1
        )
        for g in range(8):
            part = stencil[g * 1024:(g + 1) * 1024, :]
            tv[g * 16:(g + 1) * 16, :] = dot(spread[g * 16:(g + 1) * 16, :], part)
        hi, lo = split(tv[...])
        return dot(out_pick, hi) + dot(out_pick, lo)

    def interpolate(own_tiles):
        rows = []
        l64, r16 = iota((16, 128), 1) // 64, iota((16, 128), 0)
        for g in range(8):
            r = dot(own_tiles[g * 16:(g + 1) * 16, :], turned[:, g * 1024:(g + 1) * 1024])
            acc = jnp.zeros((16, 128), F32)
            for i in range(8):
                acc = acc + jnp.where(l64 + 2 * i == r16, r[:, i * LANES:(i + 1) * LANES], 0.0)
            rows.append(acc)
        far = cat(rows, 0)
        return far + pltpu.roll(far, 64, 1)

    def cmul(re, im, c, s):
        return re * c + im * s, im * c - re * s

    def cmul_conj(re, im, c, s):
        return re * c - im * s, im * c + re * s

    def lane_tile(x, j):
        return x[:, j * LANES:(j + 1) * LANES]

    head = iota((8, 128), 0) == 0

    def special_rows(parts, slot, outs):
        small = dot3(split(cat([p[:8] for p in parts], 0)), mat(slot))
        fixed = []
        for j in range(4):
            out = outs[j]
            h2 = iota((8, 256), 0) == 0
            fixed.append(cat([jnp.where(h2, small[8 * j:8 * j + 8], out[:8]), out[8:]], 0))
        return fixed

    def evaluate(which):
        step0 = which * 4
        first, last = which == 0, which == 1
        fwd, inv_ = which * 2, which * 2 + 1
        out = project()
        coded = encode_pairs(
            [[lane_tile(out[128 * k:128 * k + 128], h) for h in range(2)] for k in range(2)]
        )
        for k in range(2):
            put_row(4 + which, k, coded[k])

        @pl.when(first)
        def _():
            put_row(4, 2, id_rows.astype(jnp.int32))
            pl.semaphore_wait(barrier, NDEV - 1)
            exchange(0, swords.at[4], rwords.at[4], 4, 3)
            for copy in halo_copies:
                copy.start()
            loads["green"].wait()
            lax.fori_loop(0, 16, pack, 0)
            green_copies()
            lax.fori_loop(0, BLOCKS, near_load, 0)
            loads["table"].wait()
            split_tables()
            loads["target"].wait()
            unfold(target_ref, goal)
            arrived(0, swords.at[4], rwords.at[4], 3)
            idm = get_row(4, 2)
            tc = iota((128, 256), 1)
            for tr in range(2):
                pick = cat(
                    [
                        jnp.where(idm[:, k:k + 1] == tc + (tr * 256 + 1), one, zero)
                        for k in range(2)
                    ],
                    0,
                ).astype(BF16)
                for t in range(2):
                    wf[2 * tr + t] = dot_nt(mats[t], pick).astype(BF16)

        @pl.when(last)
        def _():
            exchange(4, swords.at[5], rwords.at[5], 4, 2)
            fold(0, near[...])
            near_adjoint()
            arrived(4, swords.at[5], rwords.at[5], 2)

        values = decode_pairs([get_row(4 + which, k) for k in range(2)])
        tiles = split(cat([cat(v, 1) for v in values], 0))
        c2, s2 = half_at("t2", 0), half_at("t2", 1)
        c1 = cat([rows_at("c0"), rows_at("c1")], 1)
        s1 = cat([rows_at("s0"), rows_at("s1")], 1)
        parts = []
        for tr in range(2):
            y = dot3((wf[2 * tr], wf[2 * tr + 1]), tiles)
            for h in range(2):
                re, im = cmul(lane_tile(y[:128], h), lane_tile(y[128:], h), c2, s2)
                parts.append(cat([re, im], 1))
        prod = dot3(split(cat(parts, 0)), mat(1))
        outs = special_rows(parts, 3, [prod[128 * j:128 * j + 128] for j in range(4)])
        put_words(fwd, [o[:, :LANES] for o in outs], [o[:, LANES:] for o in outs])
        exchange(step0 + 1, swords.at[fwd], rwords.at[fwd], 4, 4)

        @pl.when(first)
        def _():
            green_ready()
            back_table()
            turn_stencil()

        @pl.when(last)
        def _():
            near_scatter()
            green_sent()
            pass_sent(0)
            for copy in halo_copies:
                copy.wait_send()

        arrived(step0 + 1, swords.at[fwd], rwords.at[fwd], 4)
        re, im = get_words(fwd)
        y = dot3(mat(5), split(cat([cat(re, 1), cat(im, 1)], 0)))
        re, im = cmul(y[:128], y[128:], c1, s1)
        r = [lane_tile(re, j) for j in range(4)]
        i = [lane_tile(im, j) for j in range(4)]
        er, ei, dr, di = r[0] + r[2], i[0] + i[2], r[0] - r[2], i[0] - i[2]
        fr, fi, hr, hi_ = r[1] + r[3], i[1] + i[3], r[1] - r[3], i[1] - i[3]
        vs = [(er + fr, ei + fi), (dr + hi_, di - hr), (er - fr, ei - fi), (dr - hi_, di + hr)]
        spectrum = [dot3(split(cat(list(vs[m]), 1)), mat(7 + m)) for m in range(4)]
        vs = []
        for m in range(4):
            gm = ga[:, m * LANES:(m + 1) * LANES]
            p = dot3(split(spectrum[m] * cat([gm, gm], 1)), mat(11 + m))
            vs.append((p[:, :LANES], p[:, LANES:]))
        r = [v[0] for v in vs]
        i = [v[1] for v in vs]
        er, ei, dr, di = r[0] + r[2], i[0] + i[2], r[0] - r[2], i[0] - i[2]
        fr, fi, hr, hi_ = r[1] + r[3], i[1] + i[3], r[1] - r[3], i[1] - i[3]
        zs = [(er + fr, ei + fi), (dr - hi_, di + hr), (er - fr, ei - fi), (dr + hi_, di - hr)]
        re, im = cmul_conj(cat([z[0] for z in zs], 1), cat([z[1] for z in zs], 1), c1, s1)
        y = dot3(mat(6), split(cat([re, im], 0)))
        g5 = gb5[...]
        p = dot3(
            split(cat([squeeze([f[:, :LANES] for f in spectrum]) * g5,
                       squeeze([f[:, LANES:] for f in spectrum]) * g5], 1)),
            mat(15),
        )
        re, im = cmul_conj(p[:, :LANES], p[:, LANES:], t5[:, :LANES], t5[:, LANES:])
        y5 = dot3((mats[12, 128:, :], mats[13, 128:, :]), split(cat([re, im], 0)))
        here = every16 & (me == 0)
        yr = [lane_tile(y[:128], j) for j in range(4)]
        yi = [
            jnp.where(here, pltpu.roll(y5, LANES - j, 1) if j else y5, lane_tile(y[128:], j))
            for j in range(4)
        ]
        put_words(inv_, yr, yi)
        exchange(step0 + 2, swords.at[inv_], rwords.at[inv_], 4, 4)

        @pl.when(first)
        def _():
            near_forward()
            near_products(0, 9)

        arrived(step0 + 2, swords.at[inv_], rwords.at[inv_], 4)
        re, im = get_words(inv_)
        parts = [cat([re[j], im[j]], 1) for j in range(4)]
        prod = dot3(split(cat(parts, 0)), mat(2))
        outs = special_rows(parts, 4, [prod[128 * j:128 * j + 128] for j in range(4)])
        zs = [cmul_conj(o[:, :LANES], o[:, LANES:], c2, s2) for o in outs]
        y = cat(
            [
                cat([cat([zs[2 * tr][0], zs[2 * tr + 1][0]], 1), cat([zs[2 * tr][1], zs[2 * tr + 1][1]], 1)], 0)
                for tr in range(2)
            ],
            0,
        )
        back = dot3((wi[0], wi[1]), split(y))
        for h in range(2):
            order[pl.ds(h, 256, stride=2), :] = lane_tile(back, h)
        sback[which] = order[...].astype(BF16)
        exchange(step0 + 3, sback.at[which], rback.at[which], 4, 4)

        @pl.when(first)
        def _():
            near_products(9, 16)
            near[...] = sum(acc[pl.ds(k, 128, stride=4), :] for k in range(4))

        arrived(step0 + 3, sback.at[which], rback.at[which], 4)
        tiles = rback[which]
        far = interpolate(cat([dot(in_pick[h], tiles) for h in range(2)], 1).astype(BF16))

        @pl.when(first)
        def _():
            pot = far + near[...]
            val[...] = (pot - goal[...]).astype(BF16).astype(F32)
            near[...] = pot

        @pl.when(last)
        def _():
            for copy in rim_copies:
                copy.wait_recv()
            before = jnp.where(me == 0, 0.0, rim[0])
            after = jnp.where(me == NDEV - 1, 0.0, rim[1])
            grad = far + ext[:BLOCKS, :]
            grad = cat(
                [grad[:REACH] + before, grad[REACH:BLOCKS - REACH], grad[BLOCKS - REACH:] + after], 0
            )
            fold(64, grad)

    loads["stencil"].wait()

    def both_passes(which, carry):
        evaluate(which)
        return carry

    lax.fori_loop(0, 2, both_passes, 0)
    pass_sent(1)
    for copy in rim_copies:
        copy.wait_send()


def local(table, charges, target, stencil, near_matrix, green, block_dest, block_tile, near_offset):
    out = pl.pallas_call(
        kernel,
        out_shape=jax.ShapeDtypeStruct((128, LANES), F32),
        in_specs=[pl.BlockSpec(memory_space=pl.ANY)] * 9,
        out_specs=pl.BlockSpec(memory_space=pltpu.VMEM),
        scratch_shapes=[
            pltpu.VMEM((64, LANES), BF16),
            pltpu.VMEM((64, LANES), F32),
            pltpu.VMEM((32, GRID), F32),
            pltpu.VMEM((1, LANES), jnp.int32),
            pltpu.VMEM((1, LANES), jnp.int32),
            pltpu.VMEM((4, LANES), jnp.int32),
            pltpu.VMEM((TABLE_ROWS, 256), F32),
            pltpu.VMEM((BLOCKS * PANEL, CELLS), BF16),
            pltpu.VMEM((CELLS, BLOCKS * PANEL), BF16),
            pltpu.VMEM((4 * BLOCKS, PANEL * PANEL), BF16),
            pltpu.VMEM((2, 4 * NDEV, LANES), BF16),
            pltpu.VMEM((2, 4 * NDEV, LANES), BF16),
            pltpu.VMEM((6, 4 * NDEV, LANES), jnp.int32),
            pltpu.VMEM((6, 4 * NDEV, LANES), jnp.int32),
            pltpu.VMEM((512, LANES), jnp.int32),
            pltpu.VMEM((512, LANES), jnp.int32),
            pltpu.VMEM((128, 512), F32),
            pltpu.VMEM((128, LANES), F32),
            pltpu.VMEM((128, 256), F32),
            pltpu.VMEM((128, 128), F32),
            pltpu.VMEM((128, 128), F32),
            pltpu.VMEM((128, 128), F32),
            pltpu.VMEM((128, 256), F32),
            pltpu.VMEM((4, 256, 256), BF16),
            pltpu.VMEM((2, 256, 512), BF16),
            pltpu.VMEM((32, 256, 256), BF16),
            pltpu.VMEM((512, LANES), F32),
            pltpu.VMEM((512, LANES), F32),
            pltpu.VMEM((512, LANES), F32),
            pltpu.VMEM((128, LANES), F32),
            pltpu.VMEM((144, LANES), F32),
            pltpu.VMEM((2, REACH, LANES), F32),
            pltpu.VMEM((2, REACH, LANES), F32),
            pltpu.SemaphoreType.DMA((8,)),
            pltpu.SemaphoreType.DMA((8,)),
            pltpu.SemaphoreType.DMA((32,)),
            pltpu.SemaphoreType.DMA,
            pltpu.SemaphoreType.DMA((8,)),
            pltpu.SemaphoreType.DMA,
            pltpu.SemaphoreType.DMA((4,)),
            pltpu.SemaphoreType.DMA((4,)),
        ],
        compiler_params=pltpu.CompilerParams(collective_id=0, has_side_effects=True),
        name="panel_solver",
    )(
        charges.reshape(64, LANES), target.reshape(64, LANES),
        stencil.reshape(BLOCKS * PANEL, CELLS), near_matrix, green.T,
        block_dest.reshape(1, BLOCKS), block_tile.reshape(1, BLOCKS), near_offset.T, table,
    )
    return (out[:64].reshape(-1), out[64:].reshape(-1))


def solution(mesh):
    table = jnp.asarray(make_tables())
    return jax.shard_map(
        functools.partial(local, table),
        mesh=mesh,
        in_specs=(
            P(("panel", "slab")),
            P(("panel", "slab")),
            P(("panel", "slab"), None, None),
            P(("panel", "slab"), None, None),
            P(None, ("panel", "slab")),
            P(("panel", "slab"), None),
            P(("panel", "slab")),
            P(("panel", "slab"), None),
        ),
        out_specs=(P(("panel", "slab")), P(("panel", "slab"))),
        check_vma=False,
    )
```
